32 devices in a mesh: rep: 8 (over z, y), shard: 4 (over x, core).
Axes of the slice: x: 2, y: 2, z: 4, core: 2. Of those that a mesh axis runs over, the one named last changes fastest.
Arguments:
- tokens: bfloat16 [16384, 1024], P(('rep', 'shard')), may hold values from -6 to 6
- token_ids: int32 [16384], P(('rep', 'shard')), may hold values from 0 to 8007
- hash_table: int32 [8008], replicated, may hold values from 0 to 1
- piece_starts: int32 [8, 2], P('rep'), may hold values from 0 to 1792, as said below
- valid_mask: int32 [16384], P(('rep', 'shard')), may hold values from 0 to 1, as said below
- teacher: bfloat16 [16384, 1024], P(('rep', 'shard')), may hold values from -6 to 6
- cotangent: bfloat16 [16384, 1024], P(('rep', 'shard')), may hold values from -6 to 6
- ln1_gain: bfloat16 [1024], P('shard'), may hold values from 0.5 to 1.5
- ln1_bias: bfloat16 [1024], P('shard'), may hold values from -0.59765625 to 0.59765625
- w_qkv: bfloat16 [1024, 3072], P('shard'), may hold values from -0.1875 to 0.1875
- w_out: bfloat16 [1024, 1024], P('shard'), may hold values from -3 to 3
- out_bias: bfloat16 [1024], P('shard'), may hold values from -0.59765625 to 0.59765625
- ln2_gain: bfloat16 [1024], P('shard'), may hold values from 0.5 to 1.5
- ln2_bias: bfloat16 [1024], P('shard'), may hold values from -0.59765625 to 0.59765625
- w_in: bfloat16 [2, 1024, 4096], P(None, 'shard'), may hold values from -0.1875 to 0.1875
- in_bias: bfloat16 [2, 4096], P(None, 'shard'), may hold values from -0.59765625 to 0.59765625
- w_back: bfloat16 [2, 4096, 1024], P(None, 'shard'), may hold values from -0.09375 to 0.09375
- back_bias: bfloat16 [2, 1024], P(None, 'shard'), may hold values from -0.59765625 to 0.59765625
Outputs:
- output: bfloat16 [16384, 1024], P(('rep', 'shard'))
- input_grad: float32 [16384, 1024], P(('rep', 'shard'))
- ln1_gain_grad: float32 [1024], P('shard')
- ln1_bias_grad: float32 [1024], P('shard')
- w_qkv_grad: float32 [1024, 3072], P('shard')
- w_out_grad: float32 [1024, 1024], P('shard')
- out_bias_grad: float32 [1024], P('shard')
- ln2_gain_grad: float32 [1024], P('shard')
- ln2_bias_grad: float32 [1024], P('shard')
- w_in_grad: float32 [2, 1024, 4096], P(None, 'shard')
- in_bias_grad: float32 [2, 4096], P(None, 'shard')
- w_back_grad: float32 [2, 4096, 1024], P(None, 'shard')
- back_bias_grad: float32 [2, 1024], P(None, 'shard')
The draws below stay inside these ranges and needn't reach their ends.
Inputs may be any that keep to these rules, and one draw needn't show every extreme that they name: `piece_starts`: in each sequence the 2 pieces of 256 tokens rise, do not intersect and lie inside the sequence; piece j begins in the j-th of 2 equal spans of the sequence. In the first sequence the first piece begins at 0 and the last ends with the sequence. `valid_mask`: the last token of each aligned block of 512 tokens always counts.
All inputs are finite; a program needn't handle non-finite values.
Results may differ from the reference program's by a relative error of at most 0.013.
Values may be sent and summed in bfloat16 or wider, within the bound.
No kernel may reach another device: no remote copies, remote signals or barrier semaphores. Data moves between devices by JAX's collectives and lax.ppermute only.
A program may use at most 256 MiB of HBM per device.

```python
import math
import jax
import jax.numpy as jnp
import numpy as np
from jax import lax

D = 1024
HEADS = 16
HEAD_DIM = 64
FF = 4096
VOCAB = 8008
EXPERTS = 2
PIECES = 2
PIECE_LEN = 256
TOK_DEV = 512
CAP = 320
SEQ_LEN = 2048
SEQS = 8
TOKENS = 16384
N_SHARD = 4


def draw_piece_starts(key, part):
    span_each = SEQ_LEN // PIECES
    offsets = jax.random.randint(key, (SEQS, PIECES), 0, span_each - PIECE_LEN + 1, dtype=jnp.int32)
    starts = offsets + jnp.arange(PIECES, dtype=jnp.int32)[None, :] * span_each
    row_index = jnp.arange(SEQS, dtype=jnp.int32)[:, None]
    col_index = jnp.arange(PIECES, dtype=jnp.int32)[None, :]
    starts = jnp.where((row_index == 0) & (col_index == 0), 0, starts)
    starts = jnp.where((row_index == 0) & (col_index == PIECES - 1), SEQ_LEN - PIECE_LEN, starts)
    return starts.astype(jnp.int32)


def draw_valid_mask(key, part):
    drawn = jax.random.randint(key, (TOKENS,), 0, 1024, dtype=jnp.int32)
    places = jnp.arange(TOKENS, dtype=jnp.int32)
    bounds = 256 + 512 * places // TOKENS
    forced = places % TOK_DEV == TOK_DEV - 1
    return jnp.where((drawn < bounds) | forced, 1, 0).astype(jnp.int32)


def touch_ends(array, rng, least, top_value):
    longest = array.shape.index(max(array.shape))
    spots = []
    for shift in (0, 1):
        where = [jax.random.randint(jax.random.fold_in(rng, axis), (), 0, length) for axis, length in enumerate(array.shape)]
        where[longest] = (where[longest] + shift) % array.shape[longest]
        spots.append(tuple(where))
    return array.at[spots[0]].set(least).at[spots[1]].set(top_value)


def steps_of(rng, extent, cuts, smallest, top_value):
    def one(axis_at, shards_of):
        heights = jax.random.uniform(jax.random.fold_in(jax.random.fold_in(rng, 6), axis_at), (shards_of,), jnp.float32, smallest / len(cuts), top_value / len(cuts))
        return jnp.repeat(jnp.exp(heights), extent[axis_at] // shards_of).reshape((-1,) + (1,) * (len(extent) - axis_at - 1))

    level = one(*cuts[0])
    for cut in cuts[1:]:
        level = level * one(*cut)
    return level


def rank_table(amount, lean):
    loads = [(1 << 20) // math.isqrt(grade ** lean) + 1 for grade in range(1, amount + 1)]
    deviation = 1 + sum(loads) // (1 << 30)
    return np.cumsum(np.array([max(1, weight // deviation) for weight in loads]))


def ranked_ids(rng, dims, amount, slope):
    listing = rank_table(amount, slope)
    ticket = jax.random.randint(jax.random.fold_in(rng, 1), dims, 0, int(listing[amount - 1]))
    grade = jnp.searchsorted(jnp.asarray(listing, jnp.int32), ticket, side="right")
    return jax.random.permutation(jax.random.fold_in(rng, 2), amount)[grade].astype(jnp.int32)


def normal_values(key, shape, spread, most, shards=(), kind=jnp.bfloat16):
    values = spread * jax.random.normal(key, shape, jnp.float32)
    if shards:
        values = values * steps_of(key, shape, shards, -0.22, 0.18)
    return jnp.clip(values, -most, most).astype(kind)


def setup_inputs(seed: int = 0) -> dict:
    seeds = jax.random.split(jax.random.key(seed), 19)
    return {
        "tokens": normal_values(seeds[0], (TOKENS, D), 1.0, 6.0, ((0, 32),)),
        "token_ids": touch_ends(ranked_ids(seeds[1], (TOKENS,), VOCAB, 2), jax.random.fold_in(seeds[1], 3), 0, VOCAB - 1).astype(jnp.int32),
        "hash_table": touch_ends(jax.random.randint(seeds[2], (VOCAB,), 0, EXPERTS), jax.random.fold_in(seeds[2], 1), 0, EXPERTS - 1).astype(jnp.int32),
        "piece_starts": draw_piece_starts(jax.random.fold_in(seeds[18], 71), 0),
        "valid_mask": draw_valid_mask(jax.random.fold_in(seeds[18], 71), 0),
        "teacher": normal_values(seeds[5], (TOKENS, D), 1.0, 6.0, ((0, 32),)),
        "cotangent": normal_values(seeds[6], (TOKENS, D), 1.0, 6.0, ((0, 32),)),
        "ln1_gain": jnp.clip(1.0 + 0.1 * jax.random.normal(seeds[7], (D,), jnp.float32), 0.5, 1.5).astype(jnp.bfloat16),
        "ln1_bias": normal_values(seeds[8], (D,), 0.1, 0.59765625, ((0, 4),)),
        "w_qkv": normal_values(seeds[9], (D, 3 * D), D ** -0.5, 0.1875, ((0, 4),)),
        "w_out": normal_values(seeds[10], (D, D), (max(D // 256, 4)) ** -0.5, 3.0, ((0, 4),)),
        "out_bias": normal_values(seeds[11], (D,), 0.1, 0.59765625, ((0, 4),)),
        "ln2_gain": jnp.clip(1.0 + 0.1 * jax.random.normal(seeds[12], (D,), jnp.float32), 0.5, 1.5).astype(jnp.bfloat16),
        "ln2_bias": normal_values(seeds[13], (D,), 0.1, 0.59765625, ((0, 4),)),
        "w_in": normal_values(seeds[14], (EXPERTS, D, FF), D ** -0.5, 0.1875, ((1, 4),)),
        "in_bias": normal_values(seeds[15], (EXPERTS, FF), 0.1, 0.59765625, ((1, 4),)),
        "w_back": normal_values(seeds[16], (EXPERTS, FF, D), FF ** -0.5, 0.09375, ((1, 4),)),
        "back_bias": normal_values(seeds[17], (EXPERTS, D), 0.1, 0.59765625, ((1, 4),)),
    }


epsilon = 1e-05
highest = lax.Precision.HIGHEST

@jax.custom_vjp
def low(v):
    return lax.optimization_barrier(v.astype(jnp.bfloat16)).astype(jnp.float32)

@jax.custom_vjp
def low_back(v):
    return v

def low_keep(v):
    return (low(v), None)

def low_pass(kept, grad):
    return (grad,)

def back_keep(v):
    return (v, None)

def back_low(kept, grad):
    return (low(grad),)
low.defvjp(low_keep, low_pass)
low_back.defvjp(back_keep, back_low)

def normalize(tok_rows, norm_gain, norm_bias):
    row_mean = lax.optimization_barrier(jnp.mean(tok_rows, axis=-1, keepdims=True))
    centred = tok_rows - row_mean
    variance = lax.optimization_barrier(jnp.mean(centred * centred, axis=-1, keepdims=True))
    return centred * lax.rsqrt(variance + epsilon) * norm_gain + norm_bias

def piece_ids(positions, seq_starts):
    inside = (positions[:, None] >= seq_starts[None, :]) & (positions[:, None] < seq_starts[None, :] + PIECE_LEN)
    numbers = jnp.arange(1, seq_starts.shape[0] + 1, dtype=jnp.int32)
    return (lax.optimization_barrier(jnp.sum(jnp.where(inside, numbers[None, :], 0), axis=1)) - 1).astype(jnp.int32)

def allowed(query_pos, query_piece, key_pos, key_piece):
    causal = key_pos[None, :] <= query_pos[:, None]
    within = (query_piece[:, None] == key_piece[None, :]) & (query_piece[:, None] >= 0)
    return causal | within

def routing(expert_of):
    chosen = expert_of[:, None] == jnp.arange(EXPERTS, dtype=jnp.int32)[None, :]
    running = jnp.cumsum(chosen.astype(jnp.int32), axis=0) - 1
    slot_of = lax.optimization_barrier(jnp.sum(jnp.where(chosen, running, 0), axis=1)).astype(jnp.int32)
    slot_ids = jnp.arange(CAP, dtype=jnp.int32)
    return chosen.T[:, None, :] & (slot_of[None, None, :] == slot_ids[None, :, None])

def expert_block(normed_rows, expert_of, w_in, in_bias, w_back, back_bias):
    dispatch = routing(expert_of).astype(jnp.float32)
    inputs = low_back(jnp.einsum('ect,td->ecd', dispatch, normed_rows, precision=highest))
    hidden_pre = low_back(jnp.einsum('ecd,edf->ecf', inputs, w_in, precision=highest) + in_bias[:, None, :])
    hidden = low(jnp.maximum(hidden_pre, 0.0))
    result = jnp.einsum('ecf,efd->ecd', hidden, w_back, precision=highest) + back_bias[:, None, :]
    return jnp.einsum('ect,ecd->td', dispatch, result, precision=highest)

def sequence_block(params, seq_rows, seq_ids, seq_starts, hash_table):
    ln1_gain, ln1_bias, w_qkv, w_out, out_bias, ln2_gain, ln2_bias, w_in, in_bias, w_back, back_bias = params
    length = seq_rows.shape[0]
    normed = low(normalize(seq_rows, ln1_gain, ln1_bias))
    qkv_all = low(low_back(jnp.dot(normed, w_qkv, precision=highest)))
    queries = qkv_all[:, :D].reshape(length, HEADS, HEAD_DIM)
    keys_all = qkv_all[:, D:2 * D].reshape(length, HEADS, HEAD_DIM)
    values_all = qkv_all[:, 2 * D:].reshape(length, HEADS, HEAD_DIM)
    scores = low_back(jnp.einsum('qhd,khd->hqk', queries, keys_all, precision=highest) * float(HEAD_DIM) ** (-0.5))
    positions = jnp.arange(length, dtype=jnp.int32)
    pieces = piece_ids(positions, seq_starts)
    visible = allowed(positions, pieces, positions, pieces)
    masked = jnp.where(visible[None], scores, -1e+30)
    row_peak = lax.optimization_barrier(jnp.max(masked, axis=-1, keepdims=True))
    raised = jnp.exp(masked - row_peak)
    attn_probs = low(raised / lax.optimization_barrier(jnp.sum(raised, axis=-1, keepdims=True)))
    attn_mixed = jnp.einsum('hqk,khd->qhd', attn_probs, values_all, precision=highest).reshape(length, D)
    attn_mixed = low(low_back(attn_mixed))
    branch = low_back(jnp.dot(attn_mixed, w_out, precision=highest) + out_bias)
    middle = seq_rows + branch
    normed_two = low(normalize(middle, ln2_gain, ln2_bias))
    expert_of = jnp.take(hash_table, seq_ids)
    moe_out = jax.vmap(expert_block, in_axes=(0, 0, None, None, None, None))(normed_two.reshape(N_SHARD, TOK_DEV, D), expert_of.reshape(N_SHARD, TOK_DEV), w_in, in_bias, w_back, back_bias)
    return middle + low_back(moe_out.reshape(length, D))

def forward(params, tok_rows, token_ids, piece_starts, hash_table):

    def scan_step(state_in, packed):
        seq_rows, seq_ids, seq_starts = packed
        return (state_in, jax.checkpoint(sequence_block)(params, seq_rows, seq_ids, seq_starts, hash_table))
    ignored, outputs = lax.scan(scan_step, jnp.zeros((), jnp.int32), (tok_rows.reshape(SEQS, SEQ_LEN, D), token_ids.reshape(SEQS, SEQ_LEN), piece_starts))
    return outputs.reshape(SEQS * SEQ_LEN, D)

def reference(tokens, token_ids, hash_table, piece_starts, valid_mask, teacher, cotangent, ln1_gain, ln1_bias, w_qkv, w_out, out_bias, ln2_gain, ln2_bias, w_in, in_bias, w_back, back_bias):
    params = tuple((weight.astype(jnp.float32) for weight in (ln1_gain, ln1_bias, w_qkv, w_out, out_bias, ln2_gain, ln2_bias, w_in, in_bias, w_back, back_bias)))

    def run_block(block_params, block_rows):
        return forward(block_params, block_rows, token_ids, piece_starts, hash_table)
    final, pull_back = jax.vjp(run_block, params, tokens.astype(jnp.float32))
    counted = valid_mask.astype(jnp.float32)
    count_all = jnp.sum(counted)
    grad_final = cotangent.astype(jnp.float32) + TOKENS / (2.0 * count_all) * counted[:, None] * (final - teacher.astype(jnp.float32))
    grad_params, input_grad = pull_back(grad_final)
    g_gain_one, g_bias_one, g_qkv, g_out, g_out_bias, g_gain_two, g_bias_two, g_in, g_in_bias, g_back, g_back_bias = grad_params
    return (final.astype(jnp.bfloat16), input_grad, g_gain_one, g_bias_one, g_qkv, g_out, g_out_bias, g_gain_two, g_bias_two, g_in, g_in_bias, g_back, g_back_bias)
```

```python
import functools

import jax
import jax.numpy as jnp
from jax import lax
from jax.experimental import pallas as pl
from jax.experimental.pallas import tpu as pltpu
from jax.sharding import PartitionSpec as P

D = 1024
HEADS = 16
HEAD_DIM = 64
EXPERTS = 2
PIECE_LEN = 256
CAP = 320
N_SHARD = 4
OWN_HEADS = HEADS // N_SHARD
OWN = OWN_HEADS * HEAD_DIM
TILE = 256
NEG = -1e30

epsilon = 1e-05
f32 = jnp.float32
bf16 = jnp.bfloat16


def layer_norm(tok_rows):
    row_mean = jnp.mean(tok_rows, axis=-1, keepdims=True)
    centred = tok_rows - row_mean
    variance = jnp.mean(centred * centred, axis=-1, keepdims=True)
    inverse = lax.rsqrt(variance + epsilon)
    return (centred * inverse, inverse)


def norm_back(upstream, normed, inverse, norm_gain):
    scaled = upstream * norm_gain
    first_mean = jnp.mean(scaled, axis=-1, keepdims=True)
    second_mean = jnp.mean(scaled * normed, axis=-1, keepdims=True)
    return inverse * (scaled - first_mean - normed * second_mean)


def dot_nn(a, b):
    return lax.dot_general(a, b, (((1,), (0,)), ((), ())), preferred_element_type=f32)


def dot_nt(a, b):
    return lax.dot_general(a, b, (((1,), (1,)), ((), ())), preferred_element_type=f32)


def dot_tn(a, b):
    return lax.dot_general(a, b, (((0,), (0,)), ((), ())), preferred_element_type=f32)


def swap(value, mask):
    return lax.ppermute(value, "shard", [(i, i ^ mask) for i in range(N_SHARD)])


def gather_blocks(value):
    far = swap(value, 2)
    near = swap(value, 1)
    return (value, near, far, swap(far, 1))


def exchange_blocks(blocks):
    return (blocks[0], swap(blocks[1], 1), swap(blocks[2], 2), swap(blocks[3], 3))


def scatter_far(block_two, block_three):
    near = swap(block_three, 1)
    return swap((block_two.astype(f32) + near.astype(f32)).astype(bf16), 2)


def scatter_near(block_zero, block_one, far):
    near = swap(block_one, 1)
    return block_zero.astype(f32) + near.astype(f32) + far.astype(f32)


def rep_masks(count):
    masks = []
    step = 1
    while step < count:
        masks.append(step)
        step *= 2
    if count == 8:
        return [(1, (1,)), (2, (2, 4)), (6, (4,))]
    return [(m, (m,)) for m in masks]


def rep_pair(value, mask, count):
    return lax.ppermute(value, "rep", [(i, i ^ mask) for i in range(count)])


def rep_side(bits):
    index = lax.axis_index("rep")
    side = jnp.zeros((), jnp.int32)
    for bit in bits:
        side = side ^ ((index & bit) // bit)
    return side


def rep_sum_part(value, turn, count):
    dims = rep_masks(count)
    turn = turn % len(dims)
    dims = dims[turn:] + dims[:turn]
    sides = [rep_side(bits) for unused, bits in dims]
    for (mask, unused), side in zip(dims, sides):
        half = value.shape[0] // 2
        split = value.reshape(2, half, value.shape[1])
        send = lax.dynamic_index_in_dim(split, 1 - side, 0, keepdims=False)
        keep = lax.dynamic_index_in_dim(split, side, 0, keepdims=False)
        other = rep_pair(send, mask, count)
        value = (keep.astype(f32) + other.astype(f32)).astype(bf16)
    for (mask, unused), side in reversed(list(zip(dims, sides))):
        other = rep_pair(value, mask, count)
        value = jnp.where(
            side == 0,
            jnp.concatenate([value, other], axis=0),
            jnp.concatenate([other, value], axis=0),
        )
    return value


def rep_sum(value, parts, count):
    if count == 1:
        return value
    if count & (count - 1) or value.shape[0] % (16 * count):
        return lax.psum(value, "rep")
    unit = 16 * count
    total = value.shape[0] // unit
    parts = min(parts, total)
    sizes = [(total // parts + (1 if p >= parts - total % parts else 0)) * unit for p in range(parts)]
    pieces, start = [], 0
    for turn, size in enumerate(sizes):
        pieces.append(rep_sum_part(value[start : start + size], turn, count))
        start += size
    return jnp.concatenate(pieces, axis=0)


def visible_tile(key_block, query_block, starts):
    key_pos = key_block * TILE + lax.broadcasted_iota(jnp.int32, (TILE, TILE), 0)
    query_pos = query_block * TILE + lax.broadcasted_iota(jnp.int32, (TILE, TILE), 1)
    seen = key_pos <= query_pos
    for start in starts:
        low = jnp.minimum(key_pos, query_pos)
        high = jnp.maximum(key_pos, query_pos)
        seen = seen | ((low >= start) & (high < start + PIECE_LEN))
    return seen


def crosses(boundary, starts):
    met = jnp.bool_(False)
    for start in starts:
        met = met | ((start < boundary) & (start + PIECE_LEN > boundary))
    return met


def head_lanes(rows):
    return lax.broadcasted_iota(jnp.int32, (rows, OWN), 1) // HEAD_DIM


def attend_kernel(blocks, facts, near, far, mixed, logs, q_own, k_own, v_turned, acc, top, total):
    me = facts[0]
    starts = [facts[1 + i] for i in range(facts.shape[0] - 1)]
    for j in range(N_SHARD):
        src = near if j < 2 else far
        base = (j % 2) * 2 * TILE
        for half in range(2):
            rows = slice(base + half * TILE, base + (half + 1) * TILE)
            at = (me ^ j) * 2 + half
            q_own[at] = src[rows, 0:OWN] * jnp.asarray(HEAD_DIM**-0.5, bf16)
            k_own[at] = src[rows, OWN : 2 * OWN]
            v_turned[at] = src[rows, 2 * OWN : 3 * OWN].astype(f32).T.astype(bf16)
    lanes = head_lanes(TILE)

    def query_block(i, unused):
        q_i = q_own[i]
        q_heads = [jnp.where(lanes == h, q_i, jnp.zeros_like(q_i)) for h in range(OWN_HEADS)]
        acc[...] = jnp.zeros_like(acc)
        top[...] = jnp.full_like(top, NEG)
        total[...] = jnp.zeros_like(total)

        def key_block(j, masked):
            k_j = k_own[j]
            v_j = v_turned[j]
            seen = visible_tile(j, i, starts) if masked else None
            for h in range(OWN_HEADS):
                scores = dot_nt(k_j, q_heads[h])
                if masked:
                    scores = jnp.where(seen, scores, NEG)
                old_top = top[h : h + 1, :]
                new_top = jnp.maximum(old_top, jnp.max(scores, axis=0, keepdims=True))
                raised = jnp.exp(scores - new_top)
                fade = jnp.exp(old_top - new_top)
                top[h : h + 1, :] = new_top
                total[h : h + 1, :] = total[h : h + 1, :] * fade + jnp.sum(
                    raised, axis=0, keepdims=True
                )
                part = dot_nn(v_j[h * HEAD_DIM : (h + 1) * HEAD_DIM, :], raised.astype(bf16))
                rows = slice(h * HEAD_DIM, (h + 1) * HEAD_DIM)
                acc[rows, :] = acc[rows, :] * fade + part

        def plain(j, unused):
            key_block(j, False)
            return unused

        lax.fori_loop(0, i, plain, 0)
        key_block(i, True)

        @pl.when((i + 1 < blocks) & crosses((i + 1) * TILE, starts))
        def _():
            key_block(i + 1, True)

        for h in range(OWN_HEADS):
            rows = slice(h * HEAD_DIM, (h + 1) * HEAD_DIM)
            acc[rows, :] = acc[rows, :] / total[h : h + 1, :]
        place = ((i // 2) ^ me) * (2 * TILE) + (i % 2) * TILE
        mixed[pl.ds(pl.multiple_of(place, TILE), TILE), :] = acc[...].T.astype(bf16)
        logs[i] = top[...] + jnp.log(jnp.maximum(total[...], 1e-30))
        return unused

    lax.fori_loop(0, blocks, query_block, 0)


def attend(facts, near, far):
    rows = near.shape[0] + far.shape[0]
    blocks = rows // TILE
    vmem = pl.BlockSpec(memory_space=pltpu.VMEM)
    return pl.pallas_call(
        functools.partial(attend_kernel, blocks),
        out_shape=(
            jax.ShapeDtypeStruct((rows, OWN), bf16),
            jax.ShapeDtypeStruct((blocks, 8, TILE), f32),
        ),
        in_specs=[pl.BlockSpec(memory_space=pltpu.SMEM), vmem, vmem],
        out_specs=(vmem, vmem),
        scratch_shapes=[
            pltpu.VMEM((blocks, TILE, OWN), bf16),
            pltpu.VMEM((blocks, TILE, OWN), bf16),
            pltpu.VMEM((blocks, OWN, TILE), bf16),
            pltpu.VMEM((OWN, TILE), f32),
            pltpu.VMEM((8, TILE), f32),
            pltpu.VMEM((8, TILE), f32),
        ],
        compiler_params=pltpu.CompilerParams(vmem_limit_bytes=48 * 2**20),
        cost_estimate=pl.CostEstimate(
            flops=rows * rows * OWN * 8, bytes_accessed=rows * OWN * 10, transcendentals=rows * rows * 2
        ),
        name="attend",
    )(facts, near, far)


def attend_back_kernel(
    blocks, facts, near, far, mixed, g0, g1, g2, g3, logs, grads,
    q_own, k_own, v_own, k_turned, g_own, q_heads, g_heads, deltas, q_grad, k_grad, v_grad, k_heads, v_heads,
):
    me = facts[0]
    starts = [facts[1 + i] for i in range(facts.shape[0] - 1)]
    lanes = head_lanes(TILE)
    pick = (
        lax.broadcasted_iota(jnp.int32, (8, OWN), 1) // HEAD_DIM
        == lax.broadcasted_iota(jnp.int32, (8, OWN), 0)
    ).astype(f32)
    for j in range(N_SHARD):
        src = near if j < 2 else far
        grad_src = (g0, g1, g2, g3)[j]
        base = (j % 2) * 2 * TILE
        for half in range(2):
            rows = slice(base + half * TILE, base + (half + 1) * TILE)
            at = (me ^ j) * 2 + half
            q_tile = src[rows, 0:OWN] * jnp.asarray(HEAD_DIM**-0.5, bf16)
            k_tile = src[rows, OWN : 2 * OWN]
            g_tile = grad_src[half * TILE : (half + 1) * TILE, :]
            o_tile = mixed[j * 2 * TILE + half * TILE : j * 2 * TILE + (half + 1) * TILE, :]
            q_own[at] = q_tile
            k_own[at] = k_tile
            v_own[at] = src[rows, 2 * OWN : 3 * OWN]
            k_turned[at] = k_tile.astype(f32).T.astype(bf16)
            g_own[at] = g_tile
            for h in range(OWN_HEADS):
                q_heads[at, h * TILE : (h + 1) * TILE, :] = jnp.where(lanes == h, q_tile, jnp.zeros_like(q_tile))
                g_heads[at, h * TILE : (h + 1) * TILE, :] = jnp.where(lanes == h, g_tile, jnp.zeros_like(g_tile))
            both = g_tile.astype(f32) * o_tile.astype(f32)
            deltas[at] = lax.dot_general(
                pick, both, (((1,), (1,)), ((), ())),
                precision=lax.Precision.HIGHEST, preferred_element_type=f32,
            )
    q_grad[...] = jnp.zeros_like(q_grad)

    def key_block(j, unused):
        k_j = k_own[j]
        v_j = v_own[j]
        for h in range(OWN_HEADS):
            k_heads[h * TILE : (h + 1) * TILE, :] = jnp.where(lanes == h, k_j, jnp.zeros_like(k_j))
            v_heads[h * TILE : (h + 1) * TILE, :] = jnp.where(lanes == h, v_j, jnp.zeros_like(v_j))
        k_grad[...] = jnp.zeros_like(k_grad)
        v_grad[...] = jnp.zeros_like(v_grad)

        def query_block(i, masked):
            q_i = q_own[i]
            g_i = g_own[i]
            kt = k_turned[j]
            seen = visible_tile(j, i, starts) if masked else None
            softs = []
            scored = []
            for h in range(OWN_HEADS):
                rows = slice(h * TILE, (h + 1) * TILE)
                scores = dot_nt(k_heads[rows, :], q_i)
                soft = jnp.exp(scores - logs[i, h : h + 1, :])
                if masked:
                    soft = jnp.where(seen, soft, 0.0)
                grad_soft = dot_nt(v_heads[rows, :], g_i)
                grad_scores = (soft * (grad_soft - deltas[i, h : h + 1, :])).astype(bf16)
                softs.append(soft.astype(bf16))
                scored.append(grad_scores)
                head = slice(h * HEAD_DIM, (h + 1) * HEAD_DIM)
                q_grad[i, head, :] += dot_nn(kt[head, :], grad_scores)
            v_grad[...] += dot_nn(jnp.concatenate(softs, axis=1), g_heads[i])
            k_grad[...] += dot_nn(jnp.concatenate(scored, axis=1), q_heads[i])

        def plain(i, unused):
            query_block(i, False)
            return unused

        @pl.when((j > 0) & crosses(j * TILE, starts))
        def _():
            query_block(j - 1, True)

        query_block(j, True)
        lax.fori_loop(j + 1, blocks, plain, 0)
        place = pl.multiple_of(((j // 2) ^ me) * (2 * TILE) + (j % 2) * TILE, TILE)
        grads[pl.ds(place, TILE), OWN : 2 * OWN] = k_grad[...].astype(bf16)
        grads[pl.ds(place, TILE), 2 * OWN : 3 * OWN] = v_grad[...].astype(bf16)
        return unused

    lax.fori_loop(0, blocks, key_block, 0)

    def write_query(i, unused):
        place = pl.multiple_of(((i // 2) ^ me) * (2 * TILE) + (i % 2) * TILE, TILE)
        grads[pl.ds(place, TILE), 0:OWN] = (q_grad[i] * HEAD_DIM**-0.5).T.astype(bf16)
        return unused

    lax.fori_loop(0, blocks, write_query, 0)


def attend_back(facts, near, far, mixed, grad_blocks, logs):
    rows = near.shape[0] + far.shape[0]
    blocks = rows // TILE
    vmem = pl.BlockSpec(memory_space=pltpu.VMEM)
    tile = lambda n, m, kind: pltpu.VMEM((n, m), kind)
    stack = lambda n, m, kind: pltpu.VMEM((blocks, n, m), kind)
    return pl.pallas_call(
        functools.partial(attend_back_kernel, blocks),
        out_shape=jax.ShapeDtypeStruct((rows, 3 * OWN), bf16),
        in_specs=[pl.BlockSpec(memory_space=pltpu.SMEM)] + [vmem] * 8,
        out_specs=vmem,
        scratch_shapes=[
            stack(TILE, OWN, bf16),
            stack(TILE, OWN, bf16),
            stack(TILE, OWN, bf16),
            stack(OWN, TILE, bf16),
            stack(TILE, OWN, bf16),
            stack(OWN_HEADS * TILE, OWN, bf16),
            stack(OWN_HEADS * TILE, OWN, bf16),
            stack(8, TILE, f32),
            stack(OWN, TILE, f32),
            tile(TILE, OWN, f32),
            tile(TILE, OWN, f32),
            tile(OWN_HEADS * TILE, OWN, bf16),
            tile(OWN_HEADS * TILE, OWN, bf16),
        ],
        compiler_params=pltpu.CompilerParams(vmem_limit_bytes=56 * 2**20),
        cost_estimate=pl.CostEstimate(
            flops=rows * rows * OWN * 20, bytes_accessed=rows * OWN * 20, transcendentals=rows * rows * 2
        ),
        name="attend_back",
    )(facts, near, far, mixed, *grad_blocks, logs)


def expert_tile(counts, step, tiles):
    block = step // tiles
    start = (step % tiles) * TILE
    border = counts[block, 0] - start
    late = lax.broadcasted_iota(jnp.int32, (TILE, 1), 0) >= border
    return border, late


def expert_kernel(tiles, counts, rows_a, rows_b, w_in, in_bias, w_back, hidden, out_a, out_b, held):
    step = pl.program_id(0)
    border, late = expert_tile(counts, step, tiles)

    def work(rows, out):
        @pl.when(border > 0)
        def _():
            held[...] = jnp.maximum(dot_nn(rows[...], w_in[0]) + in_bias[0:1, :], 0.0).astype(bf16)

        @pl.when(border < TILE)
        def _():
            one = jnp.maximum(dot_nn(rows[...], w_in[1]) + in_bias[1:2, :], 0.0).astype(bf16)
            held[...] = jnp.where(late, one, held[...])

        hidden[...] = held[...]

        @pl.when(border > 0)
        def _():
            out[...] = dot_nn(held[...], w_back[0]).astype(bf16)

        @pl.when(border < TILE)
        def _():
            out[...] = jnp.where(late, dot_nn(held[...], w_back[1]).astype(bf16), out[...])

    @pl.when(step < tiles)
    def _():
        work(rows_a, out_a)

    @pl.when(step >= tiles)
    def _():
        work(rows_b, out_b)


def expert_back_kernel(tiles, counts, rows_a, rows_b, hidden, w_in, w_back, grad_pre, out_a, out_b, held):
    step = pl.program_id(0)
    border, late = expert_tile(counts, step, tiles)

    def work(rows, out):
        alive = hidden[...] > 0

        @pl.when(border > 0)
        def _():
            held[...] = jnp.where(alive, dot_nt(rows[...], w_back[0]), 0.0).astype(bf16)

        @pl.when(border < TILE)
        def _():
            one = jnp.where(alive, dot_nt(rows[...], w_back[1]), 0.0).astype(bf16)
            held[...] = jnp.where(late, one, held[...])

        grad_pre[...] = held[...]

        @pl.when(border > 0)
        def _():
            out[...] = dot_nt(held[...], w_in[0]).astype(bf16)

        @pl.when(border < TILE)
        def _():
            out[...] = jnp.where(late, dot_nt(held[...], w_in[1]).astype(bf16), out[...])

    @pl.when(step < tiles)
    def _():
        work(rows_a, out_a)

    @pl.when(step >= tiles)
    def _():
        work(rows_b, out_b)


def expert_specs(rows, width, inner):
    tiles = rows // TILE
    first = pl.BlockSpec((TILE, width), lambda i, c: (jnp.minimum(i, tiles - 1), 0))
    second = pl.BlockSpec((TILE, width), lambda i, c: (jnp.maximum(i - tiles, 0), 0))
    both = pl.BlockSpec((TILE, inner), lambda i, c: (i, 0))
    once = pl.Buffered(1)
    w_in = pl.BlockSpec((EXPERTS, width, inner), lambda i, c: (0, 0, 0), pipeline_mode=once)
    w_back = pl.BlockSpec((EXPERTS, inner, width), lambda i, c: (0, 0, 0), pipeline_mode=once)
    bias = pl.BlockSpec((EXPERTS, inner), lambda i, c: (0, 0), pipeline_mode=once)
    return tiles, first, second, both, w_in, w_back, bias


def run_experts(counts, rows_a, rows_b, w_in, in_bias, w_back):
    rows, width = rows_a.shape
    inner = w_in.shape[2]
    tiles, first, second, both, in_spec, back_spec, bias_spec = expert_specs(rows, width, inner)
    return pl.pallas_call(
        functools.partial(expert_kernel, tiles),
        grid_spec=pltpu.PrefetchScalarGridSpec(
            num_scalar_prefetch=1,
            grid=(2 * tiles,),
            in_specs=[first, second, in_spec, bias_spec, back_spec],
            out_specs=[both, first, second],
            scratch_shapes=[pltpu.VMEM((TILE, inner), bf16)],
        ),
        out_shape=(
            jax.ShapeDtypeStruct((2 * rows, inner), bf16),
            jax.ShapeDtypeStruct((rows, width), bf16),
            jax.ShapeDtypeStruct((rows, width), bf16),
        ),
        compiler_params=pltpu.CompilerParams(vmem_limit_bytes=40 * 2**20),
        cost_estimate=pl.CostEstimate(
            flops=2 * rows * width * inner * 4, bytes_accessed=4 * width * inner * 2, transcendentals=0
        ),
        name="experts",
    )(counts, rows_a, rows_b, w_in, in_bias, w_back)


def run_experts_back(counts, rows_a, rows_b, hidden, w_in, w_back):
    rows, width = rows_a.shape
    inner = w_in.shape[2]
    tiles, first, second, both, in_spec, back_spec, bias_spec = expert_specs(rows, width, inner)
    return pl.pallas_call(
        functools.partial(expert_back_kernel, tiles),
        grid_spec=pltpu.PrefetchScalarGridSpec(
            num_scalar_prefetch=1,
            grid=(2 * tiles,),
            in_specs=[first, second, both, in_spec, back_spec],
            out_specs=[both, first, second],
            scratch_shapes=[pltpu.VMEM((TILE, inner), bf16)],
        ),
        out_shape=(
            jax.ShapeDtypeStruct((2 * rows, inner), bf16),
            jax.ShapeDtypeStruct((rows, width), bf16),
            jax.ShapeDtypeStruct((rows, width), bf16),
        ),
        compiler_params=pltpu.CompilerParams(vmem_limit_bytes=40 * 2**20),
        cost_estimate=pl.CostEstimate(
            flops=2 * rows * width * inner * 4, bytes_accessed=4 * width * inner * 2, transcendentals=0
        ),
        name="experts_back",
    )(counts, rows_a, rows_b, hidden, w_in, w_back)


def shards(
    n_rep,
    tokens,
    token_ids,
    hash_table,
    piece_starts,
    valid_mask,
    teacher,
    cotangent,
    ln1_gain,
    ln1_bias,
    w_qkv,
    w_out,
    out_bias,
    ln2_gain,
    ln2_bias,
    w_in,
    in_bias,
    w_back,
    back_bias,
):
    local_rows = tokens.shape[0]
    tokens_all = local_rows * N_SHARD * n_rep
    me = lax.axis_index("shard").astype(jnp.int32)
    rep_at = lax.axis_index("rep")
    inner = w_back.shape[1]
    facts = jnp.concatenate([me[None], piece_starts[0]])

    tok_blocks = gather_blocks(tokens)

    expert_of = jnp.take(hash_table, token_ids)
    places = jnp.arange(local_rows, dtype=jnp.int32)
    earlier = (expert_of[:, None] == expert_of[None, :]) & (places[None, :] < places[:, None])
    slot_of = jnp.sum(earlier.astype(jnp.int32), axis=1)
    kept = slot_of < CAP
    is_late = expert_of > 0
    late_count = jnp.sum(is_late.astype(jnp.int32))
    own_counts = jnp.stack(
        [jnp.minimum(local_rows - late_count, CAP), jnp.minimum(late_count, CAP)]
    )
    sorted_at = jnp.where(kept, slot_of + jnp.where(is_late, own_counts[0], 0), -1)
    sorter = (sorted_at[None, :] == places[:, None]).astype(bf16)

    counted = valid_mask.astype(f32)
    own_count = jnp.sum(counted)
    shard_width = ln1_gain.shape[0]
    lasts = jnp.zeros((1, shard_width), f32)
    lasts = lasts.at[0, 0].set(own_counts[0].astype(f32)).at[0, 1].set(own_count)
    packed = jnp.concatenate(
        [
            jnp.stack([v.astype(f32) for v in (ln1_gain, ln1_bias, out_bias, ln2_gain, ln2_bias)]),
            back_bias.astype(f32),
            lasts,
        ],
        axis=0,
    )
    everyone = lax.all_gather(packed, ("rep", "shard"), axis=0).reshape(
        n_rep, N_SHARD, 8, shard_width
    )
    count_all = jnp.sum(everyone[:, :, 7, 1])
    mine = lax.dynamic_index_in_dim(everyone, rep_at, 0, keepdims=False)
    rows_of = mine[:, :7].transpose(1, 0, 2).reshape(7, N_SHARD * shard_width)
    gain_one, bias_one, out_shift, gain_two, bias_two = [rows_of[i] for i in range(5)]
    back_shift = rows_of[5:7]
    borders = jnp.take(mine[:, 7, 0], me ^ jnp.arange(N_SHARD, dtype=jnp.int32)).astype(jnp.int32)
    counts_near, counts_far = borders[:2, None], borders[2:, None]

    heads_in = w_qkv.reshape(shard_width, 3, N_SHARD, OWN)
    qkv_weight = lax.all_to_all(heads_in, "shard", split_axis=2, concat_axis=0, tiled=True)
    qkv_weight = qkv_weight.reshape(D, 3 * OWN)
    slice_width = inner // n_rep
    thin = lax.dynamic_index_in_dim(
        w_in.reshape(EXPERTS, shard_width, N_SHARD, n_rep, slice_width), rep_at, 3, keepdims=False
    )
    thin = lax.all_to_all(thin, "shard", split_axis=2, concat_axis=1, tiled=True)
    in_weight = lax.all_gather(thin.reshape(EXPERTS, D, slice_width), "rep", axis=0)
    in_weight = in_weight.transpose(1, 2, 0, 3).reshape(EXPERTS, D, inner)
    out_blocks = gather_blocks(w_out)

    def first_rows(block):
        normed, inverse = layer_norm(block.astype(f32))
        return (normed * gain_one + bias_one).astype(bf16), normed, inverse

    first_near = jnp.concatenate([first_rows(tok_blocks[0])[0], first_rows(tok_blocks[1])[0]], axis=0)
    first_far = jnp.concatenate([first_rows(tok_blocks[2])[0], first_rows(tok_blocks[3])[0]], axis=0)
    qkv_near = dot_nn(first_near, qkv_weight).astype(bf16)
    qkv_far = dot_nn(first_far, qkv_weight).astype(bf16)

    mixed, logs = attend(facts, qkv_near, qkv_far)
    mixed_blocks = exchange_blocks(
        [mixed[j * local_rows : (j + 1) * local_rows] for j in range(N_SHARD)]
    )
    tok_rows = tokens.astype(f32)
    branch = dot_nn(mixed_blocks[0], out_blocks[0])
    for j in range(1, N_SHARD):
        branch = branch + dot_nn(mixed_blocks[j], out_blocks[j])
    middle = tok_rows + branch + out_shift
    normed_two, inverse_two = layer_norm(middle)
    second_in = (normed_two * gain_two + bias_two).astype(bf16)
    sorted_in = dot_nn(sorter, second_in).astype(bf16)
    rows_in = gather_blocks(sorted_in)
    bias_in = in_bias.astype(f32)
    hidden_near, out0, out1 = run_experts(counts_near, rows_in[0], rows_in[1], in_weight, bias_in, w_back)
    hidden_far, out2, out3 = run_experts(counts_far, rows_in[2], rows_in[3], in_weight, bias_in, w_back)
    summed = scatter_near(out0, out1, scatter_far(out2, out3))
    picked = dot_tn(sorter, summed.astype(bf16))
    picked = picked + jnp.where(is_late[:, None], back_shift[1], back_shift[0])
    final = middle + jnp.where(kept[:, None], picked, 0.0)
    grad_final = cotangent.astype(f32) + tokens_all / (2.0 * count_all) * counted[:, None] * (
        final - teacher.astype(f32)
    )
    grad_low = grad_final.astype(bf16)

    sorted_grad = dot_nn(sorter, grad_low).astype(bf16)
    rows_grad = gather_blocks(sorted_grad)
    pre_near, gin0, gin1 = run_experts_back(
        counts_near, rows_grad[0], rows_grad[1], hidden_near, in_weight, w_back
    )
    pre_far, gin2, gin3 = run_experts_back(
        counts_far, rows_grad[2], rows_grad[3], hidden_far, in_weight, w_back
    )
    summed_grad = scatter_near(gin0, gin1, scatter_far(gin2, gin3))
    grad_second = dot_tn(sorter, summed_grad.astype(bf16))

    early = (jnp.arange(local_rows, dtype=jnp.int32)[None, :] < borders[:, None]).reshape(-1)
    hidden_all = jnp.concatenate([hidden_near, hidden_far], axis=0)
    pre_all = jnp.concatenate([pre_near, pre_far], axis=0)
    in_all = jnp.concatenate(rows_in, axis=0)
    grad_all = jnp.concatenate(rows_grad, axis=0)
    masks = [early[:, None], ~early[:, None]]
    back_grad = jnp.concatenate(
        [dot_tn(jnp.where(m, hidden_all, 0), grad_all).astype(bf16) for m in masks], axis=0
    )
    in_grad = [dot_tn(in_all, jnp.where(m, pre_all, 0)).astype(bf16) for m in masks]
    in_shift_grad = jnp.stack([jnp.sum(jnp.where(m, pre_all.astype(f32), 0), axis=0) for m in masks])
    back_grad = rep_sum(back_grad, 3, n_rep)

    grad_gain_two = jnp.sum(grad_second * normed_two, axis=0)
    grad_bias_two = jnp.sum(grad_second, axis=0)
    grad_middle = grad_final + norm_back(grad_second, normed_two, inverse_two, gain_two)
    grad_branch = grad_middle.astype(bf16)
    grad_out_shift = jnp.sum(grad_branch.astype(f32), axis=0)
    grad_mixed = exchange_blocks([dot_nt(grad_branch, w).astype(bf16) for w in out_blocks])

    grad_qkv = attend_back(facts, qkv_near, qkv_far, mixed, grad_mixed, logs)

    def row_block(array, j, size):
        return lax.dynamic_slice_in_dim(array, (me ^ j) * size, size, axis=0)

    in_parts = exchange_blocks(
        [
            jnp.concatenate([row_block(g, j, shard_width) for g in in_grad], axis=0)
            for j in range(N_SHARD)
        ]
    )
    in_parts = rep_sum(jnp.concatenate(in_parts, axis=0), 3, n_rep)

    out_parts = [dot_tn(b, grad_branch).astype(bf16) for b in mixed_blocks]
    out_grad = scatter_near(
        out_parts[0], out_parts[1], scatter_far(out_parts[2], out_parts[3])
    ).astype(bf16)

    first_grads = [
        dot_nt(grad_qkv[j * local_rows : (j + 1) * local_rows], qkv_weight).astype(bf16)
        for j in range(N_SHARD)
    ]
    grad_first = scatter_near(first_grads[0], first_grads[1], scatter_far(first_grads[2], first_grads[3]))
    first_all = jnp.concatenate([first_near, first_far], axis=0)
    qkv_grad = dot_tn(first_all, grad_qkv).astype(bf16)
    qkv_parts = exchange_blocks([row_block(qkv_grad, j, shard_width) for j in range(N_SHARD)])
    qkv_parts = jnp.concatenate(qkv_parts, axis=0)
    last_rows = jnp.concatenate([qkv_parts.reshape(-1, D), out_grad], axis=0)
    last_rows = rep_sum(last_rows, 3, n_rep)
    split_at = last_rows.shape[0] - out_grad.shape[0]
    qkv_parts = last_rows[:split_at].reshape(N_SHARD, shard_width, 3, OWN)
    out_grad = last_rows[split_at:].astype(f32)

    first_in, normed_one, inverse_one = first_rows(tokens)
    grad_gain_one = jnp.sum(grad_first * normed_one, axis=0)
    grad_bias_one = jnp.sum(grad_first, axis=0)
    input_grad = grad_middle + norm_back(grad_first, normed_one, inverse_one, gain_one)

    by_expert = jnp.stack([(kept & ~is_late), (kept & is_late)]).astype(bf16)
    grad_back_shift = dot_nn(by_expert, grad_low)
    small = jnp.concatenate(
        [
            jnp.stack([grad_gain_one, grad_bias_one, grad_out_shift, grad_gain_two, grad_bias_two]),
            grad_back_shift,
        ],
        axis=0,
    )
    small = lax.psum(small, ("rep", "shard"))
    small = lax.dynamic_slice_in_dim(small, me * shard_width, shard_width, axis=1)
    in_shift_grad = lax.psum(in_shift_grad, "rep")

    order = me ^ jnp.arange(N_SHARD, dtype=jnp.int32)
    in_grad = jnp.take(in_parts.reshape(N_SHARD, EXPERTS, shard_width, inner), order, axis=0)
    in_grad = in_grad.transpose(1, 2, 0, 3).reshape(EXPERTS, shard_width, N_SHARD * inner)
    qkv_grad = jnp.take(qkv_parts, order, axis=0).transpose(1, 2, 0, 3)
    return (
        final.astype(bf16),
        input_grad,
        small[0],
        small[1],
        qkv_grad.reshape(shard_width, 3 * D).astype(f32),
        out_grad,
        small[2],
        small[3],
        small[4],
        in_grad.astype(f32),
        in_shift_grad,
        back_grad.reshape(EXPERTS, inner, D).astype(f32),
        small[5:7],
    )


def solution(mesh):
    in_specs = (
        P(("rep", "shard"), None),
        P(("rep", "shard")),
        P(),
        P("rep", None),
        P(("rep", "shard")),
        P(("rep", "shard"), None),
        P(("rep", "shard"), None),
        P("shard"),
        P("shard"),
        P("shard", None),
        P("shard", None),
        P("shard"),
        P("shard"),
        P("shard"),
        P(None, "shard", None),
        P(None, "shard"),
        P(None, "shard", None),
        P(None, "shard"),
    )
    out_specs = (
        P(("rep", "shard"), None),
        P(("rep", "shard"), None),
        P("shard"),
        P("shard"),
        P("shard", None),
        P("shard", None),
        P("shard"),
        P("shard"),
        P("shard"),
        P(None, "shard", None),
        P(None, "shard"),
        P(None, "shard", None),
        P(None, "shard"),
    )
    body = functools.partial(shards, mesh.shape["rep"])
    return jax.shard_map(body, mesh=mesh, in_specs=in_specs, out_specs=out_specs, check_vma=False)
```

```python
import functools

import jax
import jax.numpy as jnp
from jax import lax
from jax.experimental import pallas as pl
from jax.experimental.pallas import tpu as pltpu
from jax.sharding import PartitionSpec as P

D = 1024
HEADS = 16
HEAD_DIM = 64
EXPERTS = 2
PIECE_LEN = 256
CAP = 320
N_SHARD = 4
OWN_HEADS = HEADS // N_SHARD
OWN = OWN_HEADS * HEAD_DIM
PAIR = 2
TILE = 256
NEG = -1e30

epsilon = 1e-05
LIGHT = pl.CostEstimate(flops=2**20, bytes_accessed=2**16, transcendentals=0)
f32 = jnp.float32
bf16 = jnp.bfloat16


def layer_norm(tok_rows):
    row_mean = jnp.mean(tok_rows, axis=-1, keepdims=True)
    centred = tok_rows - row_mean
    variance = jnp.mean(centred * centred, axis=-1, keepdims=True)
    inverse = lax.rsqrt(variance + epsilon)
    return (centred * inverse, inverse)


def norm_back(upstream, normed, inverse, norm_gain):
    scaled = upstream * norm_gain
    first_mean = jnp.mean(scaled, axis=-1, keepdims=True)
    second_mean = jnp.mean(scaled * normed, axis=-1, keepdims=True)
    return inverse * (scaled - first_mean - normed * second_mean)


def dot_nn(a, b):
    return lax.dot_general(a, b, (((1,), (0,)), ((), ())), preferred_element_type=f32)


def dot_nt(a, b):
    return lax.dot_general(a, b, (((1,), (1,)), ((), ())), preferred_element_type=f32)


def dot_tn(a, b):
    return lax.dot_general(a, b, (((0,), (0,)), ((), ())), preferred_element_type=f32)


def tie(value, after):
    return lax.optimization_barrier((value, after))[0]


def swap(value, mask):
    return lax.ppermute(value, "shard", [(i, i ^ mask) for i in range(N_SHARD)])


def exchange_blocks(blocks):
    return (blocks[0], swap(blocks[1], 1), swap(blocks[2], 2), swap(blocks[3], 3))


def in_order(side, own, other):
    return jnp.where(side == 0, jnp.stack([own, other]), jnp.stack([other, own]))


def gather_small(value, me):
    pair = in_order(me & 1, value, swap(value, 1))
    both = in_order(me >> 1, pair, swap(pair, 2))
    return both.reshape((N_SHARD,) + value.shape)


def scatter_far(block_two, block_three):
    near = swap(block_three, 1)
    return (block_two.astype(f32) + near.astype(f32)).astype(bf16)


def scatter_near(block_zero, block_one, far):
    near = swap(block_one, 1)
    return block_zero.astype(f32) + near.astype(f32) + far.astype(f32)


def rep_swap(value, mask, count):
    return lax.ppermute(value, "rep", [(i, i ^ mask) for i in range(count)])


QUARTERS = 4
ORDERS = ((1, 2), (2, 1))


def added(value, other, token):
    return (value.astype(f32) + tie(other, token).astype(f32)).astype(bf16)


def rep_sum_steps(quarters, count, middle):
    place = lax.axis_index("rep") & (QUARTERS - 1)
    sent = [jnp.stack([q(place ^ a), q(place ^ a ^ b)]) for q, (a, b) in zip(quarters, ORDERS)]
    others = [rep_swap(v, a, count) for v, (a, b) in zip(sent, ORDERS)]
    token = yield sent
    stay = [added(q(place), other[0], token) for q, other in zip(quarters, others)]
    sent = [
        added(q(place ^ b), other[1], token)
        for q, other, (a, b) in zip(quarters, others, ORDERS)
    ]
    others = [rep_swap(v, b, count) for v, (a, b) in zip(sent, ORDERS)]
    token = yield sent
    values = [added(v, other, token) for v, other in zip(stay, others)]
    mask = QUARTERS
    while mask < count:
        both = jnp.stack(values)
        other = rep_swap(both, mask, count)
        token = yield both
        values = [added(v, other[p], token) for p, v in enumerate(values)]
        mask *= 2
    values = yield from middle(values)
    others = [rep_swap(v, b, count) for v, (a, b) in zip(values, ORDERS)]
    token = yield values
    others = [tie(other, token) for other in others]
    sent = [jnp.stack([v, other]) for v, other in zip(values, others)]
    lasts = [rep_swap(v, a, count) for v, (a, b) in zip(sent, ORDERS)]
    token = yield sent
    return [(v, other, tie(last, token)) for v, other, last in zip(values, others, lasts)]


def rep_places():
    place = lax.axis_index("rep").astype(jnp.int32) & (QUARTERS - 1)
    return jnp.stack([place ^ mask for a, b in ORDERS for mask in (0, b, a, a ^ b)])


def middle_none(values):
    yield from ()
    return values


class Steps:
    def __init__(self, steps):
        self.steps = steps
        self.result = None
        self.sent = next(steps)

    def step(self, token):
        if self.result is not None:
            return token
        try:
            self.sent = self.steps.send(token)
        except StopIteration as end:
            self.result = end.value
        return self.sent

    def finish(self, token):
        while self.result is None:
            self.step(token)
        return self.result


def project_kernel(facts, tok_a, tok_b, w0, w1, w2, w3, first, qkv, weight, params, gains):
    me = facts[0]
    part, columns = weight.shape[0] // N_SHARD, weight.shape[1]
    for j, block in enumerate((w0, w1, w2, w3)):
        at = (me ^ j) * part
        weight[pl.ds(pl.multiple_of(at, part), part), :] = block[0:part, :]
        gains[:, pl.ds(pl.multiple_of(at, part), part)] = block[part : part + 8, 0:part].astype(f32)
    params[...] = gains[...]
    for half, tok in enumerate((tok_a, tok_b)):
        for start in range(0, tok.shape[0], TILE):
            normed = layer_norm(tok[start : start + TILE, :].astype(f32))[0]
            low = (normed * gains[0:1, :] + gains[1:2, :]).astype(bf16)
            rows = slice(half * tok.shape[0] + start, half * tok.shape[0] + start + TILE)
            first[rows, :] = low
            qkv[rows, :] = dot_nn(low, weight[...]).astype(bf16)


def project(facts, tok_a, tok_b, blocks):
    rows, width = tok_a.shape
    columns = blocks[0].shape[1]
    vmem = pl.BlockSpec(memory_space=pltpu.VMEM)
    return pl.pallas_call(
        project_kernel,
        out_shape=(
            jax.ShapeDtypeStruct((2 * rows, width), bf16),
            jax.ShapeDtypeStruct((2 * rows, columns), bf16),
            jax.ShapeDtypeStruct((width, columns), bf16),
            jax.ShapeDtypeStruct((8, width), f32),
        ),
        in_specs=[pl.BlockSpec(memory_space=pltpu.SMEM)] + [vmem] * 6,
        out_specs=(vmem,) * 4,
        scratch_shapes=[pltpu.VMEM((8, width), f32)],
        compiler_params=pltpu.CompilerParams(vmem_limit_bytes=32 * 2**20),
        cost_estimate=LIGHT,
        name="project",
    )(facts, tok_a, tok_b, *blocks)


def visible_tile(key_block, query_block, starts):
    key_pos = key_block * TILE + lax.broadcasted_iota(jnp.int32, (TILE, TILE), 0)
    query_pos = query_block * TILE + lax.broadcasted_iota(jnp.int32, (TILE, TILE), 1)
    seen = key_pos <= query_pos
    for start in starts:
        low = jnp.minimum(key_pos, query_pos)
        high = jnp.maximum(key_pos, query_pos)
        seen = seen | ((low >= start) & (high < start + PIECE_LEN))
    return seen


def crosses(boundary, starts):
    met = jnp.bool_(False)
    for start in starts:
        met = met | ((start < boundary) & (start + PIECE_LEN > boundary))
    return met


def head_lanes(rows):
    return lax.broadcasted_iota(jnp.int32, (rows, OWN), 1) // HEAD_DIM


def attend_kernel(blocks, facts, near, far, mixed, logs, q_own, k_own, v_turned, acc, top, total):
    me = facts[0]
    starts = [facts[1 + i] for i in range(facts.shape[0] - 1)]
    for j in range(N_SHARD):
        src = near if j < 2 else far
        base = (j % 2) * 2 * TILE
        for half in range(2):
            rows = slice(base + half * TILE, base + (half + 1) * TILE)
            at = (me ^ j) * 2 + half
            q_own[at] = src[rows, 0:OWN] * jnp.asarray(HEAD_DIM**-0.5, bf16)
            k_own[at] = src[rows, OWN : 2 * OWN]
            v_turned[at] = src[rows, 2 * OWN : 3 * OWN].astype(f32).T.astype(bf16)
    lanes = head_lanes(TILE)

    def query_block(i, unused):
        q_i = q_own[i]
        q_heads = [jnp.where(lanes == h, q_i, jnp.zeros_like(q_i)) for h in range(OWN_HEADS)]
        acc[...] = jnp.zeros_like(acc)
        top[...] = jnp.full_like(top, NEG)
        total[...] = jnp.zeros_like(total)

        def key_block(j, masked):
            k_j = k_own[j]
            v_j = v_turned[j]
            seen = visible_tile(j, i, starts) if masked else None
            for h in range(OWN_HEADS):
                scores = dot_nt(k_j, q_heads[h])
                if masked:
                    scores = jnp.where(seen, scores, NEG)
                old_top = top[h : h + 1, :]
                new_top = jnp.maximum(old_top, jnp.max(scores, axis=0, keepdims=True))
                raised = jnp.exp(scores - new_top)
                fade = jnp.exp(old_top - new_top)
                top[h : h + 1, :] = new_top
                total[h : h + 1, :] = total[h : h + 1, :] * fade + jnp.sum(
                    raised, axis=0, keepdims=True
                )
                part = dot_nn(v_j[h * HEAD_DIM : (h + 1) * HEAD_DIM, :], raised.astype(bf16))
                rows = slice(h * HEAD_DIM, (h + 1) * HEAD_DIM)
                acc[rows, :] = acc[rows, :] * fade + part

        def plain(j, unused):
            key_block(j, False)
            return unused

        lax.fori_loop(0, i, plain, 0)
        key_block(i, True)

        @pl.when((i + 1 < blocks) & crosses((i + 1) * TILE, starts))
        def _():
            key_block(i + 1, True)

        for h in range(OWN_HEADS):
            rows = slice(h * HEAD_DIM, (h + 1) * HEAD_DIM)
            acc[rows, :] = acc[rows, :] / total[h : h + 1, :]
        place = ((i // 2) ^ me) * (2 * TILE) + (i % 2) * TILE
        mixed[pl.ds(pl.multiple_of(place, TILE), TILE), :] = acc[...].T.astype(bf16)
        logs[i] = top[...] + jnp.log(jnp.maximum(total[...], 1e-30))
        return unused

    lax.fori_loop(0, blocks, query_block, 0)


def attend(facts, near, far):
    rows = near.shape[0] + far.shape[0]
    blocks = rows // TILE
    vmem = pl.BlockSpec(memory_space=pltpu.VMEM)
    return pl.pallas_call(
        functools.partial(attend_kernel, blocks),
        out_shape=(
            jax.ShapeDtypeStruct((rows, OWN), bf16),
            jax.ShapeDtypeStruct((blocks, 8, TILE), f32),
        ),
        in_specs=[pl.BlockSpec(memory_space=pltpu.SMEM), vmem, vmem],
        out_specs=(vmem, vmem),
        scratch_shapes=[
            pltpu.VMEM((blocks, TILE, OWN), bf16),
            pltpu.VMEM((blocks, TILE, OWN), bf16),
            pltpu.VMEM((blocks, OWN, TILE), bf16),
            pltpu.VMEM((OWN, TILE), f32),
            pltpu.VMEM((8, TILE), f32),
            pltpu.VMEM((8, TILE), f32),
        ],
        compiler_params=pltpu.CompilerParams(vmem_limit_bytes=48 * 2**20),
        cost_estimate=LIGHT,
        name="attend",
    )(facts, near, far)


def attend_back_kernel(
    blocks, pair, facts, near, far, mixed, g0, g1, g2, g3, logs, grads,
    q_own, k_own, v_own, k_turned, g_own, q_heads, g_heads, deltas, q_grad, k_grad, v_grad, k_heads, v_heads,
):
    me = facts[0]
    starts = [facts[1 + i] for i in range(facts.shape[0] - 1)]
    wide = PAIR * HEAD_DIM
    lane = pair * wide
    lanes = lax.broadcasted_iota(jnp.int32, (TILE, wide), 1) // HEAD_DIM
    pick = (
        lax.broadcasted_iota(jnp.int32, (8, wide), 1) // HEAD_DIM
        == lax.broadcasted_iota(jnp.int32, (8, wide), 0)
    ).astype(f32)
    for j in range(N_SHARD):
        src = near if j < 2 else far
        grad_src = (g0, g1, g2, g3)[j]
        base = (j % 2) * 2 * TILE
        for half in range(2):
            rows = slice(base + half * TILE, base + (half + 1) * TILE)
            at = (me ^ j) * 2 + half
            q_tile = src[rows, lane : lane + wide] * jnp.asarray(HEAD_DIM**-0.5, bf16)
            k_tile = src[rows, OWN + lane : OWN + lane + wide]
            g_tile = grad_src[half * TILE : (half + 1) * TILE, lane : lane + wide]
            o_rows = slice(j * 2 * TILE + half * TILE, j * 2 * TILE + (half + 1) * TILE)
            o_tile = mixed[o_rows, lane : lane + wide]
            q_own[at] = q_tile
            k_own[at] = k_tile
            v_own[at] = src[rows, 2 * OWN + lane : 2 * OWN + lane + wide]
            k_turned[at] = k_tile.astype(f32).T.astype(bf16)
            g_own[at] = g_tile
            for h in range(PAIR):
                place = slice(h * TILE, (h + 1) * TILE)
                q_heads[at, place, :] = jnp.where(lanes == h, q_tile, jnp.zeros_like(q_tile))
                g_heads[at, place, :] = jnp.where(lanes == h, g_tile, jnp.zeros_like(g_tile))
            both = g_tile.astype(f32) * o_tile.astype(f32)
            deltas[at] = lax.dot_general(
                pick, both, (((1,), (1,)), ((), ())),
                precision=lax.Precision.HIGHEST, preferred_element_type=f32,
            )
    q_grad[...] = jnp.zeros_like(q_grad)

    def key_block(j, unused):
        k_j = k_own[j]
        v_j = v_own[j]
        for h in range(PAIR):
            k_heads[h * TILE : (h + 1) * TILE, :] = jnp.where(lanes == h, k_j, jnp.zeros_like(k_j))
            v_heads[h * TILE : (h + 1) * TILE, :] = jnp.where(lanes == h, v_j, jnp.zeros_like(v_j))
        k_grad[...] = jnp.zeros_like(k_grad)
        v_grad[...] = jnp.zeros_like(v_grad)

        def query_block(i, masked):
            q_i = q_own[i]
            g_i = g_own[i]
            kt = k_turned[j]
            seen = visible_tile(j, i, starts) if masked else None
            softs = []
            scored = []
            for h in range(PAIR):
                rows = slice(h * TILE, (h + 1) * TILE)
                at = pair * PAIR + h
                scores = dot_nt(k_heads[rows, :], q_i)
                soft = jnp.exp(scores - logs[i, at : at + 1, :])
                if masked:
                    soft = jnp.where(seen, soft, 0.0)
                grad_soft = dot_nt(v_heads[rows, :], g_i)
                grad_scores = (soft * (grad_soft - deltas[i, h : h + 1, :])).astype(bf16)
                softs.append(soft.astype(bf16))
                scored.append(grad_scores)
                head = slice(h * HEAD_DIM, (h + 1) * HEAD_DIM)
                q_grad[i, head, :] += dot_nn(kt[head, :], grad_scores)
            v_grad[...] += dot_nn(jnp.concatenate(softs, axis=1), g_heads[i])
            k_grad[...] += dot_nn(jnp.concatenate(scored, axis=1), q_heads[i])

        def plain(i, unused):
            query_block(i, False)
            return unused

        @pl.when((j > 0) & crosses(j * TILE, starts))
        def _():
            query_block(j - 1, True)

        query_block(j, True)
        lax.fori_loop(j + 1, blocks, plain, 0)
        place = pl.multiple_of(((j // 2) ^ me) * (2 * TILE) + (j % 2) * TILE, TILE)
        grads[pl.ds(place, TILE), wide : 2 * wide] = k_grad[...].astype(bf16)
        grads[pl.ds(place, TILE), 2 * wide : 3 * wide] = v_grad[...].astype(bf16)
        return unused

    lax.fori_loop(0, blocks, key_block, 0)

    def write_query(i, unused):
        place = pl.multiple_of(((i // 2) ^ me) * (2 * TILE) + (i % 2) * TILE, TILE)
        grads[pl.ds(place, TILE), 0:wide] = (q_grad[i] * HEAD_DIM**-0.5).T.astype(bf16)
        return unused

    lax.fori_loop(0, blocks, write_query, 0)


def attend_back(pair, facts, near, far, mixed, grad_blocks, logs):
    rows = near.shape[0] + far.shape[0]
    blocks = rows // TILE
    wide = PAIR * HEAD_DIM
    vmem = pl.BlockSpec(memory_space=pltpu.VMEM)
    tile = lambda n, m, kind: pltpu.VMEM((n, m), kind)
    stack = lambda n, m, kind: pltpu.VMEM((blocks, n, m), kind)
    return pl.pallas_call(
        functools.partial(attend_back_kernel, blocks, pair),
        out_shape=jax.ShapeDtypeStruct((rows, 3 * wide), bf16),
        in_specs=[pl.BlockSpec(memory_space=pltpu.SMEM)] + [vmem] * 8,
        out_specs=vmem,
        scratch_shapes=[
            stack(TILE, wide, bf16),
            stack(TILE, wide, bf16),
            stack(TILE, wide, bf16),
            stack(wide, TILE, bf16),
            stack(TILE, wide, bf16),
            stack(PAIR * TILE, wide, bf16),
            stack(PAIR * TILE, wide, bf16),
            stack(8, TILE, f32),
            stack(wide, TILE, f32),
            tile(TILE, wide, f32),
            tile(TILE, wide, f32),
            tile(PAIR * TILE, wide, bf16),
            tile(PAIR * TILE, wide, bf16),
        ],
        compiler_params=pltpu.CompilerParams(vmem_limit_bytes=48 * 2**20),
        cost_estimate=LIGHT,
        name="attend_back",
    )(facts, near, far, mixed, *grad_blocks, logs)


def expert_tile(counts, step, tiles):
    block = step // tiles
    start = (step % tiles) * TILE
    border = counts[block, 0] - start
    late = lax.broadcasted_iota(jnp.int32, (TILE, 1), 0) >= border
    return border, late


def expert_kernel(tiles, counts, rows_a, rows_b, w_in, in_bias, w_back, hidden, out_a, out_b, held):
    step = pl.program_id(0)
    border, late = expert_tile(counts, step, tiles)

    def work(rows, out):
        @pl.when(border > 0)
        def _():
            held[...] = jnp.maximum(dot_nn(rows[...], w_in[0]) + in_bias[0:1, :], 0.0).astype(bf16)

        @pl.when(border < TILE)
        def _():
            one = jnp.maximum(dot_nn(rows[...], w_in[1]) + in_bias[1:2, :], 0.0).astype(bf16)
            held[...] = jnp.where(late, one, held[...])

        hidden[...] = held[...]

        @pl.when(border > 0)
        def _():
            out[...] = dot_nn(held[...], w_back[0]).astype(bf16)

        @pl.when(border < TILE)
        def _():
            out[...] = jnp.where(late, dot_nn(held[...], w_back[1]).astype(bf16), out[...])

    @pl.when(step < tiles)
    def _():
        work(rows_a, out_a)

    @pl.when(step >= tiles)
    def _():
        work(rows_b, out_b)


def expert_back_kernel(tiles, counts, rows_a, rows_b, hidden, w_in, w_back, grad_pre, out_a, out_b, held):
    step = pl.program_id(0)
    border, late = expert_tile(counts, step, tiles)

    def work(rows, out):
        alive = hidden[...] > 0

        @pl.when(border > 0)
        def _():
            held[...] = jnp.where(alive, dot_nt(rows[...], w_back[0]), 0.0).astype(bf16)

        @pl.when(border < TILE)
        def _():
            one = jnp.where(alive, dot_nt(rows[...], w_back[1]), 0.0).astype(bf16)
            held[...] = jnp.where(late, one, held[...])

        grad_pre[...] = held[...]

        @pl.when(border > 0)
        def _():
            out[...] = dot_nt(held[...], w_in[0]).astype(bf16)

        @pl.when(border < TILE)
        def _():
            out[...] = jnp.where(late, dot_nt(held[...], w_in[1]).astype(bf16), out[...])

    @pl.when(step < tiles)
    def _():
        work(rows_a, out_a)

    @pl.when(step >= tiles)
    def _():
        work(rows_b, out_b)


def expert_specs(rows, width, inner):
    tiles = rows // TILE
    first = pl.BlockSpec((TILE, width), lambda i, c: (jnp.minimum(i, tiles - 1), 0))
    second = pl.BlockSpec((TILE, width), lambda i, c: (jnp.maximum(i - tiles, 0), 0))
    both = pl.BlockSpec((TILE, inner), lambda i, c: (i, 0))
    once = pl.Buffered(1)
    w_in = pl.BlockSpec((EXPERTS, width, inner), lambda i, c: (0, 0, 0), pipeline_mode=once)
    w_back = pl.BlockSpec((EXPERTS, inner, width), lambda i, c: (0, 0, 0), pipeline_mode=once)
    bias = pl.BlockSpec((EXPERTS, inner), lambda i, c: (0, 0), pipeline_mode=once)
    return tiles, first, second, both, w_in, w_back, bias


def run_experts(counts, rows_a, rows_b, w_in, in_bias, w_back):
    rows, width = rows_a.shape
    inner = w_in.shape[2]
    tiles, first, second, both, in_spec, back_spec, bias_spec = expert_specs(rows, width, inner)
    return pl.pallas_call(
        functools.partial(expert_kernel, tiles),
        grid_spec=pltpu.PrefetchScalarGridSpec(
            num_scalar_prefetch=1,
            grid=(2 * tiles,),
            in_specs=[first, second, in_spec, bias_spec, back_spec],
            out_specs=[both, first, second],
            scratch_shapes=[pltpu.VMEM((TILE, inner), bf16)],
        ),
        out_shape=(
            jax.ShapeDtypeStruct((2 * rows, inner), bf16),
            jax.ShapeDtypeStruct((rows, width), bf16),
            jax.ShapeDtypeStruct((rows, width), bf16),
        ),
        compiler_params=pltpu.CompilerParams(vmem_limit_bytes=40 * 2**20),
        cost_estimate=LIGHT,
        name="experts",
    )(counts, rows_a, rows_b, w_in, in_bias, w_back)


def run_experts_back(counts, rows_a, rows_b, hidden, w_in, w_back):
    rows, width = rows_a.shape
    inner = w_in.shape[2]
    tiles, first, second, both, in_spec, back_spec, bias_spec = expert_specs(rows, width, inner)
    return pl.pallas_call(
        functools.partial(expert_back_kernel, tiles),
        grid_spec=pltpu.PrefetchScalarGridSpec(
            num_scalar_prefetch=1,
            grid=(2 * tiles,),
            in_specs=[first, second, both, in_spec, back_spec],
            out_specs=[both, first, second],
            scratch_shapes=[pltpu.VMEM((TILE, inner), bf16)],
        ),
        out_shape=(
            jax.ShapeDtypeStruct((2 * rows, inner), bf16),
            jax.ShapeDtypeStruct((rows, width), bf16),
            jax.ShapeDtypeStruct((rows, width), bf16),
        ),
        compiler_params=pltpu.CompilerParams(vmem_limit_bytes=40 * 2**20),
        cost_estimate=LIGHT,
        name="experts_back",
    )(counts, rows_a, rows_b, hidden, w_in, w_back)


def place_experts_kernel(facts, *refs):
    blocks, out = refs[:6], refs[6]
    expert, turn = pl.program_id(0), pl.program_id(1)

    def write(block):
        owners, rows, width = block.shape[-3:]
        for j in range(owners):
            at = pl.multiple_of((facts[0] ^ j) * width, width) if owners > 1 else 0
            out[0, :, pl.ds(at, width)] = (block[0, j] if len(block.shape) == 4 else block[j]).astype(f32)

    for part in range(2):
        for source, block in enumerate(blocks[3 * part : 3 * part + 3]):

            @pl.when((expert == part) & (jnp.minimum(turn, 2) == source))
            def _():
                write(block)


def place_experts(me, parts):
    owners, rows, width = parts[0][0].shape
    whole = pl.BlockSpec((owners, rows, width), lambda e, t, s: (0, 0, 0))

    def last(part):
        return pl.BlockSpec(
            (1, owners, rows, width),
            lambda e, t, s: (jnp.clip((e - part) * QUARTERS + t - 2, 0, 1), 0, 0, 0),
        )

    return pl.pallas_call(
        place_experts_kernel,
        grid_spec=pltpu.PrefetchScalarGridSpec(
            num_scalar_prefetch=1,
            grid=(2, QUARTERS),
            in_specs=[whole, whole, last(0), whole, whole, last(1)],
            out_specs=pl.BlockSpec(
                (1, rows, owners * width), lambda e, t, s: (e, s[1 + e * QUARTERS + t], 0)
            ),
        ),
        out_shape=jax.ShapeDtypeStruct((2, QUARTERS * rows, owners * width), f32),
        compiler_params=pltpu.CompilerParams(vmem_limit_bytes=24 * 2**20),
        cost_estimate=LIGHT,
        name="place_experts",
    )(jnp.concatenate([me[None], rep_places()]), *[b for p in parts for b in p])


def place_attention_kernel(facts, *refs):
    blocks, qkv_out, whole_out = refs[:6], refs[6], refs[7]
    rows = qkv_out.shape[0] // (2 * QUARTERS)
    for part in range(2):
        own, second, last = blocks[3 * part : 3 * part + 3]
        for turn in range(QUARTERS):
            block = (own, second, last.at[0], last.at[1])[turn]
            segment = part * QUARTERS + facts[1 + part * QUARTERS + turn]
            to = pl.ds(pl.multiple_of(segment * rows, rows), rows)
            for c in range(3):
                for j in range(N_SHARD):
                    at = pl.multiple_of(c * N_SHARD * OWN + (facts[0] ^ j) * OWN, OWN)
                    start = (c * N_SHARD + j) * rows
                    qkv_out[to, pl.ds(at, OWN)] = block[start : start + rows, :].astype(f32)
            for x in range(N_SHARD):
                start = (3 * N_SHARD + x) * rows
                whole_out[to, x * OWN : (x + 1) * OWN] = block[start : start + rows, :].astype(f32)


def place_attention(me, parts, rows):
    vmem = pl.BlockSpec(memory_space=pltpu.VMEM)
    return pl.pallas_call(
        place_attention_kernel,
        out_shape=(
            jax.ShapeDtypeStruct((rows, 3 * N_SHARD * OWN), f32),
            jax.ShapeDtypeStruct((rows, N_SHARD * OWN), f32),
        ),
        in_specs=[pl.BlockSpec(memory_space=pltpu.SMEM)] + [vmem] * 6,
        out_specs=(vmem, vmem),
        compiler_params=pltpu.CompilerParams(vmem_limit_bytes=24 * 2**20),
        cost_estimate=LIGHT,
        name="place_attention",
    )(jnp.concatenate([me[None], rep_places()]), *[b for p in parts for b in p])


def shards(
    n_rep,
    tokens,
    token_ids,
    hash_table,
    piece_starts,
    valid_mask,
    teacher,
    cotangent,
    ln1_gain,
    ln1_bias,
    w_qkv,
    w_out,
    out_bias,
    ln2_gain,
    ln2_bias,
    w_in,
    in_bias,
    w_back,
    back_bias,
):
    local_rows = tokens.shape[0]
    tokens_all = local_rows * N_SHARD * n_rep
    me = lax.axis_index("shard").astype(jnp.int32)
    rep_at = lax.axis_index("rep")
    inner = w_back.shape[1]
    shard_width = ln1_gain.shape[0]
    seg_rows = shard_width // n_rep
    facts = jnp.concatenate([me[None], piece_starts[0]])

    packed = jnp.concatenate(
        [
            jnp.stack([ln1_gain, ln1_bias, out_bias, ln2_gain, ln2_bias]),
            back_bias,
            jnp.zeros((1, shard_width), bf16),
        ],
        axis=0,
    )
    packed = jnp.concatenate([packed, jnp.zeros((8, 3 * OWN - shard_width), bf16)], axis=1)
    qkv_sends = [
            jnp.concatenate(
                [
                    jnp.concatenate(
                        [
                            lax.dynamic_slice_in_dim(w_qkv, c * D + (me ^ j) * OWN, OWN, axis=1)
                            for c in range(3)
                        ],
                        axis=1,
                    ),
                    packed,
                ],
                axis=0,
            )
            for j in range(N_SHARD)
    ]
    over = swap(jnp.stack(qkv_sends[2:]), 3)
    tok_far = swap(tokens, 2)
    near = swap(qkv_sends[1], 1)
    tok_near = swap(tokens, 1)
    qkv_blocks = (qkv_sends[0], near, swap(over[0], 1), over[1])

    expert_of = jnp.take(hash_table, token_ids)
    places = jnp.arange(local_rows, dtype=jnp.int32)
    earlier = (expert_of[:, None] == expert_of[None, :]) & (places[None, :] < places[:, None])
    slot_of = jnp.sum(earlier.astype(jnp.int32), axis=1)
    kept = slot_of < CAP
    is_late = expert_of > 0
    early_count = jnp.minimum(local_rows - jnp.sum(is_late.astype(jnp.int32)), CAP)
    sorted_at = jnp.where(kept, slot_of + jnp.where(is_late, early_count, 0), -1)
    sorter = (sorted_at[None, :] == places[:, None]).astype(bf16)
    counted = valid_mask.astype(f32)
    own_facts = jnp.stack([early_count.astype(f32), jnp.sum(counted)])
    own_facts = jnp.broadcast_to(own_facts[:, None], (2, 128))
    shared = gather_small(own_facts, me)
    count_all = jnp.sum(shared[:, 1], axis=0, keepdims=True)
    for bit in range(n_rep.bit_length() - 1):
        count_all = count_all + rep_swap(count_all, 1 << bit, n_rep)
    count_all = count_all[0, 0]
    indices = jnp.arange(N_SHARD, dtype=jnp.int32)
    borders = jnp.sum(
        jnp.where((indices ^ me)[:, None] == indices[None, :], shared[:, 0, 0][None, :], 0.0), axis=1
    ).astype(jnp.int32)
    counts_near, counts_far = borders[:2, None], borders[2:, None]

    first_near, qkv_near, qkv_weight, rows_of = project(facts, tokens, tok_near, qkv_blocks)
    gain_one, bias_one, out_shift, gain_two, bias_two = [rows_of[i] for i in range(5)]
    back_shift = rows_of[5:7]
    tok_both = swap(tok_far, 1)
    first_far, qkv_far = project(facts, tie(tok_far, qkv_near), tok_both, qkv_blocks)[:2]

    def first_rows(block):
        normed, inverse = layer_norm(block.astype(f32))
        return (normed * gain_one + bias_one).astype(bf16), normed, inverse

    thin = lax.dynamic_slice_in_dim(w_in, rep_at * seg_rows, seg_rows, axis=1)
    thin = tie(thin, (tok_far, over))
    thin_blocks = exchange_blocks(
        [lax.dynamic_slice_in_dim(thin, (me ^ j) * inner, inner, axis=2) for j in range(N_SHARD)]
    )
    thin = in_order(
        me >> 1,
        in_order(me & 1, thin_blocks[0], thin_blocks[1]),
        in_order(me & 1, thin_blocks[2], thin_blocks[3]),
    ).reshape(N_SHARD, EXPERTS, seg_rows, inner)
    thin = lax.all_gather(thin.transpose(1, 0, 2, 3), "rep", axis=0)
    in_weight = thin.transpose(1, 2, 0, 3, 4).reshape(EXPERTS, D, inner)
    w_out = tie(w_out, tok_far)
    out_far = swap(w_out, 2)
    out_blocks = (w_out, swap(w_out, 1), out_far, swap(out_far, 1))

    facts = tie(facts, (count_all, borders))
    mixed, logs = attend(facts, qkv_near, qkv_far)
    mixed_blocks = exchange_blocks(
        [mixed[j * local_rows : (j + 1) * local_rows] for j in range(N_SHARD)]
    )
    mixed_blocks = mixed_blocks[:2] + lax.optimization_barrier(mixed_blocks[2:] + (in_weight,))[:2]
    tok_rows = tokens.astype(f32)
    branch = dot_nn(mixed_blocks[0], out_blocks[0])
    for j in range(1, N_SHARD):
        branch = branch + dot_nn(mixed_blocks[j], out_blocks[j])
    middle = tok_rows + branch + out_shift
    normed_two, inverse_two = layer_norm(middle)
    second_in = (normed_two * gain_two + bias_two).astype(bf16)
    sorted_in = dot_nn(sorter, second_in).astype(bf16)
    in_far = swap(sorted_in, 2)
    in_near = swap(sorted_in, 1)
    bias_in = in_bias.astype(f32)
    hidden_near, out0, out1 = run_experts(counts_near, sorted_in, in_near, in_weight, bias_in, w_back)
    in_far = tie(in_far, out0)
    in_both = swap(in_far, 1)
    hidden_far, out2, out3 = run_experts(counts_far, in_far, in_both, in_weight, bias_in, w_back)
    summed = scatter_near(out0, out1, swap(scatter_far(out2, out3), 2))
    picked = dot_tn(sorter, summed.astype(bf16))
    picked = picked + jnp.where(is_late[:, None], back_shift[1], back_shift[0])
    final = middle + jnp.where(kept[:, None], picked, 0.0)
    grad_final = cotangent.astype(f32) + tokens_all / (2.0 * count_all) * counted[:, None] * (
        final - teacher.astype(f32)
    )
    grad_low = grad_final.astype(bf16)

    sorted_grad = dot_nn(sorter, grad_low).astype(bf16)
    grad_far = swap(sorted_grad, 2)
    grad_near = swap(sorted_grad, 1)
    pre_near, gin0, gin1 = run_experts_back(
        counts_near, sorted_grad, grad_near, hidden_near, in_weight, w_back
    )
    grad_far = tie(grad_far, gin0)
    grad_both = swap(grad_far, 1)
    pre_far, gin2, gin3 = run_experts_back(
        counts_far, grad_far, grad_both, hidden_far, in_weight, w_back
    )
    send_second = scatter_far(gin2, gin3)
    far_second = swap(send_second, 2)

    early = (jnp.arange(local_rows, dtype=jnp.int32)[None, :] < tie(borders, send_second)[:, None]).reshape(-1)
    masks = [early[:, None], ~early[:, None]]
    hidden_all = jnp.concatenate([hidden_near, hidden_far], axis=0)
    grad_all = jnp.concatenate([sorted_grad, grad_near, grad_far, grad_both], axis=0)
    back_grads = [dot_tn(jnp.where(m, hidden_all, 0), grad_all).astype(bf16) for m in masks]
    back_rows = EXPERTS * inner
    part = lambda a, i: lax.dynamic_index_in_dim(a, i, 1, keepdims=False)
    quarter_of = lambda a: lambda i: part(a, i)
    back_parts = [g.reshape(1, QUARTERS, inner // QUARTERS, D) for g in back_grads]
    back_sum = Steps(rep_sum_steps([quarter_of(g) for g in back_parts], n_rep, middle_none))
    pre_all = tie(jnp.concatenate([pre_near, pre_far], axis=0), back_sum.sent)
    in_all = jnp.concatenate([sorted_in, in_near, in_far, in_both], axis=0)
    in_grads = [dot_tn(in_all, jnp.where(m, pre_all, 0)).astype(bf16) for m in masks]
    quarter_rows = shard_width // QUARTERS
    in_parts = [g.reshape(N_SHARD, QUARTERS, quarter_rows, inner) for g in in_grads]

    def middle_in(values):
        blocks = [
            jnp.concatenate(
                [lax.dynamic_index_in_dim(v, me ^ j, 0, keepdims=False) for v in values], axis=0
            )
            for j in range(N_SHARD)
        ]
        moved = exchange_blocks(blocks)
        token = yield blocks
        moved = jnp.stack([tie(m, token) for m in moved])
        rows = values[0].shape[1]
        return [moved[:, p * rows : (p + 1) * rows] for p in range(len(values))]

    experts_sum = Steps(rep_sum_steps([quarter_of(g) for g in in_parts], n_rep, middle_in))

    far_second = tie(far_second, back_sum.step(experts_sum.sent))
    summed_grad = scatter_near(gin0, gin1, far_second)
    grad_second = dot_tn(sorter, summed_grad.astype(bf16))
    grad_gain_two = jnp.sum(grad_second * normed_two, axis=0)
    grad_bias_two = jnp.sum(grad_second, axis=0)
    grad_middle = grad_final + norm_back(grad_second, normed_two, inverse_two, gain_two)
    grad_branch = grad_middle.astype(bf16)
    grad_out_shift = jnp.sum(grad_branch.astype(f32), axis=0)
    grad_mixed_own = [dot_nt(grad_branch, w).astype(bf16) for w in out_blocks]
    grad_mixed = exchange_blocks(grad_mixed_own)
    out_parts = [dot_tn(b, tie(grad_branch, grad_mixed_own)).astype(bf16) for b in mixed_blocks]
    grad_mixed = lax.optimization_barrier((grad_mixed, out_parts))[0]
    sent = experts_sum.step((back_sum.step(grad_mixed_own), grad_mixed))

    half_grads = []
    near_tied = tie(qkv_near, sent)
    for pair in range(OWN_HEADS // PAIR):
        half_grads.append(attend_back(pair, facts, near_tied, qkv_far, mixed, grad_mixed, logs))
        if pair == 0:
            out_send = tie(scatter_far(out_parts[2], out_parts[3]), half_grads[0])
            out_far_sum = swap(out_send, 2)
            sent = (out_send, back_sum.step(experts_sum.step(half_grads[-1])))
        else:
            sent = experts_sum.step(back_sum.step(half_grads[-1]))
        near_tied = tie(qkv_near, sent)

    weight_halves = [
        jnp.concatenate(
            [
                qkv_weight[:, c * OWN + p * PAIR * HEAD_DIM : c * OWN + (p + 1) * PAIR * HEAD_DIM]
                for c in range(3)
            ],
            axis=1,
        )
        for p in range(OWN_HEADS // PAIR)
    ]

    def first_grad(j, token):
        rows = slice(j * local_rows, (j + 1) * local_rows)
        total = dot_nt(half_grads[0][rows], tie(weight_halves[0], token))
        for g, w in zip(half_grads[1:], weight_halves[1:]):
            total = total + dot_nt(g[rows], w)
        return total.astype(bf16)

    first2, first3 = first_grad(2, sent), first_grad(3, sent)
    send_first = scatter_far(first2, first3)
    far_first = swap(send_first, 2)

    sent = send_first
    first_all = tie(jnp.concatenate([first_near, first_far], axis=0), sent)
    half_weights = [dot_tn(first_all, g).astype(bf16) for g in half_grads]
    out_far_sum = tie(out_far_sum, half_grads[-1])
    out_grad = scatter_near(out_parts[0], out_parts[1], out_far_sum).astype(bf16)
    wide = PAIR * HEAD_DIM
    part_rows = quarter_rows // 2
    by_owner = [h.reshape(N_SHARD, 2, QUARTERS, part_rows, 3 * wide) for h in half_weights]
    out_quarters = out_grad.reshape(2, QUARTERS, part_rows, D)

    def last_quarter(p):
        def quarter(i):
            pieces = [part(h[:, p], i) for h in by_owner]
            rows = [
                jnp.concatenate([g[:, :, c * wide : (c + 1) * wide] for g in pieces], axis=2)
                for c in range(3)
            ]
            whole = lax.dynamic_index_in_dim(out_quarters[p], i, 0, keepdims=False)
            rows += [whole[:, x * OWN : (x + 1) * OWN] for x in range(N_SHARD)]
            return jnp.concatenate([r.reshape(-1, OWN) for r in rows], axis=0)

        return quarter

    def middle_last(values):
        rest = 3 * N_SHARD * part_rows
        moving = [
            v[:rest].reshape(3, N_SHARD, part_rows, OWN).transpose(1, 0, 2, 3).reshape(N_SHARD, -1, OWN)
            for v in values
        ]
        moved = yield from middle_in(moving)
        return [
            jnp.concatenate(
                [m.reshape(N_SHARD, 3, part_rows, OWN).transpose(1, 0, 2, 3).reshape(rest, OWN), v[rest:]],
                axis=0,
            )
            for m, v in zip(moved, values)
        ]

    last_sum = Steps(rep_sum_steps([last_quarter(0), last_quarter(1)], n_rep, middle_last))
    sent = last_sum.sent
    first0, first1 = first_grad(0, sent), first_grad(1, sent)
    sent = experts_sum.step((first0, first1))
    grad_first = scatter_near(first0, first1, tie(far_first, sent))
    first_in, normed_one, inverse_one = first_rows(tie(tokens, sent))
    grad_gain_one = jnp.sum(grad_first * normed_one, axis=0)
    grad_bias_one = jnp.sum(grad_first, axis=0)
    input_grad = grad_middle + norm_back(grad_first, normed_one, inverse_one, gain_one)

    by_expert = jnp.stack([(kept & ~is_late), (kept & is_late)]).astype(bf16)
    grad_back_shift = dot_nn(by_expert, grad_low)
    in_shift_grad = jnp.concatenate(
        [dot_nn(m.astype(bf16).reshape(1, -1), pre_all) for m in masks], axis=0
    )
    small = jnp.concatenate(
        [
            jnp.stack([grad_gain_one, grad_bias_one, grad_out_shift, grad_gain_two, grad_bias_two]),
            grad_back_shift,
            jnp.zeros((1, D), f32),
        ],
        axis=0,
    )
    small = small + swap(small, 1)
    small = small + swap(small, 2)
    small = lax.dynamic_slice_in_dim(small, me * shard_width, shard_width, axis=1)
    small = jnp.concatenate([small, in_shift_grad.reshape(-1, shard_width)], axis=0)
    sent = last_sum.step(experts_sum.step((input_grad, small)))
    sent = last_sum.step(sent)
    back_grad = place_experts(me, back_sum.finish(sent))
    sent = last_sum.step(back_grad)
    small = small + tie(rep_swap(small, 1, n_rep), sent)
    in_grad = place_experts(me, experts_sum.finish(small))
    sent = last_sum.step(in_grad)
    bit = 2
    while bit < n_rep:
        small = small + tie(rep_swap(small, bit, n_rep), sent)
        sent = last_sum.step(small)
        bit *= 2
    in_shift_grad = small[8:].reshape(EXPERTS, inner)
    qkv_grad, out_grad = place_attention(me, last_sum.finish(small), shard_width)
    return (
        final.astype(bf16),
        input_grad,
        small[0],
        small[1],
        qkv_grad,
        out_grad,
        small[2],
        small[3],
        small[4],
        in_grad,
        in_shift_grad,
        back_grad,
        small[5:7],
    )


def solution(mesh):
    in_specs = (
        P(("rep", "shard"), None),
        P(("rep", "shard")),
        P(),
        P("rep", None),
        P(("rep", "shard")),
        P(("rep", "shard"), None),
        P(("rep", "shard"), None),
        P("shard"),
        P("shard"),
        P("shard", None),
        P("shard", None),
        P("shard"),
        P("shard"),
        P("shard"),
        P(None, "shard", None),
        P(None, "shard"),
        P(None, "shard", None),
        P(None, "shard"),
    )
    out_specs = (
        P(("rep", "shard"), None),
        P(("rep", "shard"), None),
        P("shard"),
        P("shard"),
        P("shard", None),
        P("shard", None),
        P("shard"),
        P("shard"),
        P("shard"),
        P(None, "shard", None),
        P(None, "shard"),
        P(None, "shard", None),
        P(None, "shard"),
    )
    body = functools.partial(shards, mesh.shape["rep"])
    return jax.shard_map(body, mesh=mesh, in_specs=in_specs, out_specs=out_specs, check_vma=False)
```

```python
import functools

import jax
import jax.numpy as jnp
from jax import lax
from jax.experimental import pallas as pl
from jax.experimental.pallas import tpu as pltpu
from jax.sharding import PartitionSpec as P

D = 1024
HEADS = 16
HEAD_DIM = 64
EXPERTS = 2
PIECE_LEN = 256
CAP = 320
N_SHARD = 4
OWN_HEADS = HEADS // N_SHARD
OWN = OWN_HEADS * HEAD_DIM
PAIR = 2
CHUNKS = 1
TILE = 256
NEG = -1e30

epsilon = 1e-05
LIGHT = pl.CostEstimate(flops=2**20, bytes_accessed=2**16, transcendentals=0)
f32 = jnp.float32
bf16 = jnp.bfloat16


def layer_norm(tok_rows):
    row_mean = jnp.mean(tok_rows, axis=-1, keepdims=True)
    centred = tok_rows - row_mean
    variance = jnp.mean(centred * centred, axis=-1, keepdims=True)
    inverse = lax.rsqrt(variance + epsilon)
    return (centred * inverse, inverse)


def norm_back(upstream, normed, inverse, norm_gain):
    scaled = upstream * norm_gain
    first_mean = jnp.mean(scaled, axis=-1, keepdims=True)
    second_mean = jnp.mean(scaled * normed, axis=-1, keepdims=True)
    return inverse * (scaled - first_mean - normed * second_mean)


def dot_nn(a, b):
    return lax.dot_general(a, b, (((1,), (0,)), ((), ())), preferred_element_type=f32)


def dot_nt(a, b):
    return lax.dot_general(a, b, (((1,), (1,)), ((), ())), preferred_element_type=f32)


def dot_tn(a, b):
    return lax.dot_general(a, b, (((0,), (0,)), ((), ())), preferred_element_type=f32)


def tie(value, after):
    return lax.optimization_barrier((value, after))[0]


def swap(value, mask):
    return lax.ppermute(value, "shard", [(i, i ^ mask) for i in range(N_SHARD)])


def exchange_blocks(blocks):
    return (blocks[0], swap(blocks[1], 1), swap(blocks[2], 2), swap(blocks[3], 3))


def in_order(side, own, other):
    return jnp.where(side == 0, jnp.stack([own, other]), jnp.stack([other, own]))


def scatter_far(block_two, block_three):
    near = swap(block_three, 1)
    return (block_two.astype(f32) + near.astype(f32)).astype(bf16)


def scatter_near(block_zero, block_one, far):
    near = swap(block_one, 1)
    return block_zero.astype(f32) + near.astype(f32) + far.astype(f32)


def rep_swap(value, mask, count):
    return lax.ppermute(value, "rep", [(i, i ^ mask) for i in range(count)])


QUARTERS = 4
ORDERS = ((1, 2), (2, 1))


def added(value, other, token):
    return (value.astype(f32) + tie(other, token).astype(f32)).astype(bf16)


def rep_sum_steps(quarters, count, middle):
    place = lax.axis_index("rep") & (QUARTERS - 1)
    sent = [jnp.stack([q(place ^ a), q(place ^ a ^ b)]) for q, (a, b) in zip(quarters, ORDERS)]
    others = [rep_swap(v, a, count) for v, (a, b) in zip(sent, ORDERS)]
    token = yield sent
    stay = [added(q(place), other[0], token) for q, other in zip(quarters, others)]
    sent = [
        added(q(place ^ b), other[1], token)
        for q, other, (a, b) in zip(quarters, others, ORDERS)
    ]
    others = [rep_swap(v, b, count) for v, (a, b) in zip(sent, ORDERS)]
    token = yield sent
    values = [added(v, other, token) for v, other in zip(stay, others)]
    mask = QUARTERS
    while mask < count:
        both = jnp.stack(values)
        other = rep_swap(both, mask, count)
        token = yield both
        values = [added(v, other[p], token) for p, v in enumerate(values)]
        mask *= 2
    values = yield from middle(values)
    others = [rep_swap(v, b, count) for v, (a, b) in zip(values, ORDERS)]
    token = yield values
    others = [tie(other, token) for other in others]
    sent = [jnp.stack([v, other]) for v, other in zip(values, others)]
    lasts = [rep_swap(v, a, count) for v, (a, b) in zip(sent, ORDERS)]
    token = yield sent
    return [(v, other, tie(last, token)) for v, other, last in zip(values, others, lasts)]


def rep_places():
    place = lax.axis_index("rep").astype(jnp.int32) & (QUARTERS - 1)
    return jnp.stack([place ^ mask for a, b in ORDERS for mask in (0, b, a, a ^ b)])


def middle_none(values):
    yield from ()
    return values


class Steps:
    def __init__(self, steps):
        self.steps = steps
        self.result = None
        self.sent = next(steps)

    def step(self, token):
        if self.result is not None:
            return token
        try:
            self.sent = self.steps.send(token)
        except StopIteration as end:
            self.result = end.value
            return token
        return self.sent

    def finish(self, token):
        while self.result is None:
            self.step(token)
        return self.result


def project_kernel(facts, tok_a, tok_b, w0, w1, w2, w3, first, qkv, weight, params, gains):
    me = facts[0]
    part, columns = weight.shape[0] // N_SHARD, weight.shape[1]
    for j, block in enumerate((w0, w1, w2, w3)):
        at = (me ^ j) * part
        weight[pl.ds(pl.multiple_of(at, part), part), :] = block[0:part, :]
        gains[:, pl.ds(pl.multiple_of(at, part), part)] = block[part : part + 8, 0:part].astype(f32)
    params[...] = gains[...]
    for half, tok in enumerate((tok_a, tok_b)):
        for start in range(0, tok.shape[0], TILE):
            normed = layer_norm(tok[start : start + TILE, :].astype(f32))[0]
            low = (normed * gains[0:1, :] + gains[1:2, :]).astype(bf16)
            rows = slice(half * tok.shape[0] + start, half * tok.shape[0] + start + TILE)
            first[rows, :] = low
            qkv[rows, :] = dot_nn(low, weight[...]).astype(bf16)


def project(facts, tok_a, tok_b, blocks):
    rows, width = tok_a.shape
    columns = blocks[0].shape[1]
    vmem = pl.BlockSpec(memory_space=pltpu.VMEM)
    return pl.pallas_call(
        project_kernel,
        out_shape=(
            jax.ShapeDtypeStruct((2 * rows, width), bf16),
            jax.ShapeDtypeStruct((2 * rows, columns), bf16),
            jax.ShapeDtypeStruct((width, columns), bf16),
            jax.ShapeDtypeStruct((8, width), f32),
        ),
        in_specs=[pl.BlockSpec(memory_space=pltpu.SMEM)] + [vmem] * 6,
        out_specs=(vmem,) * 4,
        scratch_shapes=[pltpu.VMEM((8, width), f32)],
        compiler_params=pltpu.CompilerParams(vmem_limit_bytes=32 * 2**20),
        cost_estimate=LIGHT,
        name="project",
    )(facts, tok_a, tok_b, *blocks)


def visible_tile(key_block, query_block, starts):
    key_pos = key_block * TILE + lax.broadcasted_iota(jnp.int32, (TILE, TILE), 0)
    query_pos = query_block * TILE + lax.broadcasted_iota(jnp.int32, (TILE, TILE), 1)
    seen = key_pos <= query_pos
    for start in starts:
        low = jnp.minimum(key_pos, query_pos)
        high = jnp.maximum(key_pos, query_pos)
        seen = seen | ((low >= start) & (high < start + PIECE_LEN))
    return seen


def crosses(boundary, starts):
    met = jnp.bool_(False)
    for start in starts:
        met = met | ((start < boundary) & (start + PIECE_LEN > boundary))
    return met


def head_lanes(rows):
    return lax.broadcasted_iota(jnp.int32, (rows, OWN), 1) // HEAD_DIM


def attend_kernel(blocks, facts, near, far, mixed, logs, q_own, k_own, v_turned, acc, top, total):
    me = facts[0]
    starts = [facts[1 + i] for i in range(facts.shape[0] - 1)]
    for j in range(N_SHARD):
        src = near if j < 2 else far
        base = (j % 2) * 2 * TILE
        for half in range(2):
            rows = slice(base + half * TILE, base + (half + 1) * TILE)
            at = (me ^ j) * 2 + half
            q_own[at] = src[rows, 0:OWN] * jnp.asarray(HEAD_DIM**-0.5, bf16)
            k_own[at] = src[rows, OWN : 2 * OWN]
            v_turned[at] = src[rows, 2 * OWN : 3 * OWN].astype(f32).T.astype(bf16)
    lanes = head_lanes(TILE)

    def query_block(i, unused):
        q_i = q_own[i]
        q_heads = [jnp.where(lanes == h, q_i, jnp.zeros_like(q_i)) for h in range(OWN_HEADS)]
        acc[...] = jnp.zeros_like(acc)
        top[...] = jnp.full_like(top, NEG)
        total[...] = jnp.zeros_like(total)

        def key_block(j, masked):
            k_j = k_own[j]
            v_j = v_turned[j]
            seen = visible_tile(j, i, starts) if masked else None
            for h in range(OWN_HEADS):
                scores = dot_nt(k_j, q_heads[h])
                if masked:
                    scores = jnp.where(seen, scores, NEG)
                old_top = top[h : h + 1, :]
                new_top = jnp.maximum(old_top, jnp.max(scores, axis=0, keepdims=True))
                raised = jnp.exp(scores - new_top)
                fade = jnp.exp(old_top - new_top)
                top[h : h + 1, :] = new_top
                total[h : h + 1, :] = total[h : h + 1, :] * fade + jnp.sum(
                    raised, axis=0, keepdims=True
                )
                part = dot_nn(v_j[h * HEAD_DIM : (h + 1) * HEAD_DIM, :], raised.astype(bf16))
                rows = slice(h * HEAD_DIM, (h + 1) * HEAD_DIM)
                acc[rows, :] = acc[rows, :] * fade + part

        def plain(j, unused):
            key_block(j, False)
            return unused

        lax.fori_loop(0, i, plain, 0)
        key_block(i, True)

        @pl.when((i + 1 < blocks) & crosses((i + 1) * TILE, starts))
        def _():
            key_block(i + 1, True)

        for h in range(OWN_HEADS):
            rows = slice(h * HEAD_DIM, (h + 1) * HEAD_DIM)
            acc[rows, :] = acc[rows, :] / total[h : h + 1, :]
        place = ((i // 2) ^ me) * (2 * TILE) + (i % 2) * TILE
        mixed[pl.ds(pl.multiple_of(place, TILE), TILE), :] = acc[...].T.astype(bf16)
        logs[i] = top[...] + jnp.log(jnp.maximum(total[...], 1e-30))
        return unused

    lax.fori_loop(0, blocks, query_block, 0)


def attend(facts, near, far):
    rows = near.shape[0] + far.shape[0]
    blocks = rows // TILE
    vmem = pl.BlockSpec(memory_space=pltpu.VMEM)
    return pl.pallas_call(
        functools.partial(attend_kernel, blocks),
        out_shape=(
            jax.ShapeDtypeStruct((rows, OWN), bf16),
            jax.ShapeDtypeStruct((blocks, 8, TILE), f32),
        ),
        in_specs=[pl.BlockSpec(memory_space=pltpu.SMEM), vmem, vmem],
        out_specs=(vmem, vmem),
        scratch_shapes=[
            pltpu.VMEM((blocks, TILE, OWN), bf16),
            pltpu.VMEM((blocks, TILE, OWN), bf16),
            pltpu.VMEM((blocks, OWN, TILE), bf16),
            pltpu.VMEM((OWN, TILE), f32),
            pltpu.VMEM((8, TILE), f32),
            pltpu.VMEM((8, TILE), f32),
        ],
        compiler_params=pltpu.CompilerParams(vmem_limit_bytes=48 * 2**20),
        cost_estimate=LIGHT,
        name="attend",
    )(facts, near, far)


def attend_back_kernel(
    blocks, pair, facts, near, far, mixed, g0, g1, g2, g3, logs, grads,
    q_own, k_own, v_own, k_turned, g_own, q_heads, g_heads, deltas, q_grad, k_grad, v_grad, k_heads, v_heads,
):
    me = facts[0]
    starts = [facts[1 + i] for i in range(facts.shape[0] - 1)]
    wide = PAIR * HEAD_DIM
    lane = pair * wide
    lanes = lax.broadcasted_iota(jnp.int32, (TILE, wide), 1) // HEAD_DIM
    pick = (
        lax.broadcasted_iota(jnp.int32, (8, wide), 1) // HEAD_DIM
        == lax.broadcasted_iota(jnp.int32, (8, wide), 0)
    ).astype(f32)
    for j in range(N_SHARD):
        src = near if j < 2 else far
        grad_src = (g0, g1, g2, g3)[j]
        base = (j % 2) * 2 * TILE
        for half in range(2):
            rows = slice(base + half * TILE, base + (half + 1) * TILE)
            at = (me ^ j) * 2 + half
            q_tile = src[rows, lane : lane + wide] * jnp.asarray(HEAD_DIM**-0.5, bf16)
            k_tile = src[rows, OWN + lane : OWN + lane + wide]
            g_tile = grad_src[half * TILE : (half + 1) * TILE, lane : lane + wide]
            o_rows = slice(j * 2 * TILE + half * TILE, j * 2 * TILE + (half + 1) * TILE)
            o_tile = mixed[o_rows, lane : lane + wide]
            q_own[at] = q_tile
            k_own[at] = k_tile
            v_own[at] = src[rows, 2 * OWN + lane : 2 * OWN + lane + wide]
            k_turned[at] = k_tile.astype(f32).T.astype(bf16)
            g_own[at] = g_tile
            for h in range(PAIR):
                place = slice(h * TILE, (h + 1) * TILE)
                q_heads[at, place, :] = jnp.where(lanes == h, q_tile, jnp.zeros_like(q_tile))
                g_heads[at, place, :] = jnp.where(lanes == h, g_tile, jnp.zeros_like(g_tile))
            both = g_tile.astype(f32) * o_tile.astype(f32)
            deltas[at] = lax.dot_general(
                pick, both, (((1,), (1,)), ((), ())),
                precision=lax.Precision.HIGHEST, preferred_element_type=f32,
            )
    q_grad[...] = jnp.zeros_like(q_grad)

    def key_block(j, unused):
        k_j = k_own[j]
        v_j = v_own[j]
        for h in range(PAIR):
            k_heads[h * TILE : (h + 1) * TILE, :] = jnp.where(lanes == h, k_j, jnp.zeros_like(k_j))
            v_heads[h * TILE : (h + 1) * TILE, :] = jnp.where(lanes == h, v_j, jnp.zeros_like(v_j))
        k_grad[...] = jnp.zeros_like(k_grad)
        v_grad[...] = jnp.zeros_like(v_grad)

        def query_block(i, masked):
            q_i = q_own[i]
            g_i = g_own[i]
            kt = k_turned[j]
            seen = visible_tile(j, i, starts) if masked else None
            softs = []
            scored = []
            for h in range(PAIR):
                rows = slice(h * TILE, (h + 1) * TILE)
                at = pair * PAIR + h
                scores = dot_nt(k_heads[rows, :], q_i)
                soft = jnp.exp(scores - logs[i, at : at + 1, :])
                if masked:
                    soft = jnp.where(seen, soft, 0.0)
                grad_soft = dot_nt(v_heads[rows, :], g_i)
                grad_scores = (soft * (grad_soft - deltas[i, h : h + 1, :])).astype(bf16)
                softs.append(soft.astype(bf16))
                scored.append(grad_scores)
                head = slice(h * HEAD_DIM, (h + 1) * HEAD_DIM)
                q_grad[i, head, :] += dot_nn(kt[head, :], grad_scores)
            v_grad[...] += dot_nn(jnp.concatenate(softs, axis=1), g_heads[i])
            k_grad[...] += dot_nn(jnp.concatenate(scored, axis=1), q_heads[i])

        def plain(i, unused):
            query_block(i, False)
            return unused

        @pl.when((j > 0) & crosses(j * TILE, starts))
        def _():
            query_block(j - 1, True)

        query_block(j, True)
        lax.fori_loop(j + 1, blocks, plain, 0)
        place = pl.multiple_of(((j // 2) ^ me) * (2 * TILE) + (j % 2) * TILE, TILE)
        grads[pl.ds(place, TILE), wide : 2 * wide] = k_grad[...].astype(bf16)
        grads[pl.ds(place, TILE), 2 * wide : 3 * wide] = v_grad[...].astype(bf16)
        return unused

    lax.fori_loop(0, blocks, key_block, 0)

    def write_query(i, unused):
        place = pl.multiple_of(((i // 2) ^ me) * (2 * TILE) + (i % 2) * TILE, TILE)
        grads[pl.ds(place, TILE), 0:wide] = (q_grad[i] * HEAD_DIM**-0.5).T.astype(bf16)
        return unused

    lax.fori_loop(0, blocks, write_query, 0)


def attend_back(pair, facts, near, far, mixed, grad_blocks, logs):
    rows = near.shape[0] + far.shape[0]
    blocks = rows // TILE
    wide = PAIR * HEAD_DIM
    vmem = pl.BlockSpec(memory_space=pltpu.VMEM)
    tile = lambda n, m, kind: pltpu.VMEM((n, m), kind)
    stack = lambda n, m, kind: pltpu.VMEM((blocks, n, m), kind)
    return pl.pallas_call(
        functools.partial(attend_back_kernel, blocks, pair),
        out_shape=jax.ShapeDtypeStruct((rows, 3 * wide), bf16),
        in_specs=[pl.BlockSpec(memory_space=pltpu.SMEM)] + [vmem] * 8,
        out_specs=vmem,
        scratch_shapes=[
            stack(TILE, wide, bf16),
            stack(TILE, wide, bf16),
            stack(TILE, wide, bf16),
            stack(wide, TILE, bf16),
            stack(TILE, wide, bf16),
            stack(PAIR * TILE, wide, bf16),
            stack(PAIR * TILE, wide, bf16),
            stack(8, TILE, f32),
            stack(wide, TILE, f32),
            tile(TILE, wide, f32),
            tile(TILE, wide, f32),
            tile(PAIR * TILE, wide, bf16),
            tile(PAIR * TILE, wide, bf16),
        ],
        compiler_params=pltpu.CompilerParams(vmem_limit_bytes=48 * 2**20),
        cost_estimate=LIGHT,
        name="attend_back",
    )(facts, near, far, mixed, *grad_blocks, logs)


def expert_tile(counts, step, tiles):
    block = step // tiles
    start = (step % tiles) * TILE
    border = counts[block, 0] - start
    late = lax.broadcasted_iota(jnp.int32, (TILE, 1), 0) >= border
    return border, late


def take_rows(step, tiles, rows_a, rows_b, taken):
    @pl.when(step < tiles)
    def _():
        taken[...] = rows_a[...]

    @pl.when(step >= tiles)
    def _():
        taken[...] = rows_b[...]


def give_rows(step, tiles, given, out_a, out_b):
    @pl.when(step < tiles)
    def _():
        out_a[...] = given[...]

    @pl.when(step >= tiles)
    def _():
        out_b[...] = given[...]


def by_expert_rows(border, late, work, out):
    @pl.when(border > 0)
    def _():
        out[...] = work(0)

    @pl.when(border < TILE)
    def _():
        out[...] = jnp.where(late, work(1), out[...])


def expert_kernel(tiles, counts, rows_a, rows_b, w_in, in_bias, w_back, hidden, out_a, out_b, taken, given):
    step = pl.program_id(0)
    border, late = expert_tile(counts, step, tiles)
    take_rows(step, tiles, rows_a, rows_b, taken)
    by_expert_rows(
        border,
        late,
        lambda e: jnp.maximum(dot_nn(taken[...], w_in[e]) + in_bias[e : e + 1, :], 0.0).astype(bf16),
        hidden,
    )
    by_expert_rows(border, late, lambda e: dot_nn(hidden[...], w_back[e]).astype(bf16), given)
    give_rows(step, tiles, given, out_a, out_b)


def expert_back_kernel(tiles, counts, rows_a, rows_b, hidden, w_in, w_back, grad_pre, out_a, out_b, taken, given):
    step = pl.program_id(0)
    border, late = expert_tile(counts, step, tiles)
    take_rows(step, tiles, rows_a, rows_b, taken)
    by_expert_rows(
        border,
        late,
        lambda e: jnp.where(hidden[...] > 0, dot_nt(taken[...], w_back[e]), 0.0).astype(bf16),
        grad_pre,
    )
    by_expert_rows(border, late, lambda e: dot_nt(grad_pre[...], w_in[e]).astype(bf16), given)
    give_rows(step, tiles, given, out_a, out_b)


def expert_specs(rows, width, inner):
    tiles = rows // TILE
    first = pl.BlockSpec((TILE, width), lambda i, c: (jnp.minimum(i, tiles - 1), 0))
    second = pl.BlockSpec((TILE, width), lambda i, c: (jnp.maximum(i - tiles, 0), 0))
    both = pl.BlockSpec((TILE, inner), lambda i, c: (i, 0))
    once = pl.Buffered(1)
    w_in = pl.BlockSpec((EXPERTS, width, inner), lambda i, c: (0, 0, 0), pipeline_mode=once)
    w_back = pl.BlockSpec((EXPERTS, inner, width), lambda i, c: (0, 0, 0), pipeline_mode=once)
    bias = pl.BlockSpec((EXPERTS, inner), lambda i, c: (0, 0), pipeline_mode=once)
    return tiles, first, second, both, w_in, w_back, bias


def run_experts(counts, rows_a, rows_b, w_in, in_bias, w_back):
    rows, width = rows_a.shape
    inner = w_in.shape[2]
    tiles, first, second, both, in_spec, back_spec, bias_spec = expert_specs(rows, width, inner)
    return pl.pallas_call(
        functools.partial(expert_kernel, tiles),
        grid_spec=pltpu.PrefetchScalarGridSpec(
            num_scalar_prefetch=1,
            grid=(2 * tiles,),
            in_specs=[first, second, in_spec, bias_spec, back_spec],
            out_specs=[both, first, second],
            scratch_shapes=[pltpu.VMEM((TILE, width), bf16)] * 2,
        ),
        out_shape=(
            jax.ShapeDtypeStruct((2 * rows, inner), bf16),
            jax.ShapeDtypeStruct((rows, width), bf16),
            jax.ShapeDtypeStruct((rows, width), bf16),
        ),
        compiler_params=pltpu.CompilerParams(vmem_limit_bytes=40 * 2**20),
        cost_estimate=LIGHT,
        name="experts",
    )(counts, rows_a, rows_b, w_in, in_bias, w_back)


def run_experts_back(counts, rows_a, rows_b, hidden, w_in, w_back):
    rows, width = rows_a.shape
    inner = w_in.shape[2]
    tiles, first, second, both, in_spec, back_spec, bias_spec = expert_specs(rows, width, inner)
    return pl.pallas_call(
        functools.partial(expert_back_kernel, tiles),
        grid_spec=pltpu.PrefetchScalarGridSpec(
            num_scalar_prefetch=1,
            grid=(2 * tiles,),
            in_specs=[first, second, both, in_spec, back_spec],
            out_specs=[both, first, second],
            scratch_shapes=[pltpu.VMEM((TILE, width), bf16)] * 2,
        ),
        out_shape=(
            jax.ShapeDtypeStruct((2 * rows, inner), bf16),
            jax.ShapeDtypeStruct((rows, width), bf16),
            jax.ShapeDtypeStruct((rows, width), bf16),
        ),
        compiler_params=pltpu.CompilerParams(vmem_limit_bytes=40 * 2**20),
        cost_estimate=LIGHT,
        name="experts_back",
    )(counts, rows_a, rows_b, hidden, w_in, w_back)


def place_experts_kernel(facts, *refs):
    blocks, out = refs[:6], refs[6]
    expert, turn = pl.program_id(0), pl.program_id(1)

    def write(block):
        owners, rows, width = block.shape[-3:]
        for j in range(owners):
            at = pl.multiple_of((facts[0] ^ j) * width, width) if owners > 1 else 0
            out[0, :, pl.ds(at, width)] = (block[0, j] if len(block.shape) == 4 else block[j]).astype(f32)

    for part in range(2):
        for source, block in enumerate(blocks[3 * part : 3 * part + 3]):

            @pl.when((expert == part) & (jnp.minimum(turn, 2) == source))
            def _():
                write(block)


def place_experts(me, parts):
    owners, rows, width = parts[0][0].shape
    whole = pl.BlockSpec((owners, rows, width), lambda e, t, s: (0, 0, 0))

    def last(part):
        return pl.BlockSpec(
            (1, owners, rows, width),
            lambda e, t, s: (jnp.clip((e - part) * QUARTERS + t - 2, 0, 1), 0, 0, 0),
        )

    return pl.pallas_call(
        place_experts_kernel,
        grid_spec=pltpu.PrefetchScalarGridSpec(
            num_scalar_prefetch=1,
            grid=(2, QUARTERS),
            in_specs=[whole, whole, last(0), whole, whole, last(1)],
            out_specs=pl.BlockSpec(
                (1, rows, owners * width), lambda e, t, s: (e, s[1 + e * QUARTERS + t], 0)
            ),
        ),
        out_shape=jax.ShapeDtypeStruct((2, QUARTERS * rows, owners * width), f32),
        compiler_params=pltpu.CompilerParams(vmem_limit_bytes=24 * 2**20),
        cost_estimate=LIGHT,
        name="place_experts",
    )(jnp.concatenate([me[None], rep_places()]), *[b for p in parts for b in p])


def place_attention_kernel(facts, *refs):
    blocks, qkv_out, whole_out = refs[:6], refs[6], refs[7]
    rows = qkv_out.shape[0] // (2 * QUARTERS)
    for part in range(2):
        own, second, last = blocks[3 * part : 3 * part + 3]
        for turn in range(QUARTERS):
            block = (own, second, last.at[0], last.at[1])[turn]
            segment = part * QUARTERS + facts[1 + part * QUARTERS + turn]
            to = pl.ds(pl.multiple_of(segment * rows, rows), rows)
            for c in range(3):
                for j in range(N_SHARD):
                    at = pl.multiple_of(c * N_SHARD * OWN + (facts[0] ^ j) * OWN, OWN)
                    start = (c * N_SHARD + j) * rows
                    qkv_out[to, pl.ds(at, OWN)] = block[start : start + rows, :].astype(f32)
            for x in range(N_SHARD):
                start = (3 * N_SHARD + x) * rows
                whole_out[to, x * OWN : (x + 1) * OWN] = block[start : start + rows, :].astype(f32)


def place_attention(me, parts, rows):
    vmem = pl.BlockSpec(memory_space=pltpu.VMEM)
    return pl.pallas_call(
        place_attention_kernel,
        out_shape=(
            jax.ShapeDtypeStruct((rows, 3 * N_SHARD * OWN), f32),
            jax.ShapeDtypeStruct((rows, N_SHARD * OWN), f32),
        ),
        in_specs=[pl.BlockSpec(memory_space=pltpu.SMEM)] + [vmem] * 6,
        out_specs=(vmem, vmem),
        compiler_params=pltpu.CompilerParams(vmem_limit_bytes=24 * 2**20),
        cost_estimate=LIGHT,
        name="place_attention",
    )(jnp.concatenate([me[None], rep_places()]), *[b for p in parts for b in p])


def shards(
    n_rep,
    tokens,
    token_ids,
    hash_table,
    piece_starts,
    valid_mask,
    teacher,
    cotangent,
    ln1_gain,
    ln1_bias,
    w_qkv,
    w_out,
    out_bias,
    ln2_gain,
    ln2_bias,
    w_in,
    in_bias,
    w_back,
    back_bias,
):
    local_rows = tokens.shape[0]
    tokens_all = local_rows * N_SHARD * n_rep
    me = lax.axis_index("shard").astype(jnp.int32)
    rep_at = lax.axis_index("rep")
    inner = w_back.shape[1]
    shard_width = ln1_gain.shape[0]
    seg_rows = shard_width // n_rep
    facts = jnp.concatenate([me[None], piece_starts[0]])

    expert_of = jnp.take(hash_table, token_ids)
    places = jnp.arange(local_rows, dtype=jnp.int32)
    earlier = (expert_of[:, None] == expert_of[None, :]) & (places[None, :] < places[:, None])
    slot_of = jnp.sum(earlier.astype(jnp.int32), axis=1)
    kept = slot_of < CAP
    is_late = expert_of > 0
    early_count = jnp.minimum(local_rows - jnp.sum(is_late.astype(jnp.int32)), CAP)
    sorted_at = jnp.where(kept, slot_of + jnp.where(is_late, early_count, 0), -1)
    sorter = (sorted_at[None, :] == places[:, None]).astype(bf16)
    counted = valid_mask.astype(f32)
    own_facts = jnp.stack([early_count.astype(f32), jnp.sum(valid_mask).astype(f32)])

    packed = jnp.concatenate(
        [
            jnp.stack([ln1_gain, ln1_bias, out_bias, ln2_gain, ln2_bias]),
            back_bias,
            jnp.zeros((1, shard_width), bf16),
        ],
        axis=0,
    )
    packed = jnp.concatenate([packed, jnp.zeros((8, 3 * OWN - shard_width), bf16)], axis=1)
    qkv_sends = [
            jnp.concatenate(
                [
                    jnp.concatenate(
                        [
                            lax.dynamic_slice_in_dim(w_qkv, c * D + (me ^ j) * OWN, OWN, axis=1)
                            for c in range(3)
                        ],
                        axis=1,
                    ),
                    packed,
                ],
                axis=0,
            )
            for j in range(N_SHARD)
    ]
    over = swap(jnp.stack(qkv_sends[2:]), 3)
    tok_far = swap(tokens, 2)
    thin = lax.dynamic_slice_in_dim(w_in, rep_at * seg_rows, seg_rows, axis=1)
    thin_sends = [lax.dynamic_slice_in_dim(thin, (me ^ j) * inner, inner, axis=2) for j in range(N_SHARD)]
    over = tie(over, thin_sends)
    near = swap(qkv_sends[1], 1)
    tok_near = swap(tokens, 1)
    tok_both = swap(tok_far, 1)
    qkv_blocks = (qkv_sends[0], near, swap(over[0], 1), over[1])
    thin_blocks = exchange_blocks(tie(thin_sends, (tok_both, qkv_blocks[2])))

    first_near, qkv_near, qkv_weight, rows_of = project(
        tie(facts, (tok_both, own_facts, sorter)), tokens, tok_near, qkv_blocks
    )
    gain_one, bias_one, out_shift, gain_two, bias_two = [rows_of[i] for i in range(5)]
    back_shift = rows_of[5:7]
    first_far, qkv_far = project(facts, tie(tok_far, qkv_near), tok_both, qkv_blocks)[:2]

    def first_rows(block):
        normed, inverse = layer_norm(block.astype(f32))
        return (normed * gain_one + bias_one).astype(bf16), normed, inverse

    thin_blocks = tie(thin_blocks, qkv_near)
    thin = in_order(
        me >> 1,
        in_order(me & 1, thin_blocks[0], thin_blocks[1]),
        in_order(me & 1, thin_blocks[2], thin_blocks[3]),
    ).reshape(N_SHARD, EXPERTS, seg_rows, inner)
    thin = lax.all_gather(thin.transpose(1, 0, 2, 3), "rep", axis=0)
    in_weight = thin.transpose(1, 2, 0, 3, 4).reshape(EXPERTS, D, inner)
    w_out = tie(w_out, tok_far)
    out_far = swap(w_out, 2)

    own_facts = jnp.broadcast_to(tie(own_facts, qkv_far)[:, None], (2, 128))
    shared = jnp.stack(exchange_blocks([own_facts] * N_SHARD))
    borders = shared[:, 0, 0].astype(jnp.int32)
    counts_near = borders[:2, None]
    chunk = local_rows // CHUNKS
    counts_far = [borders[2:, None] - h * chunk for h in range(CHUNKS)]

    mixed, logs = attend(facts, qkv_near, qkv_far)
    count_all = jnp.sum(shared[:, 1], axis=0, keepdims=True)
    for bit in range(n_rep.bit_length() - 1):
        count_all = count_all + rep_swap(count_all, 1 << bit, n_rep)
    count_all = count_all[0, 0]
    out_far = tie(out_far, mixed)
    out_blocks = (w_out, swap(w_out, 1), out_far, swap(out_far, 1))
    mixed_blocks = exchange_blocks(
        [mixed[j * local_rows : (j + 1) * local_rows] for j in range(N_SHARD)]
    )
    mixed_blocks = mixed_blocks[:2] + lax.optimization_barrier(mixed_blocks[2:] + (borders,))[:2]
    tok_rows = tokens.astype(f32)
    branch = dot_nn(mixed_blocks[0], out_blocks[0])
    for j in range(1, N_SHARD):
        branch = branch + dot_nn(mixed_blocks[j], out_blocks[j])
    middle = tok_rows + branch + out_shift
    normed_two, inverse_two = layer_norm(middle)
    second_in = (normed_two * gain_two + bias_two).astype(bf16)
    sorted_in = dot_nn(sorter, second_in).astype(bf16)
    half_of = lambda value, h: value[h * chunk : (h + 1) * chunk]
    in_far = [swap(half_of(sorted_in, h), 2) for h in range(CHUNKS)]
    in_near = swap(sorted_in, 1)
    bias_in = in_bias.astype(f32)
    hidden_near, out0, out1 = run_experts(counts_near, sorted_in, in_near, in_weight, bias_in, w_back)
    token = out0
    in_both, hidden_far, far_sums = [], [], []
    for h in range(CHUNKS):
        in_far[h] = tie(in_far[h], token)
        in_both.append(swap(in_far[h], 1))
        hidden, out2, out3 = run_experts(
            counts_far[h], in_far[h], in_both[h], in_weight, bias_in, w_back
        )
        hidden_far.append(hidden)
        token = scatter_far(out2, out3)
        far_sums.append(swap(token, 2))
    summed = scatter_near(out0, out1, jnp.concatenate(far_sums, axis=0))
    picked = dot_tn(sorter, summed.astype(bf16))
    picked = picked + jnp.where(is_late[:, None], back_shift[1], back_shift[0])
    final = middle + jnp.where(kept[:, None], picked, 0.0)
    grad_final = cotangent.astype(f32) + tokens_all / (2.0 * count_all) * counted[:, None] * (
        final - teacher.astype(f32)
    )
    grad_low = grad_final.astype(bf16)

    sorted_grad = dot_nn(sorter, grad_low).astype(bf16)
    grad_far = [swap(half_of(sorted_grad, h), 2) for h in range(CHUNKS)]
    grad_near = swap(sorted_grad, 1)
    pre_near, gin0, gin1 = run_experts_back(
        counts_near, sorted_grad, grad_near, hidden_near, in_weight, w_back
    )
    token = gin0
    grad_both, pre_far, far_second = [], [], []
    for h in range(CHUNKS):
        grad_far[h] = tie(grad_far[h], token)
        grad_both.append(swap(grad_far[h], 1))
        pre, gin2, gin3 = run_experts_back(
            counts_far[h], grad_far[h], grad_both[h], hidden_far[h], in_weight, w_back
        )
        pre_far.append(pre)
        token = scatter_far(gin2, gin3)
        far_second.append(swap(token, 2))
    send_second = token

    bounds = tie(borders, send_second)
    tile_rows = jnp.arange(TILE, dtype=jnp.int32)
    starts = range(0, chunk, TILE)
    tiles = [bounds[j] - h for j in range(2) for h in range(0, local_rows, TILE)]
    tiles += [
        bounds[j] - h * chunk - start for h in range(CHUNKS) for j in range(2, N_SHARD) for start in starts
    ]
    early = jnp.concatenate([tile_rows < bound for bound in tiles])
    masks = [early[:, None], ~early[:, None]]
    in_tile_order = lambda own, near, far, both: jnp.concatenate(
        [own, near] + [half for pair in zip(far, both) for half in pair], axis=0
    )
    hidden_all = jnp.concatenate([hidden_near] + hidden_far, axis=0)
    grad_all = in_tile_order(sorted_grad, grad_near, grad_far, grad_both)
    back_grads = [dot_tn(jnp.where(masks[0], hidden_all, 0), grad_all).astype(bf16)]
    back_grads.append(dot_tn(jnp.where(masks[1], hidden_all, 0), grad_all).astype(bf16))
    back_rows = EXPERTS * inner
    part = lambda a, i: lax.dynamic_index_in_dim(a, i, 1, keepdims=False)
    quarter_of = lambda a: lambda i: part(a, i)
    back_parts = [g.reshape(1, QUARTERS, inner // QUARTERS, D) for g in back_grads]
    back_sum = Steps(rep_sum_steps([quarter_of(g) for g in back_parts], n_rep, middle_none))
    pre_all = tie(jnp.concatenate([pre_near] + pre_far, axis=0), back_sum.sent)
    in_all = in_tile_order(sorted_in, in_near, in_far, in_both)
    in_grads = [dot_tn(in_all, jnp.where(m, pre_all, 0)).astype(bf16) for m in masks]
    quarter_rows = shard_width // QUARTERS
    in_parts = [g.reshape(N_SHARD, QUARTERS, quarter_rows, inner) for g in in_grads]

    def middle_in(values):
        blocks = [
            jnp.concatenate(
                [lax.dynamic_index_in_dim(v, me ^ j, 0, keepdims=False) for v in values], axis=0
            )
            for j in range(N_SHARD)
        ]
        moved = exchange_blocks(blocks)
        token = yield blocks
        moved = jnp.stack([tie(m, token) for m in moved])
        rows = values[0].shape[1]
        return [moved[:, p * rows : (p + 1) * rows] for p in range(len(values))]

    experts_sum = Steps(rep_sum_steps([quarter_of(g) for g in in_parts], n_rep, middle_in))

    far_second = tie(far_second, back_sum.step(experts_sum.sent))
    summed_grad = scatter_near(gin0, gin1, jnp.concatenate(far_second, axis=0))
    grad_second = dot_tn(sorter, summed_grad.astype(bf16))
    grad_gain_two = jnp.sum(grad_second * normed_two, axis=0)
    grad_bias_two = jnp.sum(grad_second, axis=0)
    grad_middle = grad_final + norm_back(grad_second, normed_two, inverse_two, gain_two)
    grad_branch = grad_middle.astype(bf16)
    grad_out_shift = jnp.sum(grad_branch.astype(f32), axis=0)
    grad_mixed_own = [dot_nt(grad_branch, w).astype(bf16) for w in out_blocks]
    grad_mixed = exchange_blocks(grad_mixed_own)
    out_parts = [dot_tn(b, tie(grad_branch, grad_mixed_own)).astype(bf16) for b in mixed_blocks]
    grad_mixed = lax.optimization_barrier((grad_mixed, out_parts))[0]
    sent = experts_sum.step((back_sum.step(grad_mixed_own), grad_mixed))

    half_grads = []
    near_tied = tie(qkv_near, sent)
    for pair in range(OWN_HEADS // PAIR):
        half_grads.append(attend_back(pair, facts, near_tied, qkv_far, mixed, grad_mixed, logs))
        if pair == 0:
            out_send = tie(scatter_far(out_parts[2], out_parts[3]), half_grads[0])
            out_far_sum = swap(out_send, 2)
            sent = experts_sum.step(half_grads[-1])
            sent = (out_send, sent, back_sum.step(sent))
        else:
            sent = experts_sum.step(back_sum.step(half_grads[-1]))
        near_tied = tie(qkv_near, sent)

    weight_halves = [
        jnp.concatenate(
            [
                qkv_weight[:, c * OWN + p * PAIR * HEAD_DIM : c * OWN + (p + 1) * PAIR * HEAD_DIM]
                for c in range(3)
            ],
            axis=1,
        )
        for p in range(OWN_HEADS // PAIR)
    ]

    def first_grad(j, token):
        rows = slice(j * local_rows, (j + 1) * local_rows)
        total = dot_nt(half_grads[0][rows], tie(weight_halves[0], token))
        for g, w in zip(half_grads[1:], weight_halves[1:]):
            total = total + dot_nt(g[rows], w)
        return total.astype(bf16)

    first2, first3 = first_grad(2, sent), first_grad(3, sent)
    send_first = scatter_far(first2, first3)
    far_first = swap(send_first, 2)

    sent = send_first
    first_all = tie(jnp.concatenate([first_near, first_far], axis=0), sent)
    half_weights = [dot_tn(first_all, g).astype(bf16) for g in half_grads]
    out_far_sum = tie(out_far_sum, half_grads[-1])
    out_grad = scatter_near(out_parts[0], out_parts[1], out_far_sum).astype(bf16)
    wide = PAIR * HEAD_DIM
    part_rows = quarter_rows // 2
    by_owner = [h.reshape(N_SHARD, 2, QUARTERS, part_rows, 3 * wide) for h in half_weights]
    out_quarters = out_grad.reshape(2, QUARTERS, part_rows, D)

    def last_quarter(p):
        def quarter(i):
            pieces = [part(h[:, p], i) for h in by_owner]
            rows = [
                jnp.concatenate([g[:, :, c * wide : (c + 1) * wide] for g in pieces], axis=2)
                for c in range(3)
            ]
            whole = lax.dynamic_index_in_dim(out_quarters[p], i, 0, keepdims=False)
            rows += [whole[:, x * OWN : (x + 1) * OWN] for x in range(N_SHARD)]
            return jnp.concatenate([r.reshape(-1, OWN) for r in rows], axis=0)

        return quarter

    def middle_last(values):
        rest = 3 * N_SHARD * part_rows
        moving = [
            v[:rest].reshape(3, N_SHARD, part_rows, OWN).transpose(1, 0, 2, 3).reshape(N_SHARD, -1, OWN)
            for v in values
        ]
        moved = yield from middle_in(moving)
        return [
            jnp.concatenate(
                [m.reshape(N_SHARD, 3, part_rows, OWN).transpose(1, 0, 2, 3).reshape(rest, OWN), v[rest:]],
                axis=0,
            )
            for m, v in zip(moved, values)
        ]

    last_sum = Steps(rep_sum_steps([last_quarter(0), last_quarter(1)], n_rep, middle_last))
    sent = last_sum.sent
    first0, first1 = first_grad(0, sent), first_grad(1, sent)
    sent = experts_sum.step((first0, first1))
    sent = last_sum.step(sent)
    back_grad = place_experts(me, back_sum.finish(sent))
    sent = last_sum.step(back_grad)
    sent = experts_sum.step(sent)
    grad_first = scatter_near(first0, first1, tie(far_first, sent))
    first_in, normed_one, inverse_one = first_rows(tie(tokens, sent))
    grad_gain_one = jnp.sum(grad_first * normed_one, axis=0)
    grad_bias_one = jnp.sum(grad_first, axis=0)
    input_grad = grad_middle + norm_back(grad_first, normed_one, inverse_one, gain_one)

    by_expert = jnp.stack([(kept & ~is_late), (kept & is_late)]).astype(bf16)
    grad_back_shift = dot_nn(by_expert, grad_low)
    in_shift_grad = jnp.concatenate(
        [dot_nn(m.astype(bf16).reshape(1, -1), pre_all) for m in masks], axis=0
    )
    small = jnp.concatenate(
        [
            jnp.stack([grad_gain_one, grad_bias_one, grad_out_shift, grad_gain_two, grad_bias_two]),
            grad_back_shift,
            jnp.zeros((1, D), f32),
        ],
        axis=0,
    )
    small = small + swap(small, 1)
    small = small + swap(small, 2)
    small = lax.dynamic_slice_in_dim(small, me * shard_width, shard_width, axis=1)
    small = jnp.concatenate([small, in_shift_grad.reshape(-1, shard_width)], axis=0)
    sent = last_sum.step((input_grad, small))
    bit = 1
    while bit < n_rep:
        small = small + tie(rep_swap(small, bit, n_rep), sent)
        sent = small
        bit *= 2
    sent = last_sum.step(sent)
    in_grad = place_experts(me, experts_sum.finish(sent))
    in_shift_grad = small[8:].reshape(EXPERTS, inner)
    qkv_grad, out_grad = place_attention(me, last_sum.finish(in_grad), shard_width)
    return (
        final.astype(bf16),
        input_grad,
        small[0],
        small[1],
        qkv_grad,
        out_grad,
        small[2],
        small[3],
        small[4],
        in_grad,
        in_shift_grad,
        back_grad,
        small[5:7],
    )


def solution(mesh):
    in_specs = (
        P(("rep", "shard"), None),
        P(("rep", "shard")),
        P(),
        P("rep", None),
        P(("rep", "shard")),
        P(("rep", "shard"), None),
        P(("rep", "shard"), None),
        P("shard"),
        P("shard"),
        P("shard", None),
        P("shard", None),
        P("shard"),
        P("shard"),
        P("shard"),
        P(None, "shard", None),
        P(None, "shard"),
        P(None, "shard", None),
        P(None, "shard"),
    )
    out_specs = (
        P(("rep", "shard"), None),
        P(("rep", "shard"), None),
        P("shard"),
        P("shard"),
        P("shard", None),
        P("shard", None),
        P("shard"),
        P("shard"),
        P("shard"),
        P(None, "shard", None),
        P(None, "shard"),
        P(None, "shard", None),
        P(None, "shard"),
    )
    body = functools.partial(shards, mesh.shape["rep"])
    return jax.shard_map(body, mesh=mesh, in_specs=in_specs, out_specs=out_specs, check_vma=False)
```

```python
import functools

import jax
import jax.numpy as jnp
from jax import lax
from jax.experimental import pallas as pl
from jax.experimental.pallas import tpu as pltpu
from jax.sharding import PartitionSpec as P

D = 1024
HEADS = 16
HEAD_DIM = 64
EXPERTS = 2
PIECE_LEN = 256
CAP = 320
N_SHARD = 4
OWN_HEADS = HEADS // N_SHARD
OWN = OWN_HEADS * HEAD_DIM
PAIR = 2
CHUNKS = 1
TILE = 256
NEG = -1e30

epsilon = 1e-05
LIGHT = pl.CostEstimate(flops=2**20, bytes_accessed=2**16, transcendentals=0)
f32 = jnp.float32
bf16 = jnp.bfloat16


def layer_norm(tok_rows):
    row_mean = jnp.mean(tok_rows, axis=-1, keepdims=True)
    centred = tok_rows - row_mean
    variance = jnp.mean(centred * centred, axis=-1, keepdims=True)
    inverse = lax.rsqrt(variance + epsilon)
    return (centred * inverse, inverse)


def norm_back(upstream, normed, inverse, norm_gain):
    scaled = upstream * norm_gain
    first_mean = jnp.mean(scaled, axis=-1, keepdims=True)
    second_mean = jnp.mean(scaled * normed, axis=-1, keepdims=True)
    return inverse * (scaled - first_mean - normed * second_mean)


def dot_nn(a, b):
    return lax.dot_general(a, b, (((1,), (0,)), ((), ())), preferred_element_type=f32)


def dot_nt(a, b):
    return lax.dot_general(a, b, (((1,), (1,)), ((), ())), preferred_element_type=f32)


def dot_tn(a, b):
    return lax.dot_general(a, b, (((0,), (0,)), ((), ())), preferred_element_type=f32)


def tie(value, after):
    return lax.optimization_barrier((value, after))[0]


def swap(value, mask):
    return lax.ppermute(value, "shard", [(i, i ^ mask) for i in range(N_SHARD)])


def exchange_blocks(blocks):
    return (blocks[0], swap(blocks[1], 1), swap(blocks[2], 2), swap(blocks[3], 3))


def in_order(side, own, other):
    return jnp.where(side == 0, jnp.stack([own, other]), jnp.stack([other, own]))


def scatter_far(block_two, block_three):
    near = swap(block_three, 1)
    return (block_two.astype(f32) + near.astype(f32)).astype(bf16)


def scatter_near(block_zero, block_one, far):
    near = swap(block_one, 1)
    return block_zero.astype(f32) + near.astype(f32) + far.astype(f32)


def rep_swap(value, mask, count):
    return lax.ppermute(value, "rep", [(i, i ^ mask) for i in range(count)])


QUARTERS = 4
ORDERS = ((1, 2), (2, 1))


def added(value, other, token):
    return (value.astype(f32) + tie(other, token).astype(f32)).astype(bf16)


def rep_sum_steps(quarters, count, middle):
    place = lax.axis_index("rep") & (QUARTERS - 1)
    sent = [jnp.stack([q(place ^ a), q(place ^ a ^ b)]) for q, (a, b) in zip(quarters, ORDERS)]
    others = [rep_swap(v, a, count) for v, (a, b) in zip(sent, ORDERS)]
    token = yield sent
    stay = [added(q(place), other[0], token) for q, other in zip(quarters, others)]
    sent = [
        added(q(place ^ b), other[1], token)
        for q, other, (a, b) in zip(quarters, others, ORDERS)
    ]
    others = [rep_swap(v, b, count) for v, (a, b) in zip(sent, ORDERS)]
    token = yield sent
    values = [added(v, other, token) for v, other in zip(stay, others)]
    mask = QUARTERS
    while mask < count:
        both = jnp.stack(values)
        other = rep_swap(both, mask, count)
        token = yield both
        values = [added(v, other[p], token) for p, v in enumerate(values)]
        mask *= 2
    values = yield from middle(values)
    others = [rep_swap(v, b, count) for v, (a, b) in zip(values, ORDERS)]
    token = yield values
    others = [tie(other, token) for other in others]
    sent = [jnp.stack([v, other]) for v, other in zip(values, others)]
    lasts = [rep_swap(v, a, count) for v, (a, b) in zip(sent, ORDERS)]
    token = yield sent
    return [(v, other, tie(last, token)) for v, other, last in zip(values, others, lasts)]


def rep_places():
    place = lax.axis_index("rep").astype(jnp.int32) & (QUARTERS - 1)
    return jnp.stack([place ^ mask for a, b in ORDERS for mask in (0, b, a, a ^ b)])


def middle_none(values):
    yield from ()
    return values


class Steps:
    def __init__(self, steps):
        self.steps = steps
        self.result = None
        self.sent = next(steps)

    def step(self, token):
        if self.result is not None:
            return token
        try:
            self.sent = self.steps.send(token)
        except StopIteration as end:
            self.result = end.value
            return token
        return self.sent

    def finish(self, token):
        while self.result is None:
            self.step(token)
        return self.result


def project_kernel(facts, tok_a, tok_b, w0, w1, w2, w3, first, qkv, weight, params, gains):
    me = facts[0]
    part, columns = weight.shape[0] // N_SHARD, weight.shape[1]
    for j, block in enumerate((w0, w1, w2, w3)):
        at = (me ^ j) * part
        weight[pl.ds(pl.multiple_of(at, part), part), :] = block[0:part, :]
        gains[:, pl.ds(pl.multiple_of(at, part), part)] = block[part : part + 8, 0:part].astype(f32)
    params[...] = gains[...]
    for half, tok in enumerate((tok_a, tok_b)):
        for start in range(0, tok.shape[0], TILE):
            normed = layer_norm(tok[start : start + TILE, :].astype(f32))[0]
            low = (normed * gains[0:1, :] + gains[1:2, :]).astype(bf16)
            rows = slice(half * tok.shape[0] + start, half * tok.shape[0] + start + TILE)
            first[rows, :] = low
            qkv[rows, :] = dot_nn(low, weight[...]).astype(bf16)


def project(facts, tok_a, tok_b, blocks):
    rows, width = tok_a.shape
    columns = blocks[0].shape[1]
    vmem = pl.BlockSpec(memory_space=pltpu.VMEM)
    return pl.pallas_call(
        project_kernel,
        out_shape=(
            jax.ShapeDtypeStruct((2 * rows, width), bf16),
            jax.ShapeDtypeStruct((2 * rows, columns), bf16),
            jax.ShapeDtypeStruct((width, columns), bf16),
            jax.ShapeDtypeStruct((8, width), f32),
        ),
        in_specs=[pl.BlockSpec(memory_space=pltpu.SMEM)] + [vmem] * 6,
        out_specs=(vmem,) * 4,
        scratch_shapes=[pltpu.VMEM((8, width), f32)],
        compiler_params=pltpu.CompilerParams(vmem_limit_bytes=32 * 2**20),
        cost_estimate=LIGHT,
        name="project",
    )(facts, tok_a, tok_b, *blocks)


def visible_tile(key_start, query_start, keys, queries, starts):
    key_pos = key_start + lax.broadcasted_iota(jnp.int32, (keys, queries), 0)
    query_pos = query_start + lax.broadcasted_iota(jnp.int32, (keys, queries), 1)
    seen = key_pos <= query_pos
    low = jnp.minimum(key_pos, query_pos)
    high = jnp.maximum(key_pos, query_pos)
    for start in starts:
        seen = seen | ((low >= start) & (high < start + PIECE_LEN))
    return seen


def crosses(boundary, starts):
    met = jnp.bool_(False)
    for start in starts:
        met = met | ((start < boundary) & (start + PIECE_LEN > boundary))
    return met


def head_lanes(rows):
    return lax.broadcasted_iota(jnp.int32, (rows, OWN), 1) // HEAD_DIM


WIDE = 2 * TILE


def attend_kernel(blocks, facts, near, far, mixed, logs, q_own, k_own, v_turned, acc, top, total):
    me = facts[0]
    starts = [facts[1 + i] for i in range(facts.shape[0] - 1)]
    for j in range(N_SHARD):
        src = near if j < 2 else far
        rows = slice((j % 2) * WIDE, (j % 2 + 1) * WIDE)
        at = me ^ j
        q_own[at] = src[rows, 0:OWN] * jnp.asarray(HEAD_DIM**-0.5, bf16)
        k_own[at] = src[rows, OWN : 2 * OWN]
        v_turned[at] = src[rows, 2 * OWN : 3 * OWN].astype(f32).T.astype(bf16)
    lanes = head_lanes(WIDE)

    def query_block(i, unused):
        q_i = q_own[i]
        q_heads = [jnp.where(lanes == h, q_i, jnp.zeros_like(q_i)) for h in range(OWN_HEADS)]
        acc[...] = jnp.zeros_like(acc)
        top[...] = jnp.full_like(top, NEG)
        total[...] = jnp.zeros_like(total)

        def key_pair(p, masked):
            k_p = k_own[p]
            v_p = v_turned[p]
            seen = visible_tile(p * WIDE, i * WIDE, WIDE, WIDE, starts) if masked else None
            for h in range(OWN_HEADS):
                scores = dot_nt(k_p, q_heads[h])
                if masked:
                    scores = jnp.where(seen, scores, NEG)
                old_top = top[h : h + 1, :]
                new_top = jnp.maximum(old_top, jnp.max(scores, axis=0, keepdims=True))
                raised = jnp.exp(scores - new_top)
                fade = jnp.exp(old_top - new_top)
                top[h : h + 1, :] = new_top
                total[h : h + 1, :] = total[h : h + 1, :] * fade + jnp.sum(
                    raised, axis=0, keepdims=True
                )
                rows = slice(h * HEAD_DIM, (h + 1) * HEAD_DIM)
                acc[rows, :] = acc[rows, :] * fade + dot_nn(v_p[rows, :], raised.astype(bf16))

        def plain(p, unused):
            key_pair(p, False)
            return unused

        def edge(p, unused):
            key_pair(p, True)
            return unused

        lax.fori_loop(0, i, plain, 0)
        more = (i + 1 < blocks // 2) & crosses((i + 1) * WIDE, starts)
        lax.fori_loop(i, i + 1 + more.astype(jnp.int32), edge, 0)

        for h in range(OWN_HEADS):
            rows = slice(h * HEAD_DIM, (h + 1) * HEAD_DIM)
            acc[rows, :] = acc[rows, :] / total[h : h + 1, :]
        mixed[pl.ds(pl.multiple_of((i ^ me) * WIDE, WIDE), WIDE), :] = acc[...].T.astype(bf16)
        logs[i] = top[...] + jnp.log(jnp.maximum(total[...], 1e-30))
        return unused

    lax.fori_loop(0, blocks // 2, query_block, 0)


def attend(facts, near, far):
    rows = near.shape[0] + far.shape[0]
    blocks = rows // TILE
    vmem = pl.BlockSpec(memory_space=pltpu.VMEM)
    return pl.pallas_call(
        functools.partial(attend_kernel, blocks),
        out_shape=(
            jax.ShapeDtypeStruct((rows, OWN), bf16),
            jax.ShapeDtypeStruct((blocks // 2, 8, WIDE), f32),
        ),
        in_specs=[pl.BlockSpec(memory_space=pltpu.SMEM), vmem, vmem],
        out_specs=(vmem, vmem),
        scratch_shapes=[
            pltpu.VMEM((blocks // 2, WIDE, OWN), bf16),
            pltpu.VMEM((blocks // 2, WIDE, OWN), bf16),
            pltpu.VMEM((blocks // 2, OWN, WIDE), bf16),
            pltpu.VMEM((OWN, WIDE), f32),
            pltpu.VMEM((8, WIDE), f32),
            pltpu.VMEM((8, WIDE), f32),
        ],
        compiler_params=pltpu.CompilerParams(vmem_limit_bytes=48 * 2**20),
        cost_estimate=LIGHT,
        name="attend",
    )(facts, near, far)


def attend_back_kernel(
    blocks, pair, facts, near, far, mixed, g0, g1, g2, g3, logs, grads,
    q_own, k_own, v_own, k_turned, g_own, q_heads, g_heads, deltas, q_grad, k_grad, v_grad, k_heads, v_heads,
):
    me = facts[0]
    starts = [facts[1 + i] for i in range(facts.shape[0] - 1)]
    wide = PAIR * HEAD_DIM
    lane = pair * wide
    lanes = lax.broadcasted_iota(jnp.int32, (TILE, wide), 1) // HEAD_DIM
    pick = (
        lax.broadcasted_iota(jnp.int32, (8, wide), 1) // HEAD_DIM
        == lax.broadcasted_iota(jnp.int32, (8, wide), 0)
    ).astype(f32)
    for j in range(N_SHARD):
        src = near if j < 2 else far
        grad_src = (g0, g1, g2, g3)[j]
        at = me ^ j
        for half in range(2):
            base = (j % 2) * WIDE + half * TILE
            rows = slice(base, base + TILE)
            to = slice(half * TILE, (half + 1) * TILE)
            q_tile = src[rows, lane : lane + wide] * jnp.asarray(HEAD_DIM**-0.5, bf16)
            k_tile = src[rows, OWN + lane : OWN + lane + wide]
            g_tile = grad_src[to, lane : lane + wide]
            o_tile = mixed[j * WIDE + half * TILE : j * WIDE + (half + 1) * TILE, lane : lane + wide]
            q_own[at, to, :] = q_tile
            k_own[at, to, :] = k_tile
            v_own[at, to, :] = src[rows, 2 * OWN + lane : 2 * OWN + lane + wide]
            k_turned[at, :, to] = k_tile.astype(f32).T.astype(bf16)
            g_own[at, to, :] = g_tile
            for h in range(PAIR):
                place = slice(h * WIDE + half * TILE, h * WIDE + (half + 1) * TILE)
                q_heads[at, place, :] = jnp.where(lanes == h, q_tile, jnp.zeros_like(q_tile))
                g_heads[at, place, :] = jnp.where(lanes == h, g_tile, jnp.zeros_like(g_tile))
            both = g_tile.astype(f32) * o_tile.astype(f32)
            deltas[at, :, to] = lax.dot_general(
                pick, both, (((1,), (1,)), ((), ())),
                precision=lax.Precision.HIGHEST, preferred_element_type=f32,
            )
    q_grad[...] = jnp.zeros_like(q_grad)
    wide_lanes = lax.broadcasted_iota(jnp.int32, (WIDE, wide), 1) // HEAD_DIM

    def key_block(j, unused):
        k_j = k_own[j]
        v_j = v_own[j]
        for h in range(PAIR):
            rows = slice(h * WIDE, (h + 1) * WIDE)
            k_heads[rows, :] = jnp.where(wide_lanes == h, k_j, jnp.zeros_like(k_j))
            v_heads[rows, :] = jnp.where(wide_lanes == h, v_j, jnp.zeros_like(v_j))
        k_grad[...] = jnp.zeros_like(k_grad)
        v_grad[...] = jnp.zeros_like(v_grad)

        def query_pair(p, masked):
            q_p = q_own[p]
            g_p = g_own[p]
            kt = k_turned[j]
            seen = visible_tile(j * WIDE, p * WIDE, WIDE, WIDE, starts) if masked else None
            softs = []
            scored = []
            for h in range(PAIR):
                rows = slice(h * WIDE, (h + 1) * WIDE)
                at = pair * PAIR + h
                scores = dot_nt(k_heads[rows, :], q_p)
                soft = jnp.exp(scores - logs[p, at : at + 1, :])
                if masked:
                    soft = jnp.where(seen, soft, 0.0)
                grad_soft = dot_nt(v_heads[rows, :], g_p)
                grad_scores = (soft * (grad_soft - deltas[p, h : h + 1, :])).astype(bf16)
                softs.append(soft.astype(bf16))
                scored.append(grad_scores)
                head = slice(h * HEAD_DIM, (h + 1) * HEAD_DIM)
                q_grad[p, head, :] += dot_nn(kt[head, :], grad_scores)
            v_grad[...] += dot_nn(jnp.concatenate(softs, axis=1), g_heads[p])
            k_grad[...] += dot_nn(jnp.concatenate(scored, axis=1), q_heads[p])

        def plain(p, unused):
            query_pair(p, False)
            return unused

        def edge(p, unused):
            query_pair(p, True)
            return unused

        less = (j > 0) & crosses(j * WIDE, starts)
        lax.fori_loop(j - less.astype(jnp.int32), j + 1, edge, 0)
        lax.fori_loop(j + 1, blocks // 2, plain, 0)
        place = pl.multiple_of((j ^ me) * WIDE, WIDE)
        grads[pl.ds(place, WIDE), wide : 2 * wide] = k_grad[...].astype(bf16)
        grads[pl.ds(place, WIDE), 2 * wide : 3 * wide] = v_grad[...].astype(bf16)
        return unused

    lax.fori_loop(0, blocks // 2, key_block, 0)

    def write_query(p, unused):
        place = pl.multiple_of((p ^ me) * WIDE, WIDE)
        grads[pl.ds(place, WIDE), 0:wide] = (q_grad[p] * HEAD_DIM**-0.5).T.astype(bf16)
        return unused

    lax.fori_loop(0, blocks // 2, write_query, 0)


def attend_back(pair, facts, near, far, mixed, grad_blocks, logs):
    rows = near.shape[0] + far.shape[0]
    blocks = rows // TILE
    wide = PAIR * HEAD_DIM
    vmem = pl.BlockSpec(memory_space=pltpu.VMEM)
    tile = lambda n, m, kind: pltpu.VMEM((n, m), kind)
    double = lambda n, m, kind: pltpu.VMEM((blocks // 2, n, m), kind)
    return pl.pallas_call(
        functools.partial(attend_back_kernel, blocks, pair),
        out_shape=jax.ShapeDtypeStruct((rows, 3 * wide), bf16),
        in_specs=[pl.BlockSpec(memory_space=pltpu.SMEM)] + [vmem] * 8,
        out_specs=vmem,
        scratch_shapes=[
            double(WIDE, wide, bf16),
            double(WIDE, wide, bf16),
            double(WIDE, wide, bf16),
            double(wide, WIDE, bf16),
            double(WIDE, wide, bf16),
            double(PAIR * WIDE, wide, bf16),
            double(PAIR * WIDE, wide, bf16),
            double(8, WIDE, f32),
            double(wide, WIDE, f32),
            tile(WIDE, wide, f32),
            tile(WIDE, wide, f32),
            tile(PAIR * WIDE, wide, bf16),
            tile(PAIR * WIDE, wide, bf16),
        ],
        compiler_params=pltpu.CompilerParams(vmem_limit_bytes=48 * 2**20),
        cost_estimate=LIGHT,
        name="attend_back",
    )(facts, near, far, mixed, *grad_blocks, logs)


def expert_tile(counts, step, tiles):
    block = step // tiles
    start = (step % tiles) * TILE
    border = counts[block, 0] - start
    late = lax.broadcasted_iota(jnp.int32, (TILE, 1), 0) >= border
    return border, late


def take_rows(step, tiles, rows_a, rows_b, taken):
    @pl.when(step < tiles)
    def _():
        taken[...] = rows_a[...]

    @pl.when(step >= tiles)
    def _():
        taken[...] = rows_b[...]


def give_rows(step, tiles, given, out_a, out_b):
    @pl.when(step < tiles)
    def _():
        out_a[...] = given[...]

    @pl.when(step >= tiles)
    def _():
        out_b[...] = given[...]


def by_expert_rows(border, late, work, out):
    @pl.when(border > 0)
    def _():
        out[...] = work(0)

    @pl.when(border < TILE)
    def _():
        out[...] = jnp.where(late, work(1), out[...])


def expert_kernel(tiles, counts, rows_a, rows_b, w_in, in_bias, w_back, hidden, out_a, out_b, taken, given):
    step = pl.program_id(0)
    border, late = expert_tile(counts, step, tiles)
    take_rows(step, tiles, rows_a, rows_b, taken)
    by_expert_rows(
        border,
        late,
        lambda e: jnp.maximum(dot_nn(taken[...], w_in[e]) + in_bias[e : e + 1, :], 0.0).astype(bf16),
        hidden,
    )
    by_expert_rows(border, late, lambda e: dot_nn(hidden[...], w_back[e]).astype(bf16), given)
    give_rows(step, tiles, given, out_a, out_b)


def expert_back_kernel(tiles, counts, rows_a, rows_b, hidden, w_in, w_back, grad_pre, out_a, out_b, taken, given):
    step = pl.program_id(0)
    border, late = expert_tile(counts, step, tiles)
    take_rows(step, tiles, rows_a, rows_b, taken)
    by_expert_rows(
        border,
        late,
        lambda e: jnp.where(hidden[...] > 0, dot_nt(taken[...], w_back[e]), 0.0).astype(bf16),
        grad_pre,
    )
    by_expert_rows(border, late, lambda e: dot_nt(grad_pre[...], w_in[e]).astype(bf16), given)
    give_rows(step, tiles, given, out_a, out_b)


def expert_specs(rows, width, inner):
    tiles = rows // TILE
    first = pl.BlockSpec((TILE, width), lambda i, c: (jnp.minimum(i, tiles - 1), 0))
    second = pl.BlockSpec((TILE, width), lambda i, c: (jnp.maximum(i - tiles, 0), 0))
    both = pl.BlockSpec((TILE, inner), lambda i, c: (i, 0))
    once = pl.Buffered(1)
    w_in = pl.BlockSpec((EXPERTS, width, inner), lambda i, c: (0, 0, 0), pipeline_mode=once)
    w_back = pl.BlockSpec((EXPERTS, inner, width), lambda i, c: (0, 0, 0), pipeline_mode=once)
    bias = pl.BlockSpec((EXPERTS, inner), lambda i, c: (0, 0), pipeline_mode=once)
    return tiles, first, second, both, w_in, w_back, bias


def run_experts(counts, rows_a, rows_b, w_in, in_bias, w_back):
    rows, width = rows_a.shape
    inner = w_in.shape[2]
    tiles, first, second, both, in_spec, back_spec, bias_spec = expert_specs(rows, width, inner)
    return pl.pallas_call(
        functools.partial(expert_kernel, tiles),
        grid_spec=pltpu.PrefetchScalarGridSpec(
            num_scalar_prefetch=1,
            grid=(2 * tiles,),
            in_specs=[first, second, in_spec, bias_spec, back_spec],
            out_specs=[both, first, second],
            scratch_shapes=[pltpu.VMEM((TILE, width), bf16)] * 2,
        ),
        out_shape=(
            jax.ShapeDtypeStruct((2 * rows, inner), bf16),
            jax.ShapeDtypeStruct((rows, width), bf16),
            jax.ShapeDtypeStruct((rows, width), bf16),
        ),
        compiler_params=pltpu.CompilerParams(vmem_limit_bytes=40 * 2**20),
        cost_estimate=LIGHT,
        name="experts",
    )(counts, rows_a, rows_b, w_in, in_bias, w_back)


def run_experts_back(counts, rows_a, rows_b, hidden, w_in, w_back):
    rows, width = rows_a.shape
    inner = w_in.shape[2]
    tiles, first, second, both, in_spec, back_spec, bias_spec = expert_specs(rows, width, inner)
    return pl.pallas_call(
        functools.partial(expert_back_kernel, tiles),
        grid_spec=pltpu.PrefetchScalarGridSpec(
            num_scalar_prefetch=1,
            grid=(2 * tiles,),
            in_specs=[first, second, both, in_spec, back_spec],
            out_specs=[both, first, second],
            scratch_shapes=[pltpu.VMEM((TILE, width), bf16)] * 2,
        ),
        out_shape=(
            jax.ShapeDtypeStruct((2 * rows, inner), bf16),
            jax.ShapeDtypeStruct((rows, width), bf16),
            jax.ShapeDtypeStruct((rows, width), bf16),
        ),
        compiler_params=pltpu.CompilerParams(vmem_limit_bytes=40 * 2**20),
        cost_estimate=LIGHT,
        name="experts_back",
    )(counts, rows_a, rows_b, hidden, w_in, w_back)


def place_experts_kernel(facts, *refs):
    blocks, out = refs[:6], refs[6]
    expert, turn = pl.program_id(0), pl.program_id(1)

    def write(block):
        owners, rows, width = block.shape[-3:]
        for j in range(owners):
            at = pl.multiple_of((facts[0] ^ j) * width, width) if owners > 1 else 0
            out[0, :, pl.ds(at, width)] = (block[0, j] if len(block.shape) == 4 else block[j]).astype(f32)

    for part in range(2):
        for source, block in enumerate(blocks[3 * part : 3 * part + 3]):

            @pl.when((expert == part) & (jnp.minimum(turn, 2) == source))
            def _():
                write(block)


def place_experts(me, parts):
    owners, rows, width = parts[0][0].shape
    whole = pl.BlockSpec((owners, rows, width), lambda e, t, s: (0, 0, 0))

    def last(part):
        return pl.BlockSpec(
            (1, owners, rows, width),
            lambda e, t, s: (jnp.clip((e - part) * QUARTERS + t - 2, 0, 1), 0, 0, 0),
        )

    return pl.pallas_call(
        place_experts_kernel,
        grid_spec=pltpu.PrefetchScalarGridSpec(
            num_scalar_prefetch=1,
            grid=(2, QUARTERS),
            in_specs=[whole, whole, last(0), whole, whole, last(1)],
            out_specs=pl.BlockSpec(
                (1, rows, owners * width), lambda e, t, s: (e, s[1 + e * QUARTERS + t], 0)
            ),
        ),
        out_shape=jax.ShapeDtypeStruct((2, QUARTERS * rows, owners * width), f32),
        compiler_params=pltpu.CompilerParams(vmem_limit_bytes=24 * 2**20),
        cost_estimate=LIGHT,
        name="place_experts",
    )(jnp.concatenate([me[None], rep_places()]), *[b for p in parts for b in p])


def place_attention_kernel(facts, *refs):
    blocks, qkv_out, whole_out = refs[:6], refs[6], refs[7]
    rows = qkv_out.shape[0] // (2 * QUARTERS)
    for part in range(2):
        own, second, last = blocks[3 * part : 3 * part + 3]
        for turn in range(QUARTERS):
            block = (own, second, last.at[0], last.at[1])[turn]
            segment = part * QUARTERS + facts[1 + part * QUARTERS + turn]
            to = pl.ds(pl.multiple_of(segment * rows, rows), rows)
            for c in range(3):
                for j in range(N_SHARD):
                    at = pl.multiple_of(c * N_SHARD * OWN + (facts[0] ^ j) * OWN, OWN)
                    start = (c * N_SHARD + j) * rows
                    qkv_out[to, pl.ds(at, OWN)] = block[start : start + rows, :].astype(f32)
            for x in range(N_SHARD):
                start = (3 * N_SHARD + x) * rows
                whole_out[to, x * OWN : (x + 1) * OWN] = block[start : start + rows, :].astype(f32)


def place_attention(me, parts, rows):
    vmem = pl.BlockSpec(memory_space=pltpu.VMEM)
    return pl.pallas_call(
        place_attention_kernel,
        out_shape=(
            jax.ShapeDtypeStruct((rows, 3 * N_SHARD * OWN), f32),
            jax.ShapeDtypeStruct((rows, N_SHARD * OWN), f32),
        ),
        in_specs=[pl.BlockSpec(memory_space=pltpu.SMEM)] + [vmem] * 6,
        out_specs=(vmem, vmem),
        compiler_params=pltpu.CompilerParams(vmem_limit_bytes=24 * 2**20),
        cost_estimate=LIGHT,
        name="place_attention",
    )(jnp.concatenate([me[None], rep_places()]), *[b for p in parts for b in p])


def shards(
    n_rep,
    tokens,
    token_ids,
    hash_table,
    piece_starts,
    valid_mask,
    teacher,
    cotangent,
    ln1_gain,
    ln1_bias,
    w_qkv,
    w_out,
    out_bias,
    ln2_gain,
    ln2_bias,
    w_in,
    in_bias,
    w_back,
    back_bias,
):
    local_rows = tokens.shape[0]
    tokens_all = local_rows * N_SHARD * n_rep
    me = lax.axis_index("shard").astype(jnp.int32)
    rep_at = lax.axis_index("rep")
    inner = w_back.shape[1]
    shard_width = ln1_gain.shape[0]
    seg_rows = shard_width // n_rep
    facts = jnp.concatenate([me[None], piece_starts[0]])

    expert_of = jnp.take(hash_table, token_ids)
    places = jnp.arange(local_rows, dtype=jnp.int32)
    earlier = (expert_of[:, None] == expert_of[None, :]) & (places[None, :] < places[:, None])
    slot_of = jnp.sum(earlier.astype(jnp.int32), axis=1)
    kept = slot_of < CAP
    is_late = expert_of > 0
    early_count = jnp.minimum(local_rows - jnp.sum(is_late.astype(jnp.int32)), CAP)
    sorted_at = jnp.where(kept, slot_of + jnp.where(is_late, early_count, 0), -1)
    sorter = (sorted_at[None, :] == places[:, None]).astype(bf16)
    counted = valid_mask.astype(f32)
    own_facts = jnp.stack([early_count.astype(f32), jnp.sum(valid_mask).astype(f32)])

    packed = jnp.concatenate(
        [
            jnp.stack([ln1_gain, ln1_bias, out_bias, ln2_gain, ln2_bias]),
            back_bias,
            jnp.zeros((1, shard_width), bf16),
        ],
        axis=0,
    )
    packed = jnp.concatenate([packed, jnp.zeros((8, 3 * OWN - shard_width), bf16)], axis=1)
    qkv_sends = [
            jnp.concatenate(
                [
                    jnp.concatenate(
                        [
                            lax.dynamic_slice_in_dim(w_qkv, c * D + (me ^ j) * OWN, OWN, axis=1)
                            for c in range(3)
                        ],
                        axis=1,
                    ),
                    packed,
                ],
                axis=0,
            )
            for j in range(N_SHARD)
    ]
    over = swap(jnp.stack(qkv_sends[2:]), 3)
    tok_far = swap(tokens, 2)
    thin = lax.dynamic_slice_in_dim(w_in, rep_at * seg_rows, seg_rows, axis=1)
    thin_sends = [lax.dynamic_slice_in_dim(thin, (me ^ j) * inner, inner, axis=2) for j in range(N_SHARD)]
    over = tie(over, thin_sends)
    near = swap(qkv_sends[1], 1)
    tok_near = swap(tokens, 1)
    tok_both = swap(tok_far, 1)
    qkv_blocks = (qkv_sends[0], near, swap(over[0], 1), over[1])
    thin_blocks = exchange_blocks(tie(thin_sends, (tok_both, qkv_blocks[2])))

    first_near, qkv_near, qkv_weight, rows_of = project(
        tie(facts, (tok_both, own_facts, sorter)), tokens, tok_near, qkv_blocks
    )
    gain_one, bias_one, out_shift, gain_two, bias_two = [rows_of[i] for i in range(5)]
    back_shift = rows_of[5:7]
    first_far, qkv_far = project(facts, tie(tok_far, qkv_near), tok_both, qkv_blocks)[:2]

    def first_rows(block):
        normed, inverse = layer_norm(block.astype(f32))
        return (normed * gain_one + bias_one).astype(bf16), normed, inverse

    thin_blocks = tie(thin_blocks, qkv_near)
    thin = in_order(
        me >> 1,
        in_order(me & 1, thin_blocks[0], thin_blocks[1]),
        in_order(me & 1, thin_blocks[2], thin_blocks[3]),
    ).reshape(N_SHARD, EXPERTS, seg_rows, inner)
    thin = lax.all_gather(thin.transpose(1, 0, 2, 3), "rep", axis=0)
    in_weight = thin.transpose(1, 2, 0, 3, 4).reshape(EXPERTS, D, inner)
    w_out = tie(w_out, tok_far)
    out_far = swap(w_out, 2)

    own_facts = jnp.broadcast_to(tie(own_facts, qkv_far)[:, None], (2, 128))
    shared = jnp.stack(exchange_blocks([own_facts] * N_SHARD))
    borders = shared[:, 0, 0].astype(jnp.int32)
    counts_near = borders[:2, None]
    chunk = local_rows // CHUNKS
    counts_far = [borders[2:, None] - h * chunk for h in range(CHUNKS)]

    mixed, logs = attend(facts, qkv_near, qkv_far)
    count_all = jnp.sum(shared[:, 1], axis=0, keepdims=True)
    for bit in range(n_rep.bit_length() - 1):
        count_all = count_all + rep_swap(count_all, 1 << bit, n_rep)
    count_all = count_all[0, 0]
    out_far = tie(out_far, mixed)
    out_blocks = (w_out, swap(w_out, 1), out_far, swap(out_far, 1))
    mixed_blocks = exchange_blocks(
        [mixed[j * local_rows : (j + 1) * local_rows] for j in range(N_SHARD)]
    )
    mixed_blocks = mixed_blocks[:2] + lax.optimization_barrier(mixed_blocks[2:] + (borders,))[:2]
    tok_rows = tokens.astype(f32)
    branch = dot_nn(mixed_blocks[0], out_blocks[0])
    for j in range(1, N_SHARD):
        branch = branch + dot_nn(mixed_blocks[j], out_blocks[j])
    middle = tok_rows + branch + out_shift
    normed_two, inverse_two = layer_norm(middle)
    second_in = (normed_two * gain_two + bias_two).astype(bf16)
    sorted_in = dot_nn(sorter, second_in).astype(bf16)
    half_of = lambda value, h: value[h * chunk : (h + 1) * chunk]
    in_far = [swap(half_of(sorted_in, h), 2) for h in range(CHUNKS)]
    in_near = swap(sorted_in, 1)
    bias_in = in_bias.astype(f32)
    hidden_near, out0, out1 = run_experts(counts_near, sorted_in, in_near, in_weight, bias_in, w_back)
    token = out0
    in_both, hidden_far, far_sums = [], [], []
    for h in range(CHUNKS):
        in_far[h] = tie(in_far[h], token)
        in_both.append(swap(in_far[h], 1))
        hidden, out2, out3 = run_experts(
            counts_far[h], in_far[h], in_both[h], in_weight, bias_in, w_back
        )
        hidden_far.append(hidden)
        token = scatter_far(out2, out3)
        far_sums.append(swap(token, 2))
    summed = scatter_near(out0, out1, jnp.concatenate(far_sums, axis=0))
    picked = dot_tn(sorter, summed.astype(bf16))
    picked = picked + jnp.where(is_late[:, None], back_shift[1], back_shift[0])
    final = middle + jnp.where(kept[:, None], picked, 0.0)
    grad_final = cotangent.astype(f32) + tokens_all / (2.0 * count_all) * counted[:, None] * (
        final - teacher.astype(f32)
    )
    grad_low = grad_final.astype(bf16)

    sorted_grad = dot_nn(sorter, grad_low).astype(bf16)
    grad_far = [swap(half_of(sorted_grad, h), 2) for h in range(CHUNKS)]
    grad_near = swap(sorted_grad, 1)
    pre_near, gin0, gin1 = run_experts_back(
        counts_near, sorted_grad, grad_near, hidden_near, in_weight, w_back
    )
    token = gin0
    grad_both, pre_far, far_second = [], [], []
    for h in range(CHUNKS):
        grad_far[h] = tie(grad_far[h], token)
        grad_both.append(swap(grad_far[h], 1))
        pre, gin2, gin3 = run_experts_back(
            counts_far[h], grad_far[h], grad_both[h], hidden_far[h], in_weight, w_back
        )
        pre_far.append(pre)
        token = scatter_far(gin2, gin3)
        far_second.append(swap(token, 2))
    send_second = token

    bounds = tie(borders, send_second)
    tile_rows = jnp.arange(TILE, dtype=jnp.int32)
    starts = range(0, chunk, TILE)
    tiles = [bounds[j] - h for j in range(2) for h in range(0, local_rows, TILE)]
    tiles += [
        bounds[j] - h * chunk - start for h in range(CHUNKS) for j in range(2, N_SHARD) for start in starts
    ]
    early = jnp.concatenate([tile_rows < bound for bound in tiles])
    masks = [early[:, None], ~early[:, None]]
    in_tile_order = lambda own, near, far, both: jnp.concatenate(
        [own, near] + [half for pair in zip(far, both) for half in pair], axis=0
    )
    hidden_all = jnp.concatenate([hidden_near] + hidden_far, axis=0)
    grad_all = in_tile_order(sorted_grad, grad_near, grad_far, grad_both)
    back_grads = [dot_tn(jnp.where(masks[0], hidden_all, 0), grad_all).astype(bf16)]
    back_grads.append(dot_tn(jnp.where(masks[1], hidden_all, 0), grad_all).astype(bf16))
    back_rows = EXPERTS * inner
    part = lambda a, i: lax.dynamic_index_in_dim(a, i, 1, keepdims=False)
    quarter_of = lambda a: lambda i: part(a, i)
    back_parts = [g.reshape(1, QUARTERS, inner // QUARTERS, D) for g in back_grads]
    back_sum = Steps(rep_sum_steps([quarter_of(g) for g in back_parts], n_rep, middle_none))
    pre_all = tie(jnp.concatenate([pre_near] + pre_far, axis=0), back_sum.sent)
    in_all = in_tile_order(sorted_in, in_near, in_far, in_both)
    in_grads = [dot_tn(in_all, jnp.where(m, pre_all, 0)).astype(bf16) for m in masks]
    quarter_rows = shard_width // QUARTERS
    in_parts = [g.reshape(N_SHARD, QUARTERS, quarter_rows, inner) for g in in_grads]

    def middle_in(values):
        blocks = [
            jnp.concatenate(
                [lax.dynamic_index_in_dim(v, me ^ j, 0, keepdims=False) for v in values], axis=0
            )
            for j in range(N_SHARD)
        ]
        moved = exchange_blocks(blocks)
        token = yield blocks
        moved = jnp.stack([tie(m, token) for m in moved])
        rows = values[0].shape[1]
        return [moved[:, p * rows : (p + 1) * rows] for p in range(len(values))]

    experts_sum = Steps(rep_sum_steps([quarter_of(g) for g in in_parts], n_rep, middle_in))

    far_second = tie(far_second, back_sum.step(experts_sum.sent))
    summed_grad = scatter_near(gin0, gin1, jnp.concatenate(far_second, axis=0))
    grad_second = dot_tn(sorter, summed_grad.astype(bf16))
    grad_gain_two = jnp.sum(grad_second * normed_two, axis=0)
    grad_bias_two = jnp.sum(grad_second, axis=0)
    grad_middle = grad_final + norm_back(grad_second, normed_two, inverse_two, gain_two)
    grad_branch = grad_middle.astype(bf16)
    grad_out_shift = jnp.sum(grad_branch.astype(f32), axis=0)
    grad_mixed_own = [dot_nt(grad_branch, w).astype(bf16) for w in out_blocks]
    grad_mixed = exchange_blocks(grad_mixed_own)
    out_parts = [dot_tn(b, tie(grad_branch, grad_mixed_own)).astype(bf16) for b in mixed_blocks]
    grad_mixed = lax.optimization_barrier((grad_mixed, out_parts))[0]
    sent = experts_sum.step((back_sum.step(grad_mixed_own), grad_mixed))

    half_grads = []
    near_tied = tie(qkv_near, sent)
    for pair in range(OWN_HEADS // PAIR):
        half_grads.append(attend_back(pair, facts, near_tied, qkv_far, mixed, grad_mixed, logs))
        if pair == 0:
            out_send = tie(scatter_far(out_parts[2], out_parts[3]), half_grads[0])
            out_far_sum = swap(out_send, 2)
            sent = experts_sum.step(half_grads[-1])
            sent = (out_send, sent, back_sum.step(sent))
        else:
            sent = experts_sum.step(back_sum.step(half_grads[-1]))
        near_tied = tie(qkv_near, sent)

    weight_halves = [
        jnp.concatenate(
            [
                qkv_weight[:, c * OWN + p * PAIR * HEAD_DIM : c * OWN + (p + 1) * PAIR * HEAD_DIM]
                for c in range(3)
            ],
            axis=1,
        )
        for p in range(OWN_HEADS // PAIR)
    ]

    def first_grad(j, token):
        rows = slice(j * local_rows, (j + 1) * local_rows)
        total = dot_nt(half_grads[0][rows], tie(weight_halves[0], token))
        for g, w in zip(half_grads[1:], weight_halves[1:]):
            total = total + dot_nt(g[rows], w)
        return total.astype(bf16)

    first2, first3 = first_grad(2, sent), first_grad(3, sent)
    send_first = scatter_far(first2, first3)
    far_first = swap(send_first, 2)

    sent = send_first
    first_all = tie(jnp.concatenate([first_near, first_far], axis=0), sent)
    half_weights = [dot_tn(first_all, g).astype(bf16) for g in half_grads]
    out_far_sum = tie(out_far_sum, half_grads[-1])
    out_grad = scatter_near(out_parts[0], out_parts[1], out_far_sum).astype(bf16)
    wide = PAIR * HEAD_DIM
    part_rows = quarter_rows // 2
    by_owner = [h.reshape(N_SHARD, 2, QUARTERS, part_rows, 3 * wide) for h in half_weights]
    out_quarters = out_grad.reshape(2, QUARTERS, part_rows, D)

    def last_quarter(p):
        def quarter(i):
            pieces = [part(h[:, p], i) for h in by_owner]
            rows = [
                jnp.concatenate([g[:, :, c * wide : (c + 1) * wide] for g in pieces], axis=2)
                for c in range(3)
            ]
            whole = lax.dynamic_index_in_dim(out_quarters[p], i, 0, keepdims=False)
            rows += [whole[:, x * OWN : (x + 1) * OWN] for x in range(N_SHARD)]
            return jnp.concatenate([r.reshape(-1, OWN) for r in rows], axis=0)

        return quarter

    def middle_last(values):
        rest = 3 * N_SHARD * part_rows
        moving = [
            v[:rest].reshape(3, N_SHARD, part_rows, OWN).transpose(1, 0, 2, 3).reshape(N_SHARD, -1, OWN)
            for v in values
        ]
        moved = yield from middle_in(moving)
        return [
            jnp.concatenate(
                [m.reshape(N_SHARD, 3, part_rows, OWN).transpose(1, 0, 2, 3).reshape(rest, OWN), v[rest:]],
                axis=0,
            )
            for m, v in zip(moved, values)
        ]

    last_sum = Steps(rep_sum_steps([last_quarter(0), last_quarter(1)], n_rep, middle_last))
    sent = last_sum.sent
    first0, first1 = first_grad(0, sent), first_grad(1, sent)
    sent = experts_sum.step((first0, first1))
    sent = last_sum.step(sent)
    back_grad = place_experts(me, back_sum.finish(sent))
    sent = last_sum.step(back_grad)
    sent = experts_sum.step(sent)
    grad_first = scatter_near(first0, first1, tie(far_first, sent))
    first_in, normed_one, inverse_one = first_rows(tie(tokens, sent))
    grad_gain_one = jnp.sum(grad_first * normed_one, axis=0)
    grad_bias_one = jnp.sum(grad_first, axis=0)
    input_grad = grad_middle + norm_back(grad_first, normed_one, inverse_one, gain_one)

    by_expert = jnp.stack([(kept & ~is_late), (kept & is_late)]).astype(bf16)
    grad_back_shift = dot_nn(by_expert, grad_low)
    in_shift_grad = jnp.concatenate(
        [dot_nn(m.astype(bf16).reshape(1, -1), pre_all) for m in masks], axis=0
    )
    small = jnp.concatenate(
        [
            jnp.stack([grad_gain_one, grad_bias_one, grad_out_shift, grad_gain_two, grad_bias_two]),
            grad_back_shift,
            jnp.zeros((1, D), f32),
        ],
        axis=0,
    )
    small = small + swap(small, 1)
    small = small + swap(small, 2)
    small = lax.dynamic_slice_in_dim(small, me * shard_width, shard_width, axis=1)
    small = jnp.concatenate([small, in_shift_grad.reshape(-1, shard_width)], axis=0)
    sent = last_sum.step((input_grad, small))
    bit = 1
    while bit < n_rep:
        small = small + tie(rep_swap(small, bit, n_rep), sent)
        sent = small
        bit *= 2
    sent = last_sum.step(sent)
    in_grad = place_experts(me, experts_sum.finish(sent))
    in_shift_grad = small[8:].reshape(EXPERTS, inner)
    qkv_grad, out_grad = place_attention(me, last_sum.finish(in_grad), shard_width)
    return (
        final.astype(bf16),
        input_grad,
        small[0],
        small[1],
        qkv_grad,
        out_grad,
        small[2],
        small[3],
        small[4],
        in_grad,
        in_shift_grad,
        back_grad,
        small[5:7],
    )


def solution(mesh):
    in_specs = (
        P(("rep", "shard"), None),
        P(("rep", "shard")),
        P(),
        P("rep", None),
        P(("rep", "shard")),
        P(("rep", "shard"), None),
        P(("rep", "shard"), None),
        P("shard"),
        P("shard"),
        P("shard", None),
        P("shard", None),
        P("shard"),
        P("shard"),
        P("shard"),
        P(None, "shard", None),
        P(None, "shard"),
        P(None, "shard", None),
        P(None, "shard"),
    )
    out_specs = (
        P(("rep", "shard"), None),
        P(("rep", "shard"), None),
        P("shard"),
        P("shard"),
        P("shard", None),
        P("shard", None),
        P("shard"),
        P("shard"),
        P("shard"),
        P(None, "shard", None),
        P(None, "shard"),
        P(None, "shard", None),
        P(None, "shard"),
    )
    body = functools.partial(shards, mesh.shape["rep"])
    return jax.shard_map(body, mesh=mesh, in_specs=in_specs, out_specs=out_specs, check_vma=False)
```

```python
import functools

import jax
import jax.numpy as jnp
from jax import lax
from jax.experimental import pallas as pl
from jax.experimental.pallas import tpu as pltpu
from jax.sharding import PartitionSpec as P

D = 1024
HEADS = 16
HEAD_DIM = 64
EXPERTS = 2
PIECE_LEN = 256
CAP = 320
N_SHARD = 4
OWN_HEADS = HEADS // N_SHARD
OWN = OWN_HEADS * HEAD_DIM
PAIR = 2
CHUNKS = 1
TILE = 256
NEG = -1e30

epsilon = 1e-05
LIGHT = pl.CostEstimate(flops=2**20, bytes_accessed=2**16, transcendentals=0)
f32 = jnp.float32
bf16 = jnp.bfloat16


def layer_norm(tok_rows):
    row_mean = jnp.mean(tok_rows, axis=-1, keepdims=True)
    centred = tok_rows - row_mean
    variance = jnp.mean(centred * centred, axis=-1, keepdims=True)
    inverse = lax.rsqrt(variance + epsilon)
    return (centred * inverse, inverse)


def norm_back(upstream, normed, inverse, norm_gain):
    scaled = upstream * norm_gain
    first_mean = jnp.mean(scaled, axis=-1, keepdims=True)
    second_mean = jnp.mean(scaled * normed, axis=-1, keepdims=True)
    return inverse * (scaled - first_mean - normed * second_mean)


def dot_nn(a, b):
    return lax.dot_general(a, b, (((1,), (0,)), ((), ())), preferred_element_type=f32)


def dot_nt(a, b):
    return lax.dot_general(a, b, (((1,), (1,)), ((), ())), preferred_element_type=f32)


def dot_tn(a, b):
    return lax.dot_general(a, b, (((0,), (0,)), ((), ())), preferred_element_type=f32)


def tie(value, after):
    return lax.optimization_barrier((value, after))[0]


def swap(value, mask):
    return lax.ppermute(value, "shard", [(i, i ^ mask) for i in range(N_SHARD)])


def exchange_blocks(blocks):
    return (blocks[0], swap(blocks[1], 1), swap(blocks[2], 2), swap(blocks[3], 3))


def in_order(side, own, other):
    return jnp.where(side == 0, jnp.stack([own, other]), jnp.stack([other, own]))


def scatter_far(block_two, block_three):
    near = swap(block_three, 1)
    return (block_two.astype(f32) + near.astype(f32)).astype(bf16)


def scatter_near(block_zero, block_one, far):
    near = swap(block_one, 1)
    return block_zero.astype(f32) + near.astype(f32) + far.astype(f32)


def rep_swap(value, mask, count):
    return lax.ppermute(value, "rep", [(i, i ^ mask) for i in range(count)])


QUARTERS = 4
ORDERS = ((1, 2), (2, 1))


def added(value, other, token):
    return (value.astype(f32) + tie(other, token).astype(f32)).astype(bf16)


def rep_sum_steps(quarters, count, middle):
    place = lax.axis_index("rep") & (QUARTERS - 1)
    sent = [jnp.stack([q(place ^ a), q(place ^ a ^ b)]) for q, (a, b) in zip(quarters, ORDERS)]
    others = [rep_swap(v, a, count) for v, (a, b) in zip(sent, ORDERS)]
    token = yield sent
    stay = [added(q(place), other[0], token) for q, other in zip(quarters, others)]
    sent = [
        added(q(place ^ b), other[1], token)
        for q, other, (a, b) in zip(quarters, others, ORDERS)
    ]
    others = [rep_swap(v, b, count) for v, (a, b) in zip(sent, ORDERS)]
    token = yield sent
    values = [added(v, other, token) for v, other in zip(stay, others)]
    mask = QUARTERS
    while mask < count:
        both = jnp.stack(values)
        other = rep_swap(both, mask, count)
        token = yield both
        values = [added(v, other[p], token) for p, v in enumerate(values)]
        mask *= 2
    values = yield from middle(values)
    others = [rep_swap(v, b, count) for v, (a, b) in zip(values, ORDERS)]
    token = yield values
    others = [tie(other, token) for other in others]
    sent = [jnp.stack([v, other]) for v, other in zip(values, others)]
    lasts = [rep_swap(v, a, count) for v, (a, b) in zip(sent, ORDERS)]
    token = yield sent
    return [(v, other, tie(last, token)) for v, other, last in zip(values, others, lasts)]


def rep_places():
    place = lax.axis_index("rep").astype(jnp.int32) & (QUARTERS - 1)
    return jnp.stack([place ^ mask for a, b in ORDERS for mask in (0, b, a, a ^ b)])


def middle_none(values):
    yield from ()
    return values


class Steps:
    def __init__(self, steps):
        self.steps = steps
        self.result = None
        self.sent = next(steps)

    def step(self, token):
        if self.result is not None:
            return token
        try:
            self.sent = self.steps.send(token)
        except StopIteration as end:
            self.result = end.value
            return token
        return self.sent

    def finish(self, token):
        while self.result is None:
            self.step(token)
        return self.result


def project_kernel(facts, tok_a, tok_b, w0, w1, w2, w3, first, qkv, weight, params, gains):
    me = facts[0]
    part, columns = weight.shape[0] // N_SHARD, weight.shape[1]
    for j, block in enumerate((w0, w1, w2, w3)):
        at = (me ^ j) * part
        weight[pl.ds(pl.multiple_of(at, part), part), :] = block[0:part, :]
        gains[:, pl.ds(pl.multiple_of(at, part), part)] = block[part : part + 8, 0:part].astype(f32)
    params[...] = gains[...]
    for half, tok in enumerate((tok_a, tok_b)):
        for start in range(0, tok.shape[0], TILE):
            normed = layer_norm(tok[start : start + TILE, :].astype(f32))[0]
            low = (normed * gains[0:1, :] + gains[1:2, :]).astype(bf16)
            rows = slice(half * tok.shape[0] + start, half * tok.shape[0] + start + TILE)
            first[rows, :] = low
            qkv[rows, :] = dot_nn(low, weight[...]).astype(bf16)


def project(facts, tok_a, tok_b, blocks):
    rows, width = tok_a.shape
    columns = blocks[0].shape[1]
    vmem = pl.BlockSpec(memory_space=pltpu.VMEM)
    return pl.pallas_call(
        project_kernel,
        out_shape=(
            jax.ShapeDtypeStruct((2 * rows, width), bf16),
            jax.ShapeDtypeStruct((2 * rows, columns), bf16),
            jax.ShapeDtypeStruct((width, columns), bf16),
            jax.ShapeDtypeStruct((8, width), f32),
        ),
        in_specs=[pl.BlockSpec(memory_space=pltpu.SMEM)] + [vmem] * 6,
        out_specs=(vmem,) * 4,
        scratch_shapes=[pltpu.VMEM((8, width), f32)],
        compiler_params=pltpu.CompilerParams(vmem_limit_bytes=32 * 2**20),
        cost_estimate=LIGHT,
        name="project",
    )(facts, tok_a, tok_b, *blocks)


def visible_tile(key_start, query_start, keys, queries, starts):
    key_pos = key_start + lax.broadcasted_iota(jnp.int32, (keys, queries), 0)
    query_pos = query_start + lax.broadcasted_iota(jnp.int32, (keys, queries), 1)
    seen = key_pos <= query_pos
    low = jnp.minimum(key_pos, query_pos)
    high = jnp.maximum(key_pos, query_pos)
    for start in starts:
        seen = seen | ((low >= start) & (high < start + PIECE_LEN))
    return seen


def crosses(boundary, starts):
    met = jnp.bool_(False)
    for start in starts:
        met = met | ((start < boundary) & (start + PIECE_LEN > boundary))
    return met


def head_lanes(rows):
    return lax.broadcasted_iota(jnp.int32, (rows, OWN), 1) // HEAD_DIM


WIDE = 2 * TILE


def attend_kernel(blocks, facts, near, far, mixed, logs, q_own, k_own, v_turned, acc, top, total):
    me = facts[0]
    starts = [facts[1 + i] for i in range(facts.shape[0] - 1)]
    for j in range(N_SHARD):
        src = near if j < 2 else far
        rows = slice((j % 2) * WIDE, (j % 2 + 1) * WIDE)
        at = me ^ j
        q_own[at] = src[rows, 0:OWN] * jnp.asarray(HEAD_DIM**-0.5, bf16)
        k_own[at] = src[rows, OWN : 2 * OWN]
        v_turned[at] = src[rows, 2 * OWN : 3 * OWN].astype(f32).T.astype(bf16)
    lanes = head_lanes(WIDE)

    def query_block(i, unused):
        q_i = q_own[i]
        q_heads = [jnp.where(lanes == h, q_i, jnp.zeros_like(q_i)) for h in range(OWN_HEADS)]
        acc[...] = jnp.zeros_like(acc)
        top[...] = jnp.full_like(top, NEG)
        total[...] = jnp.zeros_like(total)

        def key_pair(p, masked):
            k_p = k_own[p]
            v_p = v_turned[p]
            seen = visible_tile(p * WIDE, i * WIDE, WIDE, WIDE, starts) if masked else None
            for h in range(OWN_HEADS):
                scores = dot_nt(k_p, q_heads[h])
                if masked:
                    scores = jnp.where(seen, scores, NEG)
                old_top = top[h : h + 1, :]
                new_top = jnp.maximum(old_top, jnp.max(scores, axis=0, keepdims=True))
                raised = jnp.exp(scores - new_top)
                fade = jnp.exp(old_top - new_top)
                top[h : h + 1, :] = new_top
                total[h : h + 1, :] = total[h : h + 1, :] * fade + jnp.sum(
                    raised, axis=0, keepdims=True
                )
                rows = slice(h * HEAD_DIM, (h + 1) * HEAD_DIM)
                acc[rows, :] = acc[rows, :] * fade + dot_nn(v_p[rows, :], raised.astype(bf16))

        def plain(p, unused):
            key_pair(p, False)
            return unused

        def edge(p, unused):
            key_pair(p, True)
            return unused

        lax.fori_loop(0, i, plain, 0)
        more = (i + 1 < blocks // 2) & crosses((i + 1) * WIDE, starts)
        lax.fori_loop(i, i + 1 + more.astype(jnp.int32), edge, 0)

        for h in range(OWN_HEADS):
            rows = slice(h * HEAD_DIM, (h + 1) * HEAD_DIM)
            acc[rows, :] = acc[rows, :] / total[h : h + 1, :]
        mixed[pl.ds(pl.multiple_of((i ^ me) * WIDE, WIDE), WIDE), :] = acc[...].T.astype(bf16)
        logs[i] = top[...] + jnp.log(jnp.maximum(total[...], 1e-30))
        return unused

    lax.fori_loop(0, blocks // 2, query_block, 0)


def attend(facts, near, far):
    rows = near.shape[0] + far.shape[0]
    blocks = rows // TILE
    vmem = pl.BlockSpec(memory_space=pltpu.VMEM)
    return pl.pallas_call(
        functools.partial(attend_kernel, blocks),
        out_shape=(
            jax.ShapeDtypeStruct((rows, OWN), bf16),
            jax.ShapeDtypeStruct((blocks // 2, 8, WIDE), f32),
        ),
        in_specs=[pl.BlockSpec(memory_space=pltpu.SMEM), vmem, vmem],
        out_specs=(vmem, vmem),
        scratch_shapes=[
            pltpu.VMEM((blocks // 2, WIDE, OWN), bf16),
            pltpu.VMEM((blocks // 2, WIDE, OWN), bf16),
            pltpu.VMEM((blocks // 2, OWN, WIDE), bf16),
            pltpu.VMEM((OWN, WIDE), f32),
            pltpu.VMEM((8, WIDE), f32),
            pltpu.VMEM((8, WIDE), f32),
        ],
        compiler_params=pltpu.CompilerParams(vmem_limit_bytes=48 * 2**20),
        cost_estimate=LIGHT,
        name="attend",
    )(facts, near, far)


def attend_back_kernel(
    blocks, pair, facts, near, far, mixed, g0, g1, g2, g3, logs, grads,
    q_own, k_own, v_own, k_turned, g_own, q_heads, g_heads, deltas, q_grad, k_grad, v_grad, k_heads, v_heads,
):
    me = facts[0]
    starts = [facts[1 + i] for i in range(facts.shape[0] - 1)]
    wide = PAIR * HEAD_DIM
    lane = pair * wide
    lanes = lax.broadcasted_iota(jnp.int32, (TILE, wide), 1) // HEAD_DIM
    pick = (
        lax.broadcasted_iota(jnp.int32, (8, wide), 1) // HEAD_DIM
        == lax.broadcasted_iota(jnp.int32, (8, wide), 0)
    ).astype(f32)
    for j in range(N_SHARD):
        src = near if j < 2 else far
        grad_src = (g0, g1, g2, g3)[j]
        at = me ^ j
        for half in range(2):
            base = (j % 2) * WIDE + half * TILE
            rows = slice(base, base + TILE)
            to = slice(half * TILE, (half + 1) * TILE)
            q_tile = src[rows, lane : lane + wide] * jnp.asarray(HEAD_DIM**-0.5, bf16)
            k_tile = src[rows, OWN + lane : OWN + lane + wide]
            g_tile = grad_src[to, lane : lane + wide]
            o_tile = mixed[j * WIDE + half * TILE : j * WIDE + (half + 1) * TILE, lane : lane + wide]
            q_own[at, to, :] = q_tile
            k_own[at, to, :] = k_tile
            v_own[at, to, :] = src[rows, 2 * OWN + lane : 2 * OWN + lane + wide]
            k_turned[at, :, to] = k_tile.astype(f32).T.astype(bf16)
            g_own[at, to, :] = g_tile
            for h in range(PAIR):
                place = slice(h * WIDE + half * TILE, h * WIDE + (half + 1) * TILE)
                q_heads[at, place, :] = jnp.where(lanes == h, q_tile, jnp.zeros_like(q_tile))
                g_heads[at, place, :] = jnp.where(lanes == h, g_tile, jnp.zeros_like(g_tile))
            both = g_tile.astype(f32) * o_tile.astype(f32)
            deltas[at, :, to] = lax.dot_general(
                pick, both, (((1,), (1,)), ((), ())),
                precision=lax.Precision.HIGHEST, preferred_element_type=f32,
            )
    q_grad[...] = jnp.zeros_like(q_grad)
    wide_lanes = lax.broadcasted_iota(jnp.int32, (WIDE, wide), 1) // HEAD_DIM

    def key_block(j, unused):
        k_j = k_own[j]
        v_j = v_own[j]
        for h in range(PAIR):
            rows = slice(h * WIDE, (h + 1) * WIDE)
            k_heads[rows, :] = jnp.where(wide_lanes == h, k_j, jnp.zeros_like(k_j))
            v_heads[rows, :] = jnp.where(wide_lanes == h, v_j, jnp.zeros_like(v_j))
        k_grad[...] = jnp.zeros_like(k_grad)
        v_grad[...] = jnp.zeros_like(v_grad)

        def query_pair(p, masked):
            q_p = q_own[p]
            g_p = g_own[p]
            kt = k_turned[j]
            seen = visible_tile(j * WIDE, p * WIDE, WIDE, WIDE, starts) if masked else None
            softs = []
            scored = []
            for h in range(PAIR):
                rows = slice(h * WIDE, (h + 1) * WIDE)
                at = pair * PAIR + h
                scores = dot_nt(k_heads[rows, :], q_p)
                soft = jnp.exp(scores - logs[p, at : at + 1, :])
                if masked:
                    soft = jnp.where(seen, soft, 0.0)
                grad_soft = dot_nt(v_heads[rows, :], g_p)
                grad_scores = (soft * (grad_soft - deltas[p, h : h + 1, :])).astype(bf16)
                softs.append(soft.astype(bf16))
                scored.append(grad_scores)
                head = slice(h * HEAD_DIM, (h + 1) * HEAD_DIM)
                q_grad[p, head, :] += dot_nn(kt[head, :], grad_scores)
            v_grad[...] += dot_nn(jnp.concatenate(softs, axis=1), g_heads[p])
            k_grad[...] += dot_nn(jnp.concatenate(scored, axis=1), q_heads[p])

        def plain(p, unused):
            query_pair(p, False)
            return unused

        def edge(p, unused):
            query_pair(p, True)
            return unused

        less = (j > 0) & crosses(j * WIDE, starts)
        lax.fori_loop(j - less.astype(jnp.int32), j + 1, edge, 0)
        lax.fori_loop(j + 1, blocks // 2, plain, 0)
        place = pl.multiple_of((j ^ me) * WIDE, WIDE)
        grads[pl.ds(place, WIDE), wide : 2 * wide] = k_grad[...].astype(bf16)
        grads[pl.ds(place, WIDE), 2 * wide : 3 * wide] = v_grad[...].astype(bf16)
        return unused

    lax.fori_loop(0, blocks // 2, key_block, 0)

    def write_query(p, unused):
        place = pl.multiple_of((p ^ me) * WIDE, WIDE)
        grads[pl.ds(place, WIDE), 0:wide] = (q_grad[p] * HEAD_DIM**-0.5).T.astype(bf16)
        return unused

    lax.fori_loop(0, blocks // 2, write_query, 0)


def attend_back(pair, facts, near, far, mixed, grad_blocks, logs):
    rows = near.shape[0] + far.shape[0]
    blocks = rows // TILE
    wide = PAIR * HEAD_DIM
    vmem = pl.BlockSpec(memory_space=pltpu.VMEM)
    tile = lambda n, m, kind: pltpu.VMEM((n, m), kind)
    double = lambda n, m, kind: pltpu.VMEM((blocks // 2, n, m), kind)
    return pl.pallas_call(
        functools.partial(attend_back_kernel, blocks, pair),
        out_shape=jax.ShapeDtypeStruct((rows, 3 * wide), bf16),
        in_specs=[pl.BlockSpec(memory_space=pltpu.SMEM)] + [vmem] * 8,
        out_specs=vmem,
        scratch_shapes=[
            double(WIDE, wide, bf16),
            double(WIDE, wide, bf16),
            double(WIDE, wide, bf16),
            double(wide, WIDE, bf16),
            double(WIDE, wide, bf16),
            double(PAIR * WIDE, wide, bf16),
            double(PAIR * WIDE, wide, bf16),
            double(8, WIDE, f32),
            double(wide, WIDE, f32),
            tile(WIDE, wide, f32),
            tile(WIDE, wide, f32),
            tile(PAIR * WIDE, wide, bf16),
            tile(PAIR * WIDE, wide, bf16),
        ],
        compiler_params=pltpu.CompilerParams(vmem_limit_bytes=48 * 2**20),
        cost_estimate=LIGHT,
        name="attend_back",
    )(facts, near, far, mixed, *grad_blocks, logs)


def expert_tile(counts, step, tiles):
    block = step // tiles
    start = (step % tiles) * TILE
    border = counts[block, 0] - start
    late = lax.broadcasted_iota(jnp.int32, (TILE, 1), 0) >= border
    return border, late


def take_rows(step, tiles, rows_a, rows_b, taken):
    @pl.when(step < tiles)
    def _():
        taken[...] = rows_a[...]

    @pl.when(step >= tiles)
    def _():
        taken[...] = rows_b[...]


def give_rows(step, tiles, given, out_a, out_b):
    @pl.when(step < tiles)
    def _():
        out_a[...] = given[...]

    @pl.when(step >= tiles)
    def _():
        out_b[...] = given[...]


def by_expert_rows(border, late, work, out):
    @pl.when(border > 0)
    def _():
        out[...] = work(0)

    @pl.when(border < TILE)
    def _():
        out[...] = jnp.where(late, work(1), out[...])


def expert_kernel(tiles, counts, rows_a, rows_b, w_in, in_bias, w_back, hidden, out_a, out_b, taken, given):
    step = pl.program_id(0)
    border, late = expert_tile(counts, step, tiles)
    take_rows(step, tiles, rows_a, rows_b, taken)
    by_expert_rows(
        border,
        late,
        lambda e: jnp.maximum(dot_nn(taken[...], w_in[e]) + in_bias[e : e + 1, :], 0.0).astype(bf16),
        hidden,
    )
    by_expert_rows(border, late, lambda e: dot_nn(hidden[...], w_back[e]).astype(bf16), given)
    give_rows(step, tiles, given, out_a, out_b)


def expert_back_kernel(tiles, counts, rows_a, rows_b, hidden, w_in, w_back, grad_pre, out_a, out_b, taken, given):
    step = pl.program_id(0)
    border, late = expert_tile(counts, step, tiles)
    take_rows(step, tiles, rows_a, rows_b, taken)
    by_expert_rows(
        border,
        late,
        lambda e: jnp.where(hidden[...] > 0, dot_nt(taken[...], w_back[e]), 0.0).astype(bf16),
        grad_pre,
    )
    by_expert_rows(border, late, lambda e: dot_nt(grad_pre[...], w_in[e]).astype(bf16), given)
    give_rows(step, tiles, given, out_a, out_b)


def expert_specs(rows, width, inner):
    tiles = rows // TILE
    first = pl.BlockSpec((TILE, width), lambda i, c: (jnp.minimum(i, tiles - 1), 0))
    second = pl.BlockSpec((TILE, width), lambda i, c: (jnp.maximum(i - tiles, 0), 0))
    both = pl.BlockSpec((TILE, inner), lambda i, c: (i, 0))
    once = pl.Buffered(1)
    w_in = pl.BlockSpec((EXPERTS, width, inner), lambda i, c: (0, 0, 0), pipeline_mode=once)
    w_back = pl.BlockSpec((EXPERTS, inner, width), lambda i, c: (0, 0, 0), pipeline_mode=once)
    bias = pl.BlockSpec((EXPERTS, inner), lambda i, c: (0, 0), pipeline_mode=once)
    return tiles, first, second, both, w_in, w_back, bias


def run_experts(counts, rows_a, rows_b, w_in, in_bias, w_back):
    rows, width = rows_a.shape
    inner = w_in.shape[2]
    tiles, first, second, both, in_spec, back_spec, bias_spec = expert_specs(rows, width, inner)
    return pl.pallas_call(
        functools.partial(expert_kernel, tiles),
        grid_spec=pltpu.PrefetchScalarGridSpec(
            num_scalar_prefetch=1,
            grid=(2 * tiles,),
            in_specs=[first, second, in_spec, bias_spec, back_spec],
            out_specs=[both, first, second],
            scratch_shapes=[pltpu.VMEM((TILE, width), bf16)] * 2,
        ),
        out_shape=(
            jax.ShapeDtypeStruct((2 * rows, inner), bf16),
            jax.ShapeDtypeStruct((rows, width), bf16),
            jax.ShapeDtypeStruct((rows, width), bf16),
        ),
        compiler_params=pltpu.CompilerParams(vmem_limit_bytes=40 * 2**20),
        cost_estimate=LIGHT,
        name="experts",
    )(counts, rows_a, rows_b, w_in, in_bias, w_back)


def run_experts_back(counts, rows_a, rows_b, hidden, w_in, w_back):
    rows, width = rows_a.shape
    inner = w_in.shape[2]
    tiles, first, second, both, in_spec, back_spec, bias_spec = expert_specs(rows, width, inner)
    return pl.pallas_call(
        functools.partial(expert_back_kernel, tiles),
        grid_spec=pltpu.PrefetchScalarGridSpec(
            num_scalar_prefetch=1,
            grid=(2 * tiles,),
            in_specs=[first, second, both, in_spec, back_spec],
            out_specs=[both, first, second],
            scratch_shapes=[pltpu.VMEM((TILE, width), bf16)] * 2,
        ),
        out_shape=(
            jax.ShapeDtypeStruct((2 * rows, inner), bf16),
            jax.ShapeDtypeStruct((rows, width), bf16),
            jax.ShapeDtypeStruct((rows, width), bf16),
        ),
        compiler_params=pltpu.CompilerParams(vmem_limit_bytes=40 * 2**20),
        cost_estimate=LIGHT,
        name="experts_back",
    )(counts, rows_a, rows_b, hidden, w_in, w_back)


def place_experts_kernel(facts, *refs):
    blocks, out = refs[:6], refs[6]
    expert, turn = pl.program_id(0), pl.program_id(1)

    def write(block):
        owners, rows, width = block.shape[-3:]
        for j in range(owners):
            at = pl.multiple_of((facts[0] ^ j) * width, width) if owners > 1 else 0
            out[0, :, pl.ds(at, width)] = (block[0, j] if len(block.shape) == 4 else block[j]).astype(f32)

    for part in range(2):
        for source, block in enumerate(blocks[3 * part : 3 * part + 3]):

            @pl.when((expert == part) & (jnp.minimum(turn, 2) == source))
            def _():
                write(block)


def place_experts(me, parts):
    owners, rows, width = parts[0][0].shape
    whole = pl.BlockSpec((owners, rows, width), lambda e, t, s: (0, 0, 0))

    def last(part):
        return pl.BlockSpec(
            (1, owners, rows, width),
            lambda e, t, s: (jnp.clip((e - part) * QUARTERS + t - 2, 0, 1), 0, 0, 0),
        )

    return pl.pallas_call(
        place_experts_kernel,
        grid_spec=pltpu.PrefetchScalarGridSpec(
            num_scalar_prefetch=1,
            grid=(2, QUARTERS),
            in_specs=[whole, whole, last(0), whole, whole, last(1)],
            out_specs=pl.BlockSpec(
                (1, rows, owners * width), lambda e, t, s: (e, s[1 + e * QUARTERS + t], 0)
            ),
        ),
        out_shape=jax.ShapeDtypeStruct((2, QUARTERS * rows, owners * width), f32),
        compiler_params=pltpu.CompilerParams(vmem_limit_bytes=24 * 2**20),
        cost_estimate=LIGHT,
        name="place_experts",
    )(jnp.concatenate([me[None], rep_places()]), *[b for p in parts for b in p])


def place_attention_kernel(facts, *refs):
    blocks, qkv_out, whole_out = refs[:6], refs[6], refs[7]
    rows = qkv_out.shape[0] // (2 * QUARTERS)
    for part in range(2):
        own, second, last = blocks[3 * part : 3 * part + 3]
        for turn in range(QUARTERS):
            block = (own, second, last.at[0], last.at[1])[turn]
            segment = part * QUARTERS + facts[1 + part * QUARTERS + turn]
            to = pl.ds(pl.multiple_of(segment * rows, rows), rows)
            for c in range(3):
                for j in range(N_SHARD):
                    at = pl.multiple_of(c * N_SHARD * OWN + (facts[0] ^ j) * OWN, OWN)
                    start = (c * N_SHARD + j) * rows
                    qkv_out[to, pl.ds(at, OWN)] = block[start : start + rows, :].astype(f32)
            for x in range(N_SHARD):
                start = (3 * N_SHARD + x) * rows
                whole_out[to, x * OWN : (x + 1) * OWN] = block[start : start + rows, :].astype(f32)


def place_attention(me, parts, rows):
    vmem = pl.BlockSpec(memory_space=pltpu.VMEM)
    return pl.pallas_call(
        place_attention_kernel,
        out_shape=(
            jax.ShapeDtypeStruct((rows, 3 * N_SHARD * OWN), f32),
            jax.ShapeDtypeStruct((rows, N_SHARD * OWN), f32),
        ),
        in_specs=[pl.BlockSpec(memory_space=pltpu.SMEM)] + [vmem] * 6,
        out_specs=(vmem, vmem),
        compiler_params=pltpu.CompilerParams(vmem_limit_bytes=24 * 2**20),
        cost_estimate=LIGHT,
        name="place_attention",
    )(jnp.concatenate([me[None], rep_places()]), *[b for p in parts for b in p])


def shards(
    n_rep,
    tokens,
    token_ids,
    hash_table,
    piece_starts,
    valid_mask,
    teacher,
    cotangent,
    ln1_gain,
    ln1_bias,
    w_qkv,
    w_out,
    out_bias,
    ln2_gain,
    ln2_bias,
    w_in,
    in_bias,
    w_back,
    back_bias,
):
    local_rows = tokens.shape[0]
    tokens_all = local_rows * N_SHARD * n_rep
    me = lax.axis_index("shard").astype(jnp.int32)
    rep_at = lax.axis_index("rep")
    inner = w_back.shape[1]
    shard_width = ln1_gain.shape[0]
    seg_rows = shard_width // n_rep
    facts = jnp.concatenate([me[None], piece_starts[0]])

    expert_of = jnp.take(hash_table, token_ids)
    places = jnp.arange(local_rows, dtype=jnp.int32)
    earlier = (expert_of[:, None] == expert_of[None, :]) & (places[None, :] < places[:, None])
    slot_of = jnp.sum(earlier.astype(jnp.int32), axis=1)
    kept = slot_of < CAP
    is_late = expert_of > 0
    early_count = jnp.minimum(local_rows - jnp.sum(is_late.astype(jnp.int32)), CAP)
    sorted_at = jnp.where(kept, slot_of + jnp.where(is_late, early_count, 0), -1)
    sorter = (sorted_at[None, :] == places[:, None]).astype(bf16)
    counted = valid_mask.astype(f32)
    own_facts = jnp.stack([early_count.astype(f32), jnp.sum(valid_mask).astype(f32)])

    packed = jnp.concatenate(
        [
            jnp.stack([ln1_gain, ln1_bias, out_bias, ln2_gain, ln2_bias]),
            back_bias,
            jnp.zeros((1, shard_width), bf16),
        ],
        axis=0,
    )
    packed = jnp.concatenate([packed, jnp.zeros((8, 3 * OWN - shard_width), bf16)], axis=1)
    qkv_sends = [
            jnp.concatenate(
                [
                    jnp.concatenate(
                        [
                            lax.dynamic_slice_in_dim(w_qkv, c * D + (me ^ j) * OWN, OWN, axis=1)
                            for c in range(3)
                        ],
                        axis=1,
                    ),
                    packed,
                ],
                axis=0,
            )
            for j in range(N_SHARD)
    ]
    over = swap(jnp.stack(qkv_sends[2:]), 3)
    tok_far = swap(tokens, 2)
    thin = lax.dynamic_slice_in_dim(w_in, rep_at * seg_rows, seg_rows, axis=1)
    thin_sends = [lax.dynamic_slice_in_dim(thin, (me ^ j) * inner, inner, axis=2) for j in range(N_SHARD)]
    over = tie(over, thin_sends)
    near = swap(qkv_sends[1], 1)
    tok_near = swap(tokens, 1)
    tok_both = swap(tok_far, 1)
    qkv_blocks = (qkv_sends[0], near, swap(over[0], 1), over[1])
    thin_blocks = exchange_blocks(tie(thin_sends, (tok_both, qkv_blocks[2])))

    first_near, qkv_near, qkv_weight, rows_of = project(
        tie(facts, (tok_both, own_facts, sorter)), tokens, tok_near, qkv_blocks
    )
    gain_one, bias_one, out_shift, gain_two, bias_two = [rows_of[i] for i in range(5)]
    back_shift = rows_of[5:7]
    first_far, qkv_far = project(facts, tie(tok_far, qkv_near), tok_both, qkv_blocks)[:2]

    def first_rows(block):
        normed, inverse = layer_norm(block.astype(f32))
        return (normed * gain_one + bias_one).astype(bf16), normed, inverse

    thin_blocks = tie(thin_blocks, qkv_near)
    thin = in_order(
        me >> 1,
        in_order(me & 1, thin_blocks[0], thin_blocks[1]),
        in_order(me & 1, thin_blocks[2], thin_blocks[3]),
    ).reshape(N_SHARD, EXPERTS, seg_rows, inner)
    thin = lax.all_gather(thin.transpose(1, 0, 2, 3), "rep", axis=0)
    in_weight = thin.transpose(1, 2, 0, 3, 4).reshape(EXPERTS, D, inner)
    w_out = tie(w_out, tok_far)
    out_far = swap(w_out, 2)

    own_facts = jnp.broadcast_to(tie(own_facts, qkv_far)[:, None], (2, 128))
    shared = jnp.stack(exchange_blocks([own_facts] * N_SHARD))
    borders = shared[:, 0, 0].astype(jnp.int32)
    counts_near = borders[:2, None]
    chunk = local_rows // CHUNKS
    counts_far = [borders[2:, None] - h * chunk for h in range(CHUNKS)]

    mixed, logs = attend(facts, qkv_near, qkv_far)
    count_all = jnp.sum(shared[:, 1], axis=0, keepdims=True)
    for bit in range(n_rep.bit_length() - 1):
        count_all = count_all + rep_swap(count_all, 1 << bit, n_rep)
    count_all = count_all[0, 0]
    out_far = tie(out_far, mixed)
    out_blocks = (w_out, swap(w_out, 1), out_far, swap(out_far, 1))
    mixed_blocks = exchange_blocks(
        [mixed[j * local_rows : (j + 1) * local_rows] for j in range(N_SHARD)]
    )
    mixed_blocks = mixed_blocks[:2] + lax.optimization_barrier(mixed_blocks[2:] + (borders,))[:2]
    tok_rows = tokens.astype(f32)
    branch = dot_nn(mixed_blocks[0], out_blocks[0])
    for j in range(1, N_SHARD):
        branch = branch + dot_nn(mixed_blocks[j], out_blocks[j])
    middle = tok_rows + branch + out_shift
    normed_two, inverse_two = layer_norm(middle)
    second_in = (normed_two * gain_two + bias_two).astype(bf16)
    sorted_in = dot_nn(sorter, second_in).astype(bf16)
    half_of = lambda value, h: value[h * chunk : (h + 1) * chunk]
    in_far = [swap(half_of(sorted_in, h), 2) for h in range(CHUNKS)]
    in_near = swap(sorted_in, 1)
    bias_in = in_bias.astype(f32)
    hidden_near, out0, out1 = run_experts(counts_near, sorted_in, in_near, in_weight, bias_in, w_back)
    token = out0
    in_both, hidden_far, far_sums = [], [], []
    for h in range(CHUNKS):
        in_far[h] = tie(in_far[h], token)
        in_both.append(swap(in_far[h], 1))
        hidden, out2, out3 = run_experts(
            counts_far[h], in_far[h], in_both[h], in_weight, bias_in, w_back
        )
        hidden_far.append(hidden)
        token = scatter_far(out2, out3)
        far_sums.append(swap(token, 2))
    summed = scatter_near(out0, out1, jnp.concatenate(far_sums, axis=0))
    picked = dot_tn(sorter, summed.astype(bf16))
    picked = picked + jnp.where(is_late[:, None], back_shift[1], back_shift[0])
    final = middle + jnp.where(kept[:, None], picked, 0.0)
    grad_final = cotangent.astype(f32) + tokens_all / (2.0 * count_all) * counted[:, None] * (
        final - teacher.astype(f32)
    )
    grad_low = grad_final.astype(bf16)

    sorted_grad = dot_nn(sorter, grad_low).astype(bf16)
    grad_far = [swap(half_of(sorted_grad, h), 2) for h in range(CHUNKS)]
    grad_near = swap(sorted_grad, 1)
    pre_near, gin0, gin1 = run_experts_back(
        counts_near, sorted_grad, grad_near, hidden_near, in_weight, w_back
    )
    token = gin0
    grad_both, pre_far, far_second = [], [], []
    for h in range(CHUNKS):
        grad_far[h] = tie(grad_far[h], token)
        grad_both.append(swap(grad_far[h], 1))
        pre, gin2, gin3 = run_experts_back(
            counts_far[h], grad_far[h], grad_both[h], hidden_far[h], in_weight, w_back
        )
        pre_far.append(pre)
        token = scatter_far(gin2, gin3)
        far_second.append(swap(token, 2))
    send_second = token

    bounds = tie(borders, send_second)
    tile_rows = jnp.arange(TILE, dtype=jnp.int32)
    starts = range(0, chunk, TILE)
    tiles = [bounds[j] - h for j in range(2) for h in range(0, local_rows, TILE)]
    tiles += [
        bounds[j] - h * chunk - start for h in range(CHUNKS) for j in range(2, N_SHARD) for start in starts
    ]
    early = jnp.concatenate([tile_rows < bound for bound in tiles])
    masks = [early[:, None], ~early[:, None]]
    in_tile_order = lambda own, near, far, both: jnp.concatenate(
        [own, near] + [half for pair in zip(far, both) for half in pair], axis=0
    )
    hidden_all = jnp.concatenate([hidden_near] + hidden_far, axis=0)
    grad_all = in_tile_order(sorted_grad, grad_near, grad_far, grad_both)
    back_grads = [dot_tn(jnp.where(masks[0], hidden_all, 0), grad_all).astype(bf16)]
    back_grads.append(dot_tn(jnp.where(masks[1], hidden_all, 0), grad_all).astype(bf16))
    back_rows = EXPERTS * inner
    part = lambda a, i: lax.dynamic_index_in_dim(a, i, 1, keepdims=False)
    quarter_of = lambda a: lambda i: part(a, i)
    back_parts = [g.reshape(1, QUARTERS, inner // QUARTERS, D) for g in back_grads]
    back_sum = Steps(rep_sum_steps([quarter_of(g) for g in back_parts], n_rep, middle_none))
    pre_all = tie(jnp.concatenate([pre_near] + pre_far, axis=0), back_sum.sent)
    in_all = in_tile_order(sorted_in, in_near, in_far, in_both)
    in_grads = [dot_tn(in_all, jnp.where(m, pre_all, 0)).astype(bf16) for m in masks]
    quarter_rows = shard_width // QUARTERS
    in_parts = [g.reshape(N_SHARD, QUARTERS, quarter_rows, inner) for g in in_grads]

    def middle_in(values):
        blocks = [
            jnp.concatenate(
                [lax.dynamic_index_in_dim(v, me ^ j, 0, keepdims=False) for v in values], axis=0
            )
            for j in range(N_SHARD)
        ]
        moved = exchange_blocks(blocks)
        token = yield blocks
        moved = jnp.stack([tie(m, token) for m in moved])
        rows = values[0].shape[1]
        return [moved[:, p * rows : (p + 1) * rows] for p in range(len(values))]

    experts_sum = Steps(rep_sum_steps([quarter_of(g) for g in in_parts], n_rep, middle_in))

    far_second = tie(far_second, back_sum.step(experts_sum.sent))
    summed_grad = scatter_near(gin0, gin1, jnp.concatenate(far_second, axis=0))
    grad_second = dot_tn(sorter, summed_grad.astype(bf16))
    grad_gain_two = jnp.sum(grad_second * normed_two, axis=0)
    grad_bias_two = jnp.sum(grad_second, axis=0)
    grad_middle = grad_final + norm_back(grad_second, normed_two, inverse_two, gain_two)
    grad_branch = grad_middle.astype(bf16)
    grad_out_shift = jnp.sum(grad_branch.astype(f32), axis=0)
    grad_mixed_own = [dot_nt(grad_branch, w).astype(bf16) for w in out_blocks]
    grad_mixed = exchange_blocks(grad_mixed_own)
    out_parts = [dot_tn(b, tie(grad_branch, grad_mixed_own)).astype(bf16) for b in mixed_blocks]
    grad_mixed = lax.optimization_barrier((grad_mixed, out_parts))[0]
    sent = experts_sum.step((back_sum.step(grad_mixed_own), grad_mixed))

    half_grads = []
    near_tied = tie(qkv_near, sent)
    for pair in range(OWN_HEADS // PAIR):
        half_grads.append(attend_back(pair, facts, near_tied, qkv_far, mixed, grad_mixed, logs))
        if pair == 0:
            out_send = tie(scatter_far(out_parts[2], out_parts[3]), half_grads[0])
            out_far_sum = swap(out_send, 2)
            sent = experts_sum.step(half_grads[-1])
            sent = (out_send, sent, back_sum.step(sent))
        else:
            sent = experts_sum.step(back_sum.step(half_grads[-1]))
        near_tied = tie(qkv_near, sent)

    weight_halves = [
        jnp.concatenate(
            [
                qkv_weight[:, c * OWN + p * PAIR * HEAD_DIM : c * OWN + (p + 1) * PAIR * HEAD_DIM]
                for c in range(3)
            ],
            axis=1,
        )
        for p in range(OWN_HEADS // PAIR)
    ]

    def first_grad(j, token):
        rows = slice(j * local_rows, (j + 1) * local_rows)
        total = dot_nt(half_grads[0][rows], tie(weight_halves[0], token))
        for g, w in zip(half_grads[1:], weight_halves[1:]):
            total = total + dot_nt(g[rows], w)
        return total.astype(bf16)

    first2, first3 = first_grad(2, sent), first_grad(3, sent)
    send_first = scatter_far(first2, first3)
    far_first = swap(send_first, 2)

    sent = send_first
    first_all = tie(jnp.concatenate([first_near, first_far], axis=0), sent)
    half_weights = [dot_tn(first_all, g).astype(bf16) for g in half_grads]
    out_far_sum = tie(out_far_sum, half_grads[-1])
    out_grad = scatter_near(out_parts[0], out_parts[1], out_far_sum).astype(bf16)
    wide = PAIR * HEAD_DIM
    part_rows = quarter_rows // 2
    by_owner = [h.reshape(N_SHARD, 2, QUARTERS, part_rows, 3 * wide) for h in half_weights]
    out_quarters = out_grad.reshape(2, QUARTERS, part_rows, D)

    def last_quarter(p):
        def quarter(i):
            pieces = [part(h[:, p], i) for h in by_owner]
            rows = [
                jnp.concatenate([g[:, :, c * wide : (c + 1) * wide] for g in pieces], axis=2)
                for c in range(3)
            ]
            whole = lax.dynamic_index_in_dim(out_quarters[p], i, 0, keepdims=False)
            rows += [whole[:, x * OWN : (x + 1) * OWN] for x in range(N_SHARD)]
            return jnp.concatenate([r.reshape(-1, OWN) for r in rows], axis=0)

        return quarter

    def middle_last(values):
        rest = 3 * N_SHARD * part_rows
        moving = [
            v[:rest].reshape(3, N_SHARD, part_rows, OWN).transpose(1, 0, 2, 3).reshape(N_SHARD, -1, OWN)
            for v in values
        ]
        moved = yield from middle_in(moving)
        return [
            jnp.concatenate(
                [m.reshape(N_SHARD, 3, part_rows, OWN).transpose(1, 0, 2, 3).reshape(rest, OWN), v[rest:]],
                axis=0,
            )
            for m, v in zip(moved, values)
        ]

    last_sum = Steps(rep_sum_steps([last_quarter(0), last_quarter(1)], n_rep, middle_last))
    sent = last_sum.sent
    first0, first1 = first_grad(0, sent), first_grad(1, sent)
    sent = experts_sum.step((first0, first1))
    sent = last_sum.step(sent)
    back_grad = place_experts(me, back_sum.finish(sent))
    sent = last_sum.step(back_grad)
    sent = experts_sum.step(sent)
    grad_first = scatter_near(first0, first1, tie(far_first, sent))
    first_in, normed_one, inverse_one = first_rows(tie(tokens, sent))
    grad_gain_one = jnp.sum(grad_first * normed_one, axis=0)
    grad_bias_one = jnp.sum(grad_first, axis=0)
    input_grad = grad_middle + norm_back(grad_first, normed_one, inverse_one, gain_one)

    by_expert = jnp.stack([(kept & ~is_late), (kept & is_late)]).astype(bf16)
    grad_back_shift = dot_nn(by_expert, grad_low)
    in_shift_grad = jnp.concatenate(
        [dot_nn(m.astype(bf16).reshape(1, -1), pre_all) for m in masks], axis=0
    )
    small = jnp.concatenate(
        [
            jnp.stack([grad_gain_one, grad_bias_one, grad_out_shift, grad_gain_two, grad_bias_two]),
            grad_back_shift,
            jnp.zeros((1, D), f32),
        ],
        axis=0,
    )
    small = small + swap(small, 1)
    small = small + swap(small, 2)
    small = lax.dynamic_slice_in_dim(small, me * shard_width, shard_width, axis=1)
    small = jnp.concatenate([small, in_shift_grad.reshape(-1, shard_width)], axis=0)
    sent = last_sum.step((input_grad, small))
    bit = 1
    while bit < n_rep:
        small = small + tie(rep_swap(small, bit, n_rep), sent)
        sent = small
        bit *= 2
    sent = last_sum.step(sent)
    in_done = experts_sum.finish(sent)
    sent = last_sum.step(in_done)
    in_grad = place_experts(me, tie(in_done, sent))
    in_shift_grad = small[8:].reshape(EXPERTS, inner)
    qkv_grad, out_grad = place_attention(me, last_sum.finish(in_grad), shard_width)
    return (
        final.astype(bf16),
        input_grad,
        small[0],
        small[1],
        qkv_grad,
        out_grad,
        small[2],
        small[3],
        small[4],
        in_grad,
        in_shift_grad,
        back_grad,
        small[5:7],
    )


def solution(mesh):
    in_specs = (
        P(("rep", "shard"), None),
        P(("rep", "shard")),
        P(),
        P("rep", None),
        P(("rep", "shard")),
        P(("rep", "shard"), None),
        P(("rep", "shard"), None),
        P("shard"),
        P("shard"),
        P("shard", None),
        P("shard", None),
        P("shard"),
        P("shard"),
        P("shard"),
        P(None, "shard", None),
        P(None, "shard"),
        P(None, "shard", None),
        P(None, "shard"),
    )
    out_specs = (
        P(("rep", "shard"), None),
        P(("rep", "shard"), None),
        P("shard"),
        P("shard"),
        P("shard", None),
        P("shard", None),
        P("shard"),
        P("shard"),
        P("shard"),
        P(None, "shard", None),
        P(None, "shard"),
        P(None, "shard", None),
        P(None, "shard"),
    )
    body = functools.partial(shards, mesh.shape["rep"])
    return jax.shard_map(body, mesh=mesh, in_specs=in_specs, out_specs=out_specs, check_vma=False)
```
